128 devices in a mesh: img: 8 (over z_hi, x), sp: 16 (over y, z_lo, core).
Axes of the slice: x: 4, y: 4, z: 4 (z_hi: 2, z_lo: 2; z = z_hi * 2 + z_lo), core: 2. Of those that a mesh axis runs over, the one named last changes fastest.
Arguments:
- tokens: bfloat16 [8, 14336, 2240], P('img', 'sp'), may hold values from -12 to 12
- queries: bfloat16 [8, 14336, 1120], P('img', 'sp'), may hold values from -6 to 6
- w_key: bfloat16 [2240, 1120], P('img'), may hold values from -0.125 to 0.125
- w_value: bfloat16 [2240, 1120], P('img'), may hold values from -0.125 to 0.125
- cotangent: bfloat16 [8, 14336, 1120], P('img', 'sp'), may hold values from -6 to 6
Outputs:
- attended: bfloat16 [8, 14336, 1120], P('img', 'sp')
- d_tokens: bfloat16 [8, 14336, 2240], P('img', 'sp')
- d_queries: bfloat16 [8, 14336, 1120], P('img', 'sp')
- d_w_key: float32 [2240, 1120], P('img')
- d_w_value: float32 [2240, 1120], P('img')
The draws below stay inside these ranges and needn't reach their ends.
All inputs are finite; a program needn't handle non-finite values.
Results may differ from the reference program's by a relative error of at most 0.006.
Values may be sent and summed in bfloat16 or wider, within the bound.
A program may use at most 128 MiB of HBM per device.

```python
import jax
import jax.numpy as jnp
from jax import lax

D = 2240
HEADS = 35
HD = 32
TOK_DEV = 896
HK = 1120
TOK_IMG = 14336
IMAGES = 8


def draw_tokens(key, part):
    first = jax.random.fold_in(key, 11)
    tiles = TOK_IMG // TOK_DEV
    rough = jnp.clip(jax.random.normal(first, (IMAGES, tiles, TOK_DEV, D), jnp.float32), -4.0, 4.0)
    rise = 1.0 + 2.0 * jnp.arange(tiles, dtype=jnp.float32) / max(tiles - 1, 1)
    values = rise.reshape(1, tiles, 1, 1) * rough
    return values.reshape(IMAGES, TOK_IMG, D).astype(jnp.bfloat16)


def level_of(rng, dims, split, least, largest):
    gain = 1.0
    for axis_at, blocks in split:
        draws = jax.random.uniform(jax.random.fold_in(jax.random.fold_in(rng, 6), axis_at), (blocks,), jnp.float32, least / len(split), largest / len(split))
        gain = gain * jnp.repeat(jnp.exp(draws), dims[axis_at] // blocks).reshape((-1,) + (1,) * (len(dims) - 1 - axis_at))
    return gain


def noise(key, shape, scale, most, shards=(), kind=jnp.bfloat16):
    entries = scale * jax.random.normal(key, shape, jnp.float32)
    if shards:
        entries = entries * level_of(key, shape, shards, -0.22, 0.18)
    return jnp.clip(entries, -most, most).astype(kind)


def setup_inputs(seed: int = 0) -> dict:
    arg_keys = jax.random.split(jax.random.key(seed), 6)
    return {
        "tokens": draw_tokens(jax.random.fold_in(arg_keys[5], 71), 0),
        "queries": noise(arg_keys[1], (IMAGES, TOK_IMG, HK), 1.0, 6.0, ((0, 8), (1, 16))),
        "w_key": noise(arg_keys[2], (D, HK), D ** -0.5, 0.125, ((0, 8),)),
        "w_value": noise(arg_keys[3], (D, HK), D ** -0.5, 0.125, ((0, 8),)),
        "cotangent": noise(arg_keys[4], (IMAGES, TOK_IMG, HK), 1.0, 6.0, ((0, 8), (1, 16))),
    }


EPS_DEN = 1e-06

def reference(tokens, queries, w_key, w_value, cotangent):
    high = lax.Precision.HIGHEST
    flat = tokens.reshape(-1, D)
    key_pre = jnp.dot(flat, w_key, preferred_element_type=jnp.float32)
    key_feat = jnp.maximum(key_pre, 0.0).astype(jnp.bfloat16)
    val_feat = jnp.dot(flat, w_value, preferred_element_type=jnp.float32).astype(jnp.bfloat16)
    key_f32 = key_feat.astype(jnp.float32).reshape(IMAGES, TOK_IMG, HEADS, HD)
    val_f32 = val_feat.astype(jnp.float32).reshape(IMAGES, TOK_IMG, HEADS, HD)
    kv_state = jnp.einsum('nthi,nthj->nhij', key_f32, val_f32, precision=high)
    key_norm = lax.optimization_barrier(jnp.sum(key_f32, axis=1))
    q_feat = jnp.maximum(queries.astype(jnp.float32), 0.0).reshape(IMAGES, TOK_IMG, HEADS, HD)
    numerator = jnp.einsum('nthi,nhij->nthj', q_feat, kv_state, precision=high)
    denominator = jnp.einsum('nthi,nhi->nth', q_feat, key_norm, precision=high) + EPS_DEN
    attn_f32 = numerator / denominator[..., None]
    attended = attn_f32.astype(jnp.bfloat16).reshape(IMAGES, TOK_IMG, HK)
    cot_f32 = cotangent.astype(jnp.float32).reshape(IMAGES, TOK_IMG, HEADS, HD)
    d_num = cot_f32 / denominator[..., None]
    d_den = -lax.optimization_barrier(jnp.sum(cot_f32 * attn_f32, axis=-1)) / denominator
    d_feat = jnp.einsum('nthj,nhij->nthi', d_num, kv_state, precision=high) + d_den[..., None] * key_norm[:, None]
    d_queries = jnp.where(q_feat > 0, d_feat, 0.0).astype(jnp.bfloat16).reshape(IMAGES, TOK_IMG, HK)
    grad_state = TOK_IMG * jnp.einsum('nthi,nthj->nhij', q_feat, d_num, precision=high)
    grad_norm = TOK_IMG * jnp.einsum('nth,nthi->nhi', d_den, q_feat, precision=high)
    d_key_f = jnp.einsum('nthj,nhij->nthi', val_f32, grad_state, precision=high) + grad_norm[:, None]
    d_key = jnp.where(key_f32 > 0, d_key_f, 0.0).astype(jnp.bfloat16).reshape(-1, HK)
    d_value = jnp.einsum('nthi,nhij->nthj', key_f32, grad_state, precision=high).astype(jnp.bfloat16).reshape(-1, HK)
    d_flat = jnp.dot(d_key, w_key.T, preferred_element_type=jnp.float32) + jnp.dot(d_value, w_value.T, preferred_element_type=jnp.float32)
    d_tokens = d_flat.astype(jnp.bfloat16).reshape(IMAGES, TOK_IMG, D)
    scale = 1.0 / jnp.sqrt(jnp.float32(IMAGES * TOK_IMG))
    d_w_key = jnp.dot(flat.T, d_key, preferred_element_type=jnp.float32) * scale
    d_w_value = jnp.dot(flat.T, d_value, preferred_element_type=jnp.float32) * scale
    return (attended, d_tokens, d_queries, d_w_key, d_w_value)
```

```python
import jax
import jax.numpy as jnp
from jax import lax
from jax.experimental import pallas as pl
from jax.experimental.pallas import tpu as pltpu
from jax.sharding import PartitionSpec as P

HD = 32
EPS_DEN = 1e-06
BF = jnp.bfloat16
F32 = jnp.float32
MESH = pl.DeviceIdType.MESH
LANE = 128
VMEM_MAX = 64 * 1024 * 1024 - 65536
DMA = pltpu.SemaphoreType.DMA


def params(cid=None, sem=None):
    return pltpu.CompilerParams(
        collective_id=cid,
        has_side_effects=cid is not None,
        vmem_limit_bytes=VMEM_MAX,
        dimension_semantics=sem,
    )


class Seat:
    def __init__(self):
        img, sp = lax.axis_index("img"), lax.axis_index("sp")
        self.img, self.sp = img, sp
        self.zhi, self.x = img // 4, img % 4
        self.y, self.zlo, self.core = sp // 4, (sp // 2) % 2, sp % 2

    def at(self, dx=0, dy=0, hi=None, lo=None, core=None):
        x = (self.x + dx + 4) % 4
        y = (self.y + dy + 4) % 4
        hi = self.zhi if hi is None else hi
        lo = self.zlo if lo is None else lo
        core = self.core if core is None else core
        return {"img": hi * 4 + x, "sp": (y * 2 + lo) * 2 + core}

    def across(self):
        return self.at(hi=1 - self.zhi, lo=1 - self.zlo)

    def beside(self):
        return self.at(lo=1 - self.zlo)

    def partner(self):
        return self.at(core=1 - self.core)


def meet(devices):
    bar = pltpu.get_barrier_semaphore()
    for d in devices:
        pl.semaphore_signal(bar, inc=1, device_id=d, device_id_type=MESH)
    pl.semaphore_wait(bar, len(devices))


def remote(src, dst, ssem, rsem, device):
    return pltpu.make_async_remote_copy(
        src_ref=src, dst_ref=dst, send_sem=ssem, recv_sem=rsem, device_id=device, device_id_type=MESH
    )


HALVES = ((0, 144), (144, 136))
L0, L1, R0, R1, O0, O1, YL0, YR0, YO0, YL1, YR1, YO1, ZM0, ZM1, ZN0, ZN1 = range(16)


def gather_kernel(w_ref, tok_ref, out, tok_out, ssem, rsem, csem, lsem, tsem):
    s = Seat()
    m = s.y % 2
    right, left = s.at(dx=1), s.at(dx=-1)
    up, down = s.at(dy=1), s.at(dy=-1)
    partner, across = s.partner(), s.across()
    meet((right, left, up, down, partner, across))

    def part(mat, shard, h):
        return out.at[mat, shard, pl.ds(HALVES[h][0], HALVES[h][1])]

    def mine(mat, h):
        return w_ref.at[mat, pl.ds(HALVES[h][0], HALVES[h][1])]

    def place(k, core):
        hi = (s.zhi + core) % 2
        if k >= ZM0:
            return part(m if k < ZN0 else 1 - m, (1 - s.zhi) * 4 + s.x, (k - ZM0) % 2)
        dx, h = {
            L0: (3, 0), L1: (3, 1), R0: (1, 0), R1: (1, 1), O0: (2, 0), O1: (2, 1),
            YL0: (3, 0), YR0: (1, 0), YO0: (2, 0), YL1: (3, 1), YR1: (1, 1), YO1: (2, 1),
        }[k]
        return part(m if k < YL0 else 1 - m, hi * 4 + (s.x + dx) % 4, h)

    swap = remote(tok_ref, tok_out, tsem.at[0], tsem.at[1], partner)
    owns = [
        pltpu.make_async_copy(w_ref.at[i], out.at[i, s.img], lsem.at[i]) for i in range(2)
    ]
    sent = []

    def send(src, dst, k, device, sems, start=True):
        slot = len(sent)
        c = remote(src, dst, ssem.at[slot], sems.at[k], device)
        sent.append(c)
        if start:
            c.start()
        return c

    is0, is1 = s.core == 0, s.core == 1
    hi = (s.zhi + s.core) % 2
    seed = hi * 4 + s.x

    zs = [
        send(mine(mat, h), part(mat, s.img, h), k, across, rsem, False)
        for k, mat, h in ((ZM0, m, 0), (ZM1, m, 1), (ZN0, 1 - m, 0), (ZN1, 1 - m, 1))
    ]
    first = [
        (send(mine(m, h), part(m, s.img, h), k, d, rsem, False), h)
        for h, k, d in ((0, L0, right), (1, R1, left), (1, L1, right), (0, R0, left))
    ]
    second = [
        (remote(part(m, seed, h), part(m, seed, h), ssem.at[4 + i], rsem.at[k], d), h)
        for i, (h, k, d) in enumerate(((0, L0, right), (1, R1, left), (1, L1, right), (0, R0, left)))
    ]

    @pl.when(is1)
    def _():
        for c in zs:
            c.start()

    @pl.when(is0)
    def _():
        for c, _h in first:
            c.start()

    for c in owns:
        c.start()
    swap.start()

    def got(k, sems, core):
        ref = place(k, core)
        pltpu.make_async_copy(ref, ref, sems.at[k]).wait()

    chips = {}

    def onchip(k, start=True):
        ref = place(k, s.core)
        chips[k] = send(ref, ref, k, partner, csem, start)

    for k in (ZM0, ZM1, ZN0, ZN1):
        onchip(k, False)

    @pl.when(is1)
    def _():
        for h, k in ((0, ZM0), (1, ZM1)):
            got(k, rsem, s.core)
            for c, ch in second:
                if ch == h:
                    c.start()
            chips[k].start()

    def arrive(k):
        got(k, rsem, s.core)
        ref = place(k, s.core)
        if k == L0:
            send(ref, ref, O0, right, rsem)
        if k == R1:
            send(ref, ref, O1, left, rsem)
        for a, b, d in (
            (L0, YL0, up), (R0, YR0, up), (O0, YO0, up),
            (L1, YL1, down), (R1, YR1, down), (O1, YO1, down),
        ):
            if k == a:
                send(ref, ref, b, d, rsem)
        onchip(k)

    for k in (L0, R1, L1, R0, YL0, YR1):
        arrive(k)

    @pl.when(is1)
    def _():
        for k in (ZN0, ZN1):
            got(k, rsem, s.core)
            chips[k].start()

    for k in (O0, O1, YR0, YL1, YO0, YO1):
        arrive(k)

    for k in range(ZM0):
        got(k, csem, 1 - s.core)

    @pl.when(is0)
    def _():
        for k in (ZM0, ZM1, ZN0, ZN1):
            got(k, csem, 1 - s.core)

    conditional = {id(c) for c in zs} | {id(chips[k]) for k in (ZM0, ZM1, ZN0, ZN1)}
    for c in sent:
        if id(c) not in conditional:
            c.wait_send()

    @pl.when(is1)
    def _():
        for c in zs:
            c.wait_send()
        for k in (ZM0, ZM1, ZN0, ZN1):
            chips[k].wait_send()

    for c in owns:
        c.wait()
    swap.wait()


def gather(w_pair, tok):
    rows, cols = w_pair.shape[1:]
    hbm = pl.BlockSpec(memory_space=pl.ANY)
    return pl.pallas_call(
        gather_kernel,
        name="gather",
        out_shape=(
            jax.ShapeDtypeStruct((2, 8, rows, cols), BF),
            jax.ShapeDtypeStruct(tok.shape, BF),
        ),
        in_specs=[pl.BlockSpec(memory_space=pltpu.VMEM), hbm],
        out_specs=(hbm, hbm),
        scratch_shapes=[DMA((40,)), DMA((16,)), DMA((16,)), DMA((2,)), DMA((2,))],
        compiler_params=params(1),
    )(w_pair, tok)


def split(a):
    hi = a.astype(BF)
    return hi, (a - hi.astype(F32)).astype(BF)


def same_head():
    r = lax.broadcasted_iota(jnp.int32, (LANE, LANE), 0) // HD
    c = lax.broadcasted_iota(jnp.int32, (LANE, LANE), 1) // HD
    return r == c


def fold(block, mask):
    b = jnp.where(mask, block, 0.0)
    return b[0:32] + b[32:64] + b[64:96] + b[96:128]


def unfold(state, mask):
    return jnp.where(mask, jnp.concatenate([state] * 4, axis=0), 0.0)


def put_state(ref, state, row):
    ref[0:4] = state.reshape(4, 8, LANE)
    ref[4] = jnp.broadcast_to(row, (8, LANE))


def dot(a, b):
    return lax.dot_general(a, b, (((1,), (0,)), ((), ())), preferred_element_type=F32)


def dot_t(a, b):
    return lax.dot_general(a, b, (((0,), (0,)), ((), ())), preferred_element_type=F32)


def inside(shape, width):
    lane = lax.broadcasted_iota(jnp.int32, shape, 1) + pl.program_id(0) * LANE
    return lane < width


def project_kernel(width, tok_ref, w_ref, kv_ref, part_ref):
    both = jnp.concatenate([w_ref[0], w_ref[1]], axis=1)
    acc = dot(tok_ref[...], both)
    ok = inside((acc.shape[0], LANE), width)
    key = jnp.where(ok, jnp.maximum(acc[:, :LANE], 0.0), 0.0).astype(BF)
    val = jnp.where(ok, acc[:, LANE:], 0.0).astype(BF)
    kv_ref[0] = key
    kv_ref[1] = val
    put_state(
        part_ref,
        fold(dot_t(key, val), same_head()),
        jnp.sum(key.astype(F32), axis=0, keepdims=True),
    )


def project(tok, w):
    count, depth = tok.shape
    width = w.shape[2]
    steps = pl.cdiv(width, LANE)
    return pl.pallas_call(
        lambda *r: project_kernel(width, *r),
        name="project",
        grid=(steps,),
        out_shape=(
            jax.ShapeDtypeStruct((2, count, width), BF),
            jax.ShapeDtypeStruct((48, 8, LANE), F32),
        ),
        in_specs=[
            pl.BlockSpec((count, depth), lambda g: (0, 0)),
            pl.BlockSpec((2, depth, LANE), lambda g: (0, 0, g)),
        ],
        out_specs=(
            pl.BlockSpec((2, count, LANE), lambda g: (0, 0, g)),
            pl.BlockSpec((5, 8, LANE), lambda g: (g, 0, 0)),
        ),
        compiler_params=params(),
    )(tok, w)


def total_kernel(part_ref, out_ref, slots, ssem, rsem, ssem2, rsem2):
    s = Seat()
    me = s.sp
    peers = [(me + k) % 16 for k in range(16)]
    devs = [{"img": s.img, "sp": p} for p in peers]
    meet(devs[1:])
    out = []
    for k in range(1, 16):
        c = remote(part_ref.at[peers[k]], slots.at[k], ssem.at[k], rsem.at[k], devs[k])
        c.start()
        out.append(c)
    acc = part_ref[me]
    for k in range(1, 16):
        out[k - 1].wait_recv()
        acc = acc + slots[k]
    out_ref[me] = acc
    back = []
    for k in range(1, 16):
        c = remote(out_ref.at[me], out_ref.at[me], ssem2.at[k], rsem2.at[k], devs[k])
        c.start()
        back.append(c)
    for k in range(1, 16):
        src = (me + 16 - k) % 16
        pltpu.make_async_copy(out_ref.at[src], out_ref.at[src], rsem2.at[k]).wait()
    for c in out + back:
        c.wait_send()


def total(part, cid):
    four = part.reshape(16, 3, 8, LANE)
    vm = pl.BlockSpec(memory_space=pltpu.VMEM)
    got = pl.pallas_call(
        total_kernel,
        name=f"total{cid}",
        out_shape=jax.ShapeDtypeStruct(four.shape, F32),
        in_specs=[vm],
        out_specs=vm,
        scratch_shapes=[pltpu.VMEM(four.shape, F32)] + [DMA((16,))] * 4,
        compiler_params=params(cid),
    )(four)
    return got.reshape(48, 8, LANE)


def attend_kernel(width, q_ref, g_ref, st_ref, att_ref, dq_ref, part_ref):
    mask = same_head()
    state = st_ref[0:4].reshape(32, LANE)
    row = st_ref[4][0:1]
    kv = unfold(state, mask)
    norm = jnp.where(mask, jnp.transpose(jnp.broadcast_to(row, (LANE, LANE))), 0.0)
    kvh, kvl = split(kv)
    nh, nl = split(norm)
    kvth, kvtl = split(jnp.transpose(kv))
    ok = inside(q_ref.shape, width)
    zero = jnp.zeros((), BF)
    q = jnp.where(ok, jnp.maximum(q_ref[...], zero), zero)
    g = jnp.where(ok, g_ref[...], zero).astype(F32)
    fwd = jnp.concatenate(
        [jnp.concatenate([kvh, nh], axis=1), jnp.concatenate([kvl, nl], axis=1)], axis=0
    )
    both = dot(jnp.concatenate([q, q], axis=1), fwd)
    inv = 1.0 / (both[:, LANE:] + EPS_DEN)
    attn = both[:, :LANE] * inv
    att_ref[...] = attn.astype(BF)
    d_num = g * inv
    gah, gal = split(g * attn)
    ones = jnp.where(mask, 1.0, 0.0).astype(BF)
    dots = dot(jnp.concatenate([gah, gal], axis=1), jnp.concatenate([ones, ones], axis=0))
    d_den = -dots * inv
    pair = jnp.concatenate(split(d_num), axis=1)
    back = jnp.concatenate(
        [
            jnp.concatenate([kvth, kvtl], axis=1),
            jnp.concatenate([kvth, jnp.zeros_like(kvtl)], axis=1),
        ],
        axis=0,
    )
    feat = dot(pair, back)
    feat = feat[:, :LANE] + feat[:, LANE:] + d_den * row
    dq_ref[...] = jnp.where(q > 0, feat, 0.0).astype(BF)
    gs = dot_t(q, pair)
    put_state(
        part_ref,
        fold(gs[:, :LANE] + gs[:, LANE:], mask),
        jnp.sum(d_den * q.astype(F32), axis=0, keepdims=True),
    )


def attend(q, g, state):
    count, width = q.shape
    cols = pl.BlockSpec((count, LANE), lambda i: (0, i))
    tiles = pl.BlockSpec((5, 8, LANE), lambda i: (i, 0, 0))
    return pl.pallas_call(
        lambda *r: attend_kernel(width, *r),
        name="attend",
        grid=(pl.cdiv(width, LANE),),
        out_shape=(
            jax.ShapeDtypeStruct((count, width), BF),
            jax.ShapeDtypeStruct((count, width), BF),
            jax.ShapeDtypeStruct((48, 8, LANE), F32),
        ),
        in_specs=[cols, cols, tiles],
        out_specs=(cols, cols, tiles),
        compiler_params=params(),
    )(q, g, state)


def features_kernel(tok_img, kv_ref, st_ref, d_ref):
    mask = same_head()
    state = st_ref[0:4].reshape(32, LANE) * tok_img
    row = st_ref[4][0:1] * tok_img
    gs = unfold(state, mask)
    gh, gl = split(gs)
    th, tl = split(jnp.transpose(gs))
    key, val = kv_ref[0], kv_ref[1]
    dk = dot(jnp.concatenate([val, val], axis=1), jnp.concatenate([th, tl], axis=0)) + row
    d_ref[0] = jnp.where(key > 0, dk, 0.0).astype(BF)
    dv = dot(jnp.concatenate([key, key], axis=1), jnp.concatenate([gh, gl], axis=0))
    d_ref[1] = dv.astype(BF)


def features(kv, state, tok_img):
    _, count, width = kv.shape
    cols = pl.BlockSpec((2, count, LANE), lambda i: (0, 0, i))
    return pl.pallas_call(
        lambda *r: features_kernel(float(tok_img), *r),
        name="features",
        grid=(pl.cdiv(width, LANE),),
        out_shape=jax.ShapeDtypeStruct(kv.shape, BF),
        in_specs=[cols, pl.BlockSpec((5, 8, LANE), lambda i: (i, 0, 0))],
        out_specs=cols,
        compiler_params=params(),
    )(kv, state)


ROWS = 256


def outer_kernel(d_ref, tok, tok2, out, mine, theirs, acc, stage, ssem, rsem, lsem, osem):
    s = Seat()
    partner = s.partner()
    meet((partner,))
    swap = remote(d_ref.at[1 - s.core], theirs, ssem, rsem, partner)
    swap.start()
    load = pltpu.make_async_copy(d_ref.at[s.core], mine, lsem)
    load.start()
    load.wait()
    depth = tok.shape[1]
    whole = depth // ROWS
    rest = depth - whole * ROWS

    def one(i, _):
        at = pl.ds(pl.multiple_of(i * ROWS, ROWS), ROWS)
        acc[at] = dot_t(tok[:, at], mine[...])
        return 0

    lax.fori_loop(0, whole, one, 0)
    acc[pl.ds(whole * ROWS, rest)] = dot_t(tok[:, pl.ds(whole * ROWS, rest)], mine[...])
    swap.wait()

    def two(i, _):
        at = pl.ds(pl.multiple_of(i * ROWS, ROWS), ROWS)
        stage[at] = (acc[at] + dot_t(tok2[:, at], theirs[...])).astype(BF)
        pltpu.make_async_copy(stage.at[at], out.at[at], osem.at[i]).start()
        return 0

    lax.fori_loop(0, whole, two, 0)
    at = pl.ds(whole * ROWS, rest)
    stage[at] = (acc[at] + dot_t(tok2[:, at], theirs[...])).astype(BF)
    last = pltpu.make_async_copy(stage.at[at], out.at[at], osem.at[whole])
    last.start()
    for i in range(whole):
        at = pl.ds(i * ROWS, ROWS)
        pltpu.make_async_copy(stage.at[at], out.at[at], osem.at[i]).wait()
    last.wait()


def outer(d, tok, tok2):
    _, count, width = d.shape
    depth = tok.shape[1]
    hbm = pl.BlockSpec(memory_space=pl.ANY)
    vm = pl.BlockSpec(memory_space=pltpu.VMEM)
    return pl.pallas_call(
        outer_kernel,
        name="outer",
        out_shape=jax.ShapeDtypeStruct((depth, width), BF),
        in_specs=[hbm, vm, vm],
        out_specs=hbm,
        scratch_shapes=[
            pltpu.VMEM((count, width), BF),
            pltpu.VMEM((count, width), BF),
            pltpu.VMEM((depth, width), F32),
            pltpu.VMEM((depth, width), BF),
            DMA, DMA, DMA, DMA((depth // ROWS + 1,)),
        ],
        compiler_params=params(4),
    )(d, tok, tok2)


PIECE = 72
CUT = 640


def reduce_kernel(scale, g_ref, ok_ref, ov_ref, own, relay, final, comb, res1, relay2, final2,
                  res2, zbuf, fin, ssem, rsem, lsem, csem):
    s = Seat()
    core = s.core
    x_r, x_l, y_r, y_l = s.at(dx=1), s.at(dx=-1), s.at(dy=1), s.at(dy=-1)
    right1, left1 = s.at(dx=1 - core, dy=core), s.at(dx=core - 1, dy=-core)
    right2, left2 = s.at(dx=core, dy=1 - core), s.at(dx=-core, dy=core - 1)
    me1 = s.x * (1 - core) + s.y * core
    me2 = s.y * (1 - core) + s.x * core
    across, beside, partner = s.across(), s.beside(), s.partner()
    meet((x_r, x_l, y_r, y_l, across, beside, partner))

    def piece(h, c, j):
        xx = c * (1 - core) + j * core
        yy = j * (1 - core) + c * core
        row = pl.multiple_of(PIECE * yy - 8 * (yy // 3), 8)
        return g_ref.at[h, xx, pl.ds(row, PIECE)]

    pending = []

    def go(src, dst, i, device):
        c = remote(src, dst, ssem.at[i], rsem.at[i], device)
        c.start()
        pending.append(c)
        return c

    def go4(c, h, dst, i, device):
        for j in range(4):
            remote(piece(h, c, j), dst.at[j], ssem.at[i], rsem.at[i], device).start()
        pending.append(remote(dst, dst, ssem.at[i], rsem.at[i], device))

    def load4(c, h, dst, i):
        for j in range(4):
            pltpu.make_async_copy(piece(h, c, j), dst.at[j], lsem.at[i]).start()

    def arrived(ref, sem):
        pltpu.make_async_copy(ref, ref, sem).wait()

    def nxt(v, k):
        return (v + k) % 4

    go4(nxt(me1, 2), 0, relay.at[0], 0, right1)
    go4(nxt(me1, 2), 1, relay.at[1], 1, left1)
    go4(nxt(me1, 1), 1, final.at[0, 1], 2, right1)
    go4(nxt(me1, 3), 0, final.at[1, 0], 3, left1)
    load4(nxt(me1, 1), 0, own.at[2], 2)
    load4(nxt(me1, 3), 1, own.at[3], 3)
    load4(me1, 0, own.at[0], 0)
    load4(me1, 1, own.at[1], 1)

    def add(dst, *srcs):
        def body(j, _):
            v = srcs[0][j].astype(F32)
            for r in srcs[1:]:
                v = v + r[j].astype(F32)
            dst[j] = v.astype(BF)
            return 0

        lax.fori_loop(0, 4, body, 0)

    arrived(own.at[2], lsem.at[2])
    arrived(relay.at[0], rsem.at[0])
    add(comb.at[0], own.at[2], relay.at[0])
    go(comb.at[0], final.at[0, 0], 4, right1)
    arrived(own.at[3], lsem.at[3])
    arrived(relay.at[1], rsem.at[1])
    add(comb.at[1], own.at[3], relay.at[1])
    go(comb.at[1], final.at[1, 1], 5, left1)
    for h in range(2):
        arrived(own.at[h], lsem.at[h])
    arrived(final.at[1, 0], rsem.at[3])
    arrived(final.at[0, 1], rsem.at[2])
    arrived(final.at[0, 0], rsem.at[4])
    add(res1.at[0], own.at[0], final.at[0, 0], final.at[1, 0])

    go(res1.at[0, nxt(me2, 2)], relay2.at[0], 6, right2)
    arrived(final.at[1, 1], rsem.at[5])
    add(res1.at[1], own.at[1], final.at[0, 1], final.at[1, 1])
    go(res1.at[1, nxt(me2, 2)], relay2.at[1], 7, left2)
    go(res1.at[1, nxt(me2, 1)], final2.at[0, 1], 8, right2)
    go(res1.at[0, nxt(me2, 3)], final2.at[1, 0], 9, left2)

    def sum2(*refs):
        v = refs[0][...].astype(F32)
        for r in refs[1:]:
            v = v + r[...].astype(F32)
        return v.astype(BF)

    arrived(relay2.at[0], rsem.at[6])
    relay2[0] = sum2(relay2.at[0], res1.at[0, nxt(me2, 1)])
    go(relay2.at[0], final2.at[0, 0], 10, right2)
    arrived(relay2.at[1], rsem.at[7])
    relay2[1] = sum2(relay2.at[1], res1.at[1, nxt(me2, 3)])
    go(relay2.at[1], final2.at[1, 1], 11, left2)
    arrived(final2.at[1, 0], rsem.at[9])
    arrived(final2.at[0, 1], rsem.at[8])
    arrived(final2.at[0, 0], rsem.at[10])
    res2[0] = sum2(res1.at[0, me2], final2.at[0, 0], final2.at[1, 0])
    arrived(final2.at[1, 1], rsem.at[11])
    res2[1] = sum2(res1.at[1, me2], final2.at[0, 1], final2.at[1, 1])

    go(res2.at[1 - s.zhi], zbuf.at[0], 12, across)
    arrived(zbuf.at[0], rsem.at[12])
    zbuf[2] = sum2(res2.at[s.zhi], zbuf.at[0])
    go(zbuf.at[2], zbuf.at[1], 13, beside)
    arrived(zbuf.at[1], rsem.at[13])
    mine = fin.at[core, s.y]
    mine[...] = sum2(zbuf.at[1], zbuf.at[2])

    yd, yu, yo = (s.y + 3) % 4, (s.y + 1) % 4, (s.y + 2) % 4
    go(mine, mine, 14, y_r)
    go(mine, mine, 15, y_l)

    def chip(ref, k):
        c = remote(ref, ref, ssem.at[k], csem.at[k - 18], partner)
        c.start()
        pending.append(c)

    chip(mine, 18)
    a, b = pl.ds(0, CUT), pl.ds(CUT, mine.shape[1] - CUT)
    arrived(fin.at[core, yd], rsem.at[14])
    go(fin.at[core, yd, :, a], fin.at[core, yd, :, a], 16, y_r)
    chip(fin.at[core, yd], 19)
    arrived(fin.at[core, yu], rsem.at[15])
    go(fin.at[core, yu, :, b], fin.at[core, yu, :, b], 17, y_l)
    chip(fin.at[core, yu], 20)
    arrived(fin.at[core, yo, :, a], rsem.at[16])
    arrived(fin.at[core, yo, :, b], rsem.at[17])
    chip(fin.at[core, yo], 21)
    for k, y in enumerate((s.y, yd, yu, yo)):
        arrived(fin.at[1 - core, y], csem.at[k])
    for c in pending:
        c.wait_send()
    for ref, i in ((ok_ref, 0), (ov_ref, 1)):
        for y in range(3):
            ref[pl.ds(PIECE * y, PIECE)] = fin[i, y].astype(F32) * scale
        ref[pl.ds(216, 64)] = fin[i, 3].astype(F32)[8:] * scale


def reduce_all(g, scale):
    depth, width = g.shape
    rows = depth // 8
    vm = pl.BlockSpec(memory_space=pltpu.VMEM)
    p = (PIECE, width)
    return pl.pallas_call(
        lambda *r: reduce_kernel(scale, *r),
        name="reduce",
        out_shape=(jax.ShapeDtypeStruct((rows, width), F32),) * 2,
        in_specs=[pl.BlockSpec(memory_space=pl.ANY)],
        out_specs=(vm, vm),
        scratch_shapes=[
            pltpu.VMEM((4, 4) + p, BF),
            pltpu.VMEM((2, 4) + p, BF),
            pltpu.VMEM((2, 2, 4) + p, BF),
            pltpu.VMEM((2, 4) + p, BF),
            pltpu.VMEM((2, 4) + p, BF),
            pltpu.VMEM((2,) + p, BF),
            pltpu.VMEM((2, 2) + p, BF),
            pltpu.VMEM((2,) + p, BF),
            pltpu.VMEM((3,) + p, BF),
            pltpu.VMEM((2, 4) + p, BF),
            DMA((22,)), DMA((18,)), DMA((4,)), DMA((4,)),
        ],
        compiler_params=params(5),
    )(g.reshape(2, 4, rows, width))


def body(tokens, queries, w_key, w_value, cotangent):
    tok = tokens[0]
    count, depth = tok.shape
    width = w_key.shape[1]
    tok_img = count * lax.axis_size("sp")
    images = lax.axis_size("img")
    w4, tok2 = gather(jnp.stack([w_key, w_value]), tok)
    w = w4.reshape(2, depth, width)
    kv, part = project(tok, w)
    state = total(part, 2)
    att, dq, gpart = attend(queries[0], cotangent[0], state)
    gstate = total(gpart, 3)
    d = features(kv, gstate, tok_img)
    g = outer(d, tok, tok2)
    dwk, dwv = reduce_all(g, float((images * tok_img) ** -0.5))
    back = (((1,), (1,)), ((), ()))
    d_flat = lax.dot_general(d[0], w[0], back, preferred_element_type=F32) + lax.dot_general(
        d[1], w[1], back, preferred_element_type=F32
    )
    return att[None], d_flat.astype(BF)[None], dq[None], dwk, dwv


def solution(mesh):
    rows, flat = P("img", "sp", None), P("img", None)
    return jax.shard_map(
        body,
        mesh=mesh,
        in_specs=(rows, rows, flat, flat, rows),
        out_specs=(rows, rows, rows, flat, flat),
        check_vma=False,
    )
```

```python
import jax
import jax.numpy as jnp
from jax import lax
from jax.experimental import pallas as pl
from jax.experimental.pallas import tpu as pltpu
from jax.sharding import PartitionSpec as P

HD = 32
EPS_DEN = 1e-06
BF = jnp.bfloat16
F32 = jnp.float32
MESH = pl.DeviceIdType.MESH
LANE = 128
ROWS = 256
VMEM_MAX = 64 * 1024 * 1024 - 65536
DMA = pltpu.SemaphoreType.DMA


def params(cid=None, sem=None):
    return pltpu.CompilerParams(
        collective_id=cid,
        has_side_effects=cid is not None,
        vmem_limit_bytes=VMEM_MAX,
        dimension_semantics=sem,
    )


class Seat:
    def __init__(self):
        img, sp = lax.axis_index("img"), lax.axis_index("sp")
        self.img, self.sp = img, sp
        self.zhi, self.x = img // 4, img % 4
        self.y, self.zlo, self.core = sp // 4, (sp // 2) % 2, sp % 2

    def at(self, dx=0, dy=0, hi=None, lo=None, core=None):
        x = (self.x + dx + 4) % 4
        y = (self.y + dy + 4) % 4
        hi = self.zhi if hi is None else hi
        lo = self.zlo if lo is None else lo
        core = self.core if core is None else core
        return {"img": hi * 4 + x, "sp": (y * 2 + lo) * 2 + core}

    def across(self):
        return self.at(hi=1 - self.zhi, lo=1 - self.zlo)

    def beside(self):
        return self.at(lo=1 - self.zlo)

    def partner(self):
        return self.at(core=1 - self.core)


def meet(devices):
    bar = pltpu.get_barrier_semaphore()
    for d in devices:
        pl.semaphore_signal(bar, inc=1, device_id=d, device_id_type=MESH)
    pl.semaphore_wait(bar, len(devices))


def remote(src, dst, ssem, rsem, device):
    return pltpu.make_async_remote_copy(
        src_ref=src, dst_ref=dst, send_sem=ssem, recv_sem=rsem, device_id=device, device_id_type=MESH
    )


HALVES = ((0, 144), (144, 136))
L0, L1, R0, R1, O0, O1, YL0, YR0, YO0, YL1, YR1, YO1, ZM0, ZM1, ZN0, ZN1 = range(16)


def gather_kernel(wk_ref, wv_ref, tok_ref, out, tok_out, tok_t, w_ref, tin, tup, ssem, rsem, csem,
                  lsem, tsem, usem):
    s = Seat()
    m = s.y % 2
    right, left = s.at(dx=1), s.at(dx=-1)
    up, down = s.at(dy=1), s.at(dy=-1)
    partner, across = s.partner(), s.across()
    loads = [
        pltpu.make_async_copy(r, w_ref.at[i], lsem.at[2 + i]) for i, r in enumerate((wk_ref, wv_ref))
    ]
    read = pltpu.make_async_copy(tok_ref, tin, usem.at[0])
    for c in loads:
        c.start()
    read.start()
    meet((right, left, up, down, partner, across))
    for c in loads:
        c.wait()

    def part(mat, shard, h):
        return out.at[mat, shard, pl.ds(HALVES[h][0], HALVES[h][1])]

    def mine(mat, h):
        return w_ref.at[mat, pl.ds(HALVES[h][0], HALVES[h][1])]

    def place(k, core):
        hi = (s.zhi + core) % 2
        if k >= ZM0:
            return part(m if k < ZN0 else 1 - m, (1 - s.zhi) * 4 + s.x, (k - ZM0) % 2)
        dx, h = {
            L0: (3, 0), L1: (3, 1), R0: (1, 0), R1: (1, 1), O0: (2, 0), O1: (2, 1),
            YL0: (3, 0), YR0: (1, 0), YO0: (2, 0), YL1: (3, 1), YR1: (1, 1), YO1: (2, 1),
        }[k]
        return part(m if k < YL0 else 1 - m, hi * 4 + (s.x + dx) % 4, h)

    swap = remote(tok_ref, tok_out, tsem.at[0], tsem.at[1], partner)
    owns = [
        pltpu.make_async_copy(w_ref.at[i], out.at[i, s.img], lsem.at[i]) for i in range(2)
    ]
    sent = []

    def send(src, dst, k, device, sems, start=True):
        slot = len(sent)
        c = remote(src, dst, ssem.at[slot], sems.at[k], device)
        sent.append(c)
        if start:
            c.start()
        return c

    is0, is1 = s.core == 0, s.core == 1
    hi = (s.zhi + s.core) % 2
    seed = hi * 4 + s.x

    zs = [
        send(mine(mat, h), part(mat, s.img, h), k, across, rsem, False)
        for k, mat, h in ((ZM0, m, 0), (ZM1, m, 1), (ZN0, 1 - m, 0), (ZN1, 1 - m, 1))
    ]
    first = [
        (send(mine(m, h), part(m, s.img, h), k, d, rsem, False), h)
        for h, k, d in ((0, L0, right), (1, R1, left), (1, L1, right), (0, R0, left))
    ]
    second = [
        (remote(part(m, seed, h), part(m, seed, h), ssem.at[4 + i], rsem.at[k], d), h)
        for i, (h, k, d) in enumerate(((0, L0, right), (1, R1, left), (1, L1, right), (0, R0, left)))
    ]

    @pl.when(is1)
    def _():
        for c in zs:
            c.start()

    @pl.when(is0)
    def _():
        for c, _h in first:
            c.start()

    for c in owns:
        c.start()
    swap.start()
    read.wait()
    depth = tok_ref.shape[0]
    whole = depth // ROWS
    rest = depth - whole * ROWS

    def flip(i, _):
        at = pl.ds(pl.multiple_of(i * ROWS, ROWS), ROWS)
        tup[:, at] = jnp.transpose(tin[at])
        return 0

    lax.fori_loop(0, whole, flip, 0)
    at = pl.ds(whole * ROWS, rest)
    tup[:, at] = jnp.transpose(tin[at])
    write = pltpu.make_async_copy(tup, tok_t, usem.at[1])
    write.start()

    def got(k, sems, core):
        ref = place(k, core)
        pltpu.make_async_copy(ref, ref, sems.at[k]).wait()

    chips = {}

    def onchip(k, start=True):
        ref = place(k, s.core)
        chips[k] = send(ref, ref, k, partner, csem, start)

    for k in (ZM0, ZM1, ZN0, ZN1):
        onchip(k, False)

    @pl.when(is1)
    def _():
        for h, k in ((0, ZM0), (1, ZM1)):
            got(k, rsem, s.core)
            for c, ch in second:
                if ch == h:
                    c.start()
            chips[k].start()

    def arrive(k):
        got(k, rsem, s.core)
        ref = place(k, s.core)
        if k == L0:
            send(ref, ref, O0, right, rsem)
        if k == R1:
            send(ref, ref, O1, left, rsem)
        for a, b, d in (
            (L0, YL0, up), (R0, YR0, up), (O0, YO0, up),
            (L1, YL1, down), (R1, YR1, down), (O1, YO1, down),
        ):
            if k == a:
                send(ref, ref, b, d, rsem)
        onchip(k)

    for k in (L0, R1, L1, R0, YL0, YR1):
        arrive(k)

    @pl.when(is1)
    def _():
        for k in (ZN0, ZN1):
            got(k, rsem, s.core)
            chips[k].start()

    for k in (O0, O1, YR0, YL1, YO0, YO1):
        arrive(k)

    for k in range(ZM0):
        got(k, csem, 1 - s.core)

    @pl.when(is0)
    def _():
        for k in (ZM0, ZM1, ZN0, ZN1):
            got(k, csem, 1 - s.core)

    conditional = {id(c) for c in zs} | {id(chips[k]) for k in (ZM0, ZM1, ZN0, ZN1)}
    for c in sent:
        if id(c) not in conditional:
            c.wait_send()

    @pl.when(is1)
    def _():
        for c in zs:
            c.wait_send()
        for k in (ZM0, ZM1, ZN0, ZN1):
            chips[k].wait_send()

    for c in owns:
        c.wait()
    swap.wait()
    write.wait()


def gather(wk, wv, tok):
    rows, cols = wk.shape
    hbm = pl.BlockSpec(memory_space=pl.ANY)
    return pl.pallas_call(
        gather_kernel,
        name="gather",
        out_shape=(
            jax.ShapeDtypeStruct((2, 8, rows, cols), BF),
            jax.ShapeDtypeStruct(tok.shape, BF),
            jax.ShapeDtypeStruct(tok.shape[::-1], BF),
        ),
        in_specs=[hbm] * 3,
        out_specs=(hbm,) * 3,
        scratch_shapes=[
            pltpu.VMEM((2, rows, cols), BF),
            pltpu.VMEM(tok.shape, BF),
            pltpu.VMEM(tok.shape[::-1], BF),
            DMA((40,)), DMA((16,)), DMA((16,)), DMA((4,)), DMA((2,)), DMA((2,)),
        ],
        compiler_params=params(1),
    )(wk, wv, tok)


def split(a):
    hi = a.astype(BF)
    return hi, (a - hi.astype(F32)).astype(BF)


def same_head():
    r = lax.broadcasted_iota(jnp.int32, (LANE, LANE), 0) // HD
    c = lax.broadcasted_iota(jnp.int32, (LANE, LANE), 1) // HD
    return r == c


def fold(block, mask):
    b = jnp.where(mask, block, 0.0)
    return b[0:32] + b[32:64] + b[64:96] + b[96:128]


def unfold(state, mask):
    return jnp.where(mask, jnp.concatenate([state] * 4, axis=0), 0.0)


def put_state(ref, state, row):
    ref[0:4] = state.reshape(4, 8, LANE)
    ref[4] = jnp.broadcast_to(row, (8, LANE))


def dot(a, b):
    return lax.dot_general(a, b, (((1,), (0,)), ((), ())), preferred_element_type=F32)


def dot_t(a, b):
    return lax.dot_general(a, b, (((0,), (0,)), ((), ())), preferred_element_type=F32)


def inside(shape, width):
    lane = lax.broadcasted_iota(jnp.int32, shape, 1) + pl.program_id(0) * LANE
    return lane < width


def project_kernel(width, tok_ref, w_ref, kv_ref, part_ref):
    both = jnp.concatenate([w_ref[0], w_ref[1]], axis=1)
    acc = dot(tok_ref[...], both)
    ok = inside((acc.shape[0], LANE), width)
    key = jnp.where(ok, jnp.maximum(acc[:, :LANE], 0.0), 0.0).astype(BF)
    val = jnp.where(ok, acc[:, LANE:], 0.0).astype(BF)
    kv_ref[0] = key
    kv_ref[1] = val
    put_state(
        part_ref,
        fold(dot_t(key, val), same_head()),
        jnp.sum(key.astype(F32), axis=0, keepdims=True),
    )


def project(tok, w):
    count, depth = tok.shape
    width = w.shape[2]
    steps = pl.cdiv(width, LANE)
    return pl.pallas_call(
        lambda *r: project_kernel(width, *r),
        name="project",
        grid=(steps,),
        out_shape=(
            jax.ShapeDtypeStruct((2, count, width), BF),
            jax.ShapeDtypeStruct((48, 8, LANE), F32),
        ),
        in_specs=[
            pl.BlockSpec((count, depth), lambda g: (0, 0)),
            pl.BlockSpec((2, depth, LANE), lambda g: (0, 0, g)),
        ],
        out_specs=(
            pl.BlockSpec((2, count, LANE), lambda g: (0, 0, g)),
            pl.BlockSpec((5, 8, LANE), lambda g: (g, 0, 0)),
        ),
        compiler_params=params(),
    )(tok, w)


def total_kernel(part_ref, out_ref, slots, ssem, rsem, ssem2, rsem2):
    s = Seat()
    me = s.sp
    peers = [(me + k) % 16 for k in range(16)]
    devs = [{"img": s.img, "sp": p} for p in peers]
    meet(devs[1:])
    out = []
    for k in range(1, 16):
        c = remote(part_ref.at[peers[k]], slots.at[k], ssem.at[k], rsem.at[k], devs[k])
        c.start()
        out.append(c)
    acc = part_ref[me]
    for k in range(1, 16):
        out[k - 1].wait_recv()
        acc = acc + slots[k]
    out_ref[me] = acc
    back = []
    for k in range(1, 16):
        c = remote(out_ref.at[me], out_ref.at[me], ssem2.at[k], rsem2.at[k], devs[k])
        c.start()
        back.append(c)
    for k in range(1, 16):
        src = (me + 16 - k) % 16
        pltpu.make_async_copy(out_ref.at[src], out_ref.at[src], rsem2.at[k]).wait()
    for c in out + back:
        c.wait_send()


def total(part, cid):
    four = part.reshape(16, 3, 8, LANE)
    vm = pl.BlockSpec(memory_space=pltpu.VMEM)
    got = pl.pallas_call(
        total_kernel,
        name=f"total{cid}",
        out_shape=jax.ShapeDtypeStruct(four.shape, F32),
        in_specs=[vm],
        out_specs=vm,
        scratch_shapes=[pltpu.VMEM(four.shape, F32)] + [DMA((16,))] * 4,
        compiler_params=params(cid),
    )(four)
    return got.reshape(48, 8, LANE)


def dot_r(a, b):
    return lax.dot_general(a, b, (((1,), (1,)), ((), ())), preferred_element_type=F32)


def attend_kernel(width, q_ref, g_ref, st_ref, att_ref, dq_ref, part_ref):
    mask = same_head()
    state = st_ref[0:4].reshape(32, LANE)
    row = jnp.broadcast_to(st_ref[4][0:1], (LANE, LANE))
    col = jnp.transpose(row)[:, 0:1]
    kv = unfold(state, mask)
    kvh, kvl = split(kv)
    kvth, kvtl = split(jnp.transpose(kv))
    nh, nl = split(jnp.where(mask, row, 0.0))
    line = lax.broadcasted_iota(jnp.int32, q_ref.shape, 0) + pl.program_id(0) * LANE
    ok = line < width
    zero = jnp.zeros((), BF)
    q = jnp.where(ok, jnp.maximum(q_ref[...], zero), zero)
    g = jnp.where(ok, g_ref[...], zero).astype(F32)
    fwd = jnp.concatenate(
        [jnp.concatenate([kvth, kvtl], axis=1), jnp.concatenate([nh, nl], axis=1)], axis=0
    )
    both = dot(fwd, jnp.concatenate([q, q], axis=0))
    inv = 1.0 / (both[LANE:] + EPS_DEN)
    attn = both[:LANE] * inv
    att_ref[...] = attn.astype(BF)
    d_num = g * inv
    ones = jnp.where(mask, 1.0, 0.0).astype(BF)
    dots = dot(
        jnp.concatenate([ones, ones], axis=1), jnp.concatenate(split(g * attn), axis=0)
    )
    d_den = -dots * inv
    dnh, dnl = split(d_num)
    feat = dot(jnp.concatenate([kvh, kvh], axis=1), jnp.concatenate([dnh, dnl], axis=0))
    feat = feat + dot(kvl, dnh) + d_den * col
    dq_ref[...] = jnp.where(q > 0, feat, 0.0).astype(BF)
    gs = dot_r(q, jnp.concatenate([dnh, dnl], axis=0))
    gn = jnp.sum(d_den * q.astype(F32), axis=1, keepdims=True)
    put_state(
        part_ref,
        fold(gs[:, :LANE] + gs[:, LANE:], mask),
        jnp.transpose(jnp.broadcast_to(gn, (LANE, LANE)))[0:1],
    )


def attend(q, g, state):
    width, count = q.shape
    lines = pl.BlockSpec((LANE, count), lambda i: (i, 0))
    tiles = pl.BlockSpec((5, 8, LANE), lambda i: (i, 0, 0))
    return pl.pallas_call(
        lambda *r: attend_kernel(width, *r),
        name="attend",
        grid=(pl.cdiv(width, LANE),),
        out_shape=(
            jax.ShapeDtypeStruct((width, count), BF),
            jax.ShapeDtypeStruct((width, count), BF),
            jax.ShapeDtypeStruct((48, 8, LANE), F32),
        ),
        in_specs=[lines, lines, tiles],
        out_specs=(lines, lines, tiles),
        compiler_params=params(),
    )(q, g, state)


def features_kernel(tok_img, kv_ref, st_ref, d_ref):
    mask = same_head()
    state = st_ref[0:4].reshape(32, LANE) * tok_img
    row = st_ref[4][0:1] * tok_img
    gs = unfold(state, mask)
    gh, gl = split(gs)
    th, tl = split(jnp.transpose(gs))
    key, val = kv_ref[0], kv_ref[1]
    dk = dot(jnp.concatenate([val, val], axis=1), jnp.concatenate([th, tl], axis=0)) + row
    d_ref[0] = jnp.where(key > 0, dk, 0.0).astype(BF)
    dv = dot(jnp.concatenate([key, key], axis=1), jnp.concatenate([gh, gl], axis=0))
    d_ref[1] = dv.astype(BF)


def features(kv, state, tok_img):
    _, count, width = kv.shape
    cols = pl.BlockSpec((2, count, LANE), lambda i: (0, 0, i))
    return pl.pallas_call(
        lambda *r: features_kernel(float(tok_img), *r),
        name="features",
        grid=(pl.cdiv(width, LANE),),
        out_shape=jax.ShapeDtypeStruct(kv.shape, BF),
        in_specs=[cols, pl.BlockSpec((5, 8, LANE), lambda i: (i, 0, 0))],
        out_specs=cols,
        compiler_params=params(),
    )(kv, state)


PIECE = 72
OFFS = (0, 72, 144, 208)
CUT = 640
BAND = 448


def finish_kernel(scale, d_ref, tok_ref, tok2_ref, w_ref, ok_ref, ov_ref, dt_ref, cat, dcat, dboth,
                  gp, relay, final, comb, res1, relay2, final2, res2, zbuf, fin, wbuf, tbuf,
                  ssem, rsem, lsem, csem, wsem, osem):
    s = Seat()
    core = s.core
    x_r, x_l, y_r, y_l = s.at(dx=1), s.at(dx=-1), s.at(dy=1), s.at(dy=-1)
    right1, left1 = s.at(dx=1 - core, dy=core), s.at(dx=core - 1, dy=-core)
    right2, left2 = s.at(dx=core, dy=1 - core), s.at(dx=-core, dy=core - 1)
    me1 = s.x * (1 - core) + s.y * core
    me2 = s.y * (1 - core) + s.x * core
    across, beside, partner = s.across(), s.beside(), s.partner()
    count = d_ref.shape[1]

    def loader(src, dst, i):
        return pltpu.make_async_copy(src, dst, lsem.at[i])

    lo, up = pl.ds(0, count), pl.ds(count, count)
    ld = [
        loader(d_ref.at[core], dcat.at[lo], 0),
        loader(tok_ref, cat.at[:, :, lo], 1),
        loader(tok2_ref, cat.at[:, :, up], 2),
        loader(d_ref, dboth, 3),
    ]
    for c in ld:
        c.start()
    bands = w_ref.shape[1] // BAND

    def band_load(i):
        at = pl.ds(i * BAND, BAND)
        return pltpu.make_async_copy(w_ref.at[:, at], wbuf.at[i % 2], wsem.at[i])

    band_load(0).start()
    band_load(1).start()
    meet((x_r, x_l, y_r, y_l, across, beside, partner))
    swap = remote(d_ref.at[1 - core], dcat.at[up], ssem.at[22], rsem.at[18], partner)
    swap.start()

    pending = []

    def copy(src, dst, i, device):
        return remote(src, dst, ssem.at[i], rsem.at[i], device)

    def go(src, dst, i, device):
        c = copy(src, dst, i, device)
        c.start()
        pending.append(c)

    def arrived(ref, sem):
        pltpu.make_async_copy(ref, ref, sem).wait()

    def nxt(v, k):
        return (v + k) % 4

    def bands_out(i):
        at = pl.ds(i * BAND, BAND)
        return pltpu.make_async_copy(tbuf.at[i % 2], dt_ref.at[at], osem.at[i])

    def band(i):
        if i == 0:
            ld[3].wait()
        band_load(i).wait()
        if i >= 2:
            bands_out(i - 2).wait()
        both = wbuf.at[i % 2]
        v = dot_r(both[0], dboth[0]) + dot_r(both[1], dboth[1])
        tbuf[i % 2] = v.astype(BF)
        bands_out(i).start()
        if i + 2 < bands:
            band_load(i + 2).start()

    def shard(h, dx):
        xx = nxt(s.x, dx)
        v = dot(cat[h * 4 + xx], dcat[...])
        for y in range(4):
            c = xx * (1 - core) + y * core
            j = y * (1 - core) + xx * core
            gp[h, c, j] = v[OFFS[y] : OFFS[y] + PIECE].astype(BF)

        @pl.when(core == 1)
        def _():
            j = xx
            d = (right1, left1)
            copy(gp.at[h, nxt(me1, 2), j], relay.at[h, j], h, d[h]).start()
            if h == 1:
                copy(gp.at[1, nxt(me1, 1), j], final.at[0, 1, j], 2, right1).start()
            else:
                copy(gp.at[0, nxt(me1, 3), j], final.at[1, 0, j], 3, left1).start()

        act = {
            (0, 2): (relay.at[0], 0, right1),
            (1, 2): (relay.at[1], 1, left1),
            (1, 1): (final.at[0, 1], 2, right1),
            (0, 3): (final.at[1, 0], 3, left1),
        }.get((h, dx))
        if act is not None:
            dst, i, dev = act

            @pl.when(core == 0)
            def _():
                copy(gp.at[h, nxt(me1, dx)], dst, i, dev).start()

    def add(dst, *srcs):
        def body(j, _):
            v = srcs[0][j].astype(F32)
            for r in srcs[1:]:
                v = v + r[j].astype(F32)
            dst[j] = v.astype(BF)
            return 0

        lax.fori_loop(0, 4, body, 0)

    def combine():
        arrived(relay.at[0], rsem.at[0])
        add(comb.at[0], gp.at[0, nxt(me1, 1)], relay.at[0])
        copy(comb.at[0], final.at[0, 0], 4, right1).start()
        arrived(relay.at[1], rsem.at[1])
        add(comb.at[1], gp.at[1, nxt(me1, 3)], relay.at[1])
        copy(comb.at[1], final.at[1, 1], 5, left1).start()

    for c in ld[:3]:
        c.wait()
    swap.wait()
    for h, dx in ((0, 2), (1, 2), (1, 1), (0, 3), (0, 1), (1, 3)):
        shard(h, dx)

    @pl.when(core == 0)
    def _():
        combine()

    shard(0, 0)
    shard(1, 0)

    @pl.when(core == 1)
    def _():
        combine()

    for i, dst in enumerate(
        (relay.at[0], relay.at[1], final.at[0, 1], final.at[1, 0], final.at[0, 0], final.at[1, 1])
    ):
        pending.append(copy(dst, dst, i, right1))

    band(0)
    band(1)
    band(2)
    arrived(final.at[1, 0], rsem.at[3])
    arrived(final.at[0, 1], rsem.at[2])
    arrived(final.at[0, 0], rsem.at[4])
    add(res1.at[0], gp.at[0, me1], final.at[0, 0], final.at[1, 0])

    go(res1.at[0, nxt(me2, 2)], relay2.at[0], 6, right2)
    arrived(final.at[1, 1], rsem.at[5])
    add(res1.at[1], gp.at[1, me1], final.at[0, 1], final.at[1, 1])
    go(res1.at[1, nxt(me2, 2)], relay2.at[1], 7, left2)
    go(res1.at[1, nxt(me2, 1)], final2.at[0, 1], 8, right2)
    go(res1.at[0, nxt(me2, 3)], final2.at[1, 0], 9, left2)
    band(3)

    def plus(*refs):
        v = refs[0][...].astype(F32)
        for r in refs[1:]:
            v = v + r[...].astype(F32)
        return v.astype(BF)

    arrived(relay2.at[0], rsem.at[6])
    relay2[0] = plus(relay2.at[0], res1.at[0, nxt(me2, 1)])
    go(relay2.at[0], final2.at[0, 0], 10, right2)
    arrived(relay2.at[1], rsem.at[7])
    relay2[1] = plus(relay2.at[1], res1.at[1, nxt(me2, 3)])
    go(relay2.at[1], final2.at[1, 1], 11, left2)
    band(4)
    arrived(final2.at[1, 0], rsem.at[9])
    arrived(final2.at[0, 1], rsem.at[8])
    arrived(final2.at[0, 0], rsem.at[10])
    res2[0] = plus(res1.at[0, me2], final2.at[0, 0], final2.at[1, 0])
    arrived(final2.at[1, 1], rsem.at[11])
    res2[1] = plus(res1.at[1, me2], final2.at[0, 1], final2.at[1, 1])

    go(res2.at[1 - s.zhi], zbuf.at[0], 12, across)
    arrived(zbuf.at[0], rsem.at[12])
    zbuf[2] = plus(res2.at[s.zhi], zbuf.at[0])
    go(zbuf.at[2], zbuf.at[1], 13, beside)
    arrived(zbuf.at[1], rsem.at[13])
    mine = fin.at[core, s.y]
    mine[...] = plus(zbuf.at[1], zbuf.at[2])

    yd, yu, yo = (s.y + 3) % 4, (s.y + 1) % 4, (s.y + 2) % 4
    go(mine, mine, 14, y_r)
    go(mine, mine, 15, y_l)

    def chip(ref, k):
        c = remote(ref, ref, ssem.at[k], csem.at[k - 18], partner)
        c.start()
        pending.append(c)

    chip(mine, 18)
    a, b = pl.ds(0, CUT), pl.ds(CUT, mine.shape[1] - CUT)
    arrived(fin.at[core, yd], rsem.at[14])
    go(fin.at[core, yd, :, a], fin.at[core, yd, :, a], 16, y_r)
    chip(fin.at[core, yd], 19)
    arrived(fin.at[core, yu], rsem.at[15])
    go(fin.at[core, yu, :, b], fin.at[core, yu, :, b], 17, y_l)
    chip(fin.at[core, yu], 20)
    arrived(fin.at[core, yo, :, a], rsem.at[16])
    arrived(fin.at[core, yo, :, b], rsem.at[17])
    chip(fin.at[core, yo], 21)
    for k, y in enumerate((s.y, yd, yu, yo)):
        arrived(fin.at[1 - core, y], csem.at[k])
    for c in pending:
        c.wait_send()
    for i in (bands - 2, bands - 1):
        bands_out(i).wait()
    for ref, i in ((ok_ref, 0), (ov_ref, 1)):
        for y in range(3):
            ref[pl.ds(PIECE * y, PIECE)] = fin[i, y].astype(F32) * scale
        ref[pl.ds(216, 64)] = fin[i, 3].astype(F32)[8:] * scale


def finish(d, tok, tok2, w, scale):
    _, count, width = d.shape
    depth = tok.shape[0]
    rows = depth // 8
    vm = pl.BlockSpec(memory_space=pltpu.VMEM)
    hbm = pl.BlockSpec(memory_space=pl.ANY)
    p = (PIECE, width)
    return pl.pallas_call(
        lambda *r: finish_kernel(scale, *r),
        name="finish",
        out_shape=(jax.ShapeDtypeStruct((rows, width), F32),) * 2
        + (jax.ShapeDtypeStruct((depth, count), BF),),
        in_specs=[hbm] * 4,
        out_specs=(vm, vm, hbm),
        scratch_shapes=[
            pltpu.VMEM((8, rows, 2 * count), BF),
            pltpu.VMEM((2 * count, width), BF),
            pltpu.VMEM((2, count, width), BF),
            pltpu.VMEM((2, 4, 4) + p, BF),
            pltpu.VMEM((2, 4) + p, BF),
            pltpu.VMEM((2, 2, 4) + p, BF),
            pltpu.VMEM((2, 4) + p, BF),
            pltpu.VMEM((2, 4) + p, BF),
            pltpu.VMEM((2,) + p, BF),
            pltpu.VMEM((2, 2) + p, BF),
            pltpu.VMEM((2,) + p, BF),
            pltpu.VMEM((3,) + p, BF),
            pltpu.VMEM((2, 4) + p, BF),
            pltpu.VMEM((2, 2, BAND, width), BF),
            pltpu.VMEM((2, BAND, count), BF),
            DMA((23,)), DMA((19,)), DMA((4,)), DMA((4,)), DMA((5,)), DMA((5,)),
        ],
        compiler_params=params(5),
    )(d, tok.reshape(8, rows, count), tok2.reshape(8, rows, count), w)


def body(tokens, queries, w_key, w_value, cotangent):
    tok = jnp.transpose(tokens[0])
    depth, count = tok.shape
    width = w_key.shape[1]
    tok_img = count * lax.axis_size("sp")
    images = lax.axis_size("img")
    w4, tok2, tok_t = gather(w_key, w_value, tok)
    w = w4.reshape(2, depth, width)
    kv, part = project(tok_t, w)
    state = total(part, 2)
    att, dq, gpart = attend(jnp.transpose(queries[0]), jnp.transpose(cotangent[0]), state)
    gstate = total(gpart, 3)
    d = features(kv, gstate, tok_img)
    dwk, dwv, dt = finish(d, tok, tok2, w, float((images * tok_img) ** -0.5))
    return jnp.transpose(att)[None], jnp.transpose(dt)[None], jnp.transpose(dq)[None], dwk, dwv


def solution(mesh):
    rows, flat = P("img", "sp", None), P("img", None)
    return jax.shard_map(
        body,
        mesh=mesh,
        in_specs=(rows, rows, flat, flat, rows),
        out_specs=(rows, rows, rows, flat, flat),
        check_vma=False,
    )
```

```python
import jax
import jax.numpy as jnp
from jax import lax
from jax.experimental import pallas as pl
from jax.experimental.pallas import tpu as pltpu
from jax.sharding import PartitionSpec as P

HD = 32
EPS_DEN = 1e-06
BF = jnp.bfloat16
F32 = jnp.float32
MESH = pl.DeviceIdType.MESH
LANE = 128
ROWS = 256
VMEM_MAX = 64 * 1024 * 1024 - 65536
DMA = pltpu.SemaphoreType.DMA


def params(cid=None, sem=None):
    return pltpu.CompilerParams(
        collective_id=cid,
        has_side_effects=cid is not None,
        vmem_limit_bytes=VMEM_MAX,
        dimension_semantics=sem,
    )


class Seat:
    def __init__(self):
        img, sp = lax.axis_index("img"), lax.axis_index("sp")
        self.img, self.sp = img, sp
        self.zhi, self.x = img // 4, img % 4
        self.y, self.zlo, self.core = sp // 4, (sp // 2) % 2, sp % 2

    def at(self, dx=0, dy=0, hi=None, lo=None, core=None):
        x = (self.x + dx + 4) % 4
        y = (self.y + dy + 4) % 4
        hi = self.zhi if hi is None else hi
        lo = self.zlo if lo is None else lo
        core = self.core if core is None else core
        return {"img": hi * 4 + x, "sp": (y * 2 + lo) * 2 + core}

    def across(self):
        return self.at(hi=1 - self.zhi, lo=1 - self.zlo)

    def beside(self):
        return self.at(lo=1 - self.zlo)

    def partner(self):
        return self.at(core=1 - self.core)


def meet(devices):
    bar = pltpu.get_barrier_semaphore()
    for d in devices:
        pl.semaphore_signal(bar, inc=1, device_id=d, device_id_type=MESH)
    pl.semaphore_wait(bar, len(devices))


def remote(src, dst, ssem, rsem, device):
    return pltpu.make_async_remote_copy(
        src_ref=src, dst_ref=dst, send_sem=ssem, recv_sem=rsem, device_id=device, device_id_type=MESH
    )


HALVES = ((0, 144), (144, 136))
L0, L1, R0, R1, O0, O1, YL0, YR0, YO0, YL1, YR1, YO1, ZM0, ZM1, ZN0, ZN1 = range(16)


def gather_kernel(wk_ref, wv_ref, tok_ref, out, tok_out, tok_t, w_ref, tin, tup, ssem, rsem, csem,
                  lsem, tsem, usem):
    s = Seat()
    m = s.y % 2
    right, left = s.at(dx=1), s.at(dx=-1)
    up, down = s.at(dy=1), s.at(dy=-1)
    partner, across = s.partner(), s.across()
    loads = [
        pltpu.make_async_copy(r, w_ref.at[i], lsem.at[2 + i]) for i, r in enumerate((wk_ref, wv_ref))
    ]
    read = pltpu.make_async_copy(tok_ref, tin, usem.at[0])
    for c in loads:
        c.start()
    read.start()
    meet((right, left, up, down, partner, across))
    for c in loads:
        c.wait()

    def part(mat, shard, h):
        return out.at[mat, shard, pl.ds(HALVES[h][0], HALVES[h][1])]

    def mine(mat, h):
        return w_ref.at[mat, pl.ds(HALVES[h][0], HALVES[h][1])]

    def place(k, core):
        hi = (s.zhi + core) % 2
        if k >= ZM0:
            return part(m if k < ZN0 else 1 - m, (1 - s.zhi) * 4 + s.x, (k - ZM0) % 2)
        dx, h = {
            L0: (3, 0), L1: (3, 1), R0: (1, 0), R1: (1, 1), O0: (2, 0), O1: (2, 1),
            YL0: (3, 0), YR0: (1, 0), YO0: (2, 0), YL1: (3, 1), YR1: (1, 1), YO1: (2, 1),
        }[k]
        return part(m if k < YL0 else 1 - m, hi * 4 + (s.x + dx) % 4, h)

    swap = remote(tok_ref, tok_out, tsem.at[0], tsem.at[1], partner)
    owns = [
        pltpu.make_async_copy(w_ref.at[i], out.at[i, s.img], lsem.at[i]) for i in range(2)
    ]
    sent = []

    def send(src, dst, k, device, sems, start=True):
        slot = len(sent)
        c = remote(src, dst, ssem.at[slot], sems.at[k], device)
        sent.append(c)
        if start:
            c.start()
        return c

    is0, is1 = s.core == 0, s.core == 1
    hi = (s.zhi + s.core) % 2
    seed = hi * 4 + s.x

    zs = [
        send(mine(mat, h), part(mat, s.img, h), k, across, rsem, False)
        for k, mat, h in ((ZM0, m, 0), (ZM1, m, 1), (ZN0, 1 - m, 0), (ZN1, 1 - m, 1))
    ]
    first = [
        (send(mine(m, h), part(m, s.img, h), k, d, rsem, False), h)
        for h, k, d in ((0, L0, right), (1, R1, left), (1, L1, right), (0, R0, left))
    ]
    second = [
        (remote(part(m, seed, h), part(m, seed, h), ssem.at[4 + i], rsem.at[k], d), h)
        for i, (h, k, d) in enumerate(((0, L0, right), (1, R1, left), (1, L1, right), (0, R0, left)))
    ]

    @pl.when(is1)
    def _():
        for c in zs:
            c.start()

    @pl.when(is0)
    def _():
        for c, _h in first:
            c.start()

    for c in owns:
        c.start()
    swap.start()
    read.wait()
    depth = tok_ref.shape[0]
    whole = depth // ROWS
    rest = depth - whole * ROWS

    def flip(i, _):
        at = pl.ds(pl.multiple_of(i * ROWS, ROWS), ROWS)
        tup[:, at] = jnp.transpose(tin[at])
        return 0

    lax.fori_loop(0, whole, flip, 0)
    at = pl.ds(whole * ROWS, rest)
    tup[:, at] = jnp.transpose(tin[at])
    write = pltpu.make_async_copy(tup, tok_t, usem.at[1])
    write.start()

    def got(k, sems, core):
        ref = place(k, core)
        pltpu.make_async_copy(ref, ref, sems.at[k]).wait()

    chips = {}

    def onchip(k, start=True):
        ref = place(k, s.core)
        chips[k] = send(ref, ref, k, partner, csem, start)

    for k in (ZM0, ZM1, ZN0, ZN1):
        onchip(k, False)

    @pl.when(is1)
    def _():
        for h, k in ((0, ZM0), (1, ZM1)):
            got(k, rsem, s.core)
            for c, ch in second:
                if ch == h:
                    c.start()
            chips[k].start()

    def arrive(k):
        got(k, rsem, s.core)
        ref = place(k, s.core)
        if k == L0:
            send(ref, ref, O0, right, rsem)
        if k == R1:
            send(ref, ref, O1, left, rsem)
        for a, b, d in (
            (L0, YL0, up), (R0, YR0, up), (O0, YO0, up),
            (L1, YL1, down), (R1, YR1, down), (O1, YO1, down),
        ):
            if k == a:
                send(ref, ref, b, d, rsem)
        onchip(k)

    for k in (L0, R1, L1, R0, YL0, YR1):
        arrive(k)

    @pl.when(is1)
    def _():
        for k in (ZN0, ZN1):
            got(k, rsem, s.core)
            chips[k].start()

    for k in (O0, O1, YR0, YL1, YO0, YO1):
        arrive(k)

    for k in range(ZM0):
        got(k, csem, 1 - s.core)

    @pl.when(is0)
    def _():
        for k in (ZM0, ZM1, ZN0, ZN1):
            got(k, csem, 1 - s.core)

    conditional = {id(c) for c in zs} | {id(chips[k]) for k in (ZM0, ZM1, ZN0, ZN1)}
    for c in sent:
        if id(c) not in conditional:
            c.wait_send()

    @pl.when(is1)
    def _():
        for c in zs:
            c.wait_send()
        for k in (ZM0, ZM1, ZN0, ZN1):
            chips[k].wait_send()

    for c in owns:
        c.wait()
    swap.wait()
    write.wait()


def gather(wk, wv, tok):
    rows, cols = wk.shape
    hbm = pl.BlockSpec(memory_space=pl.ANY)
    return pl.pallas_call(
        gather_kernel,
        name="gather",
        out_shape=(
            jax.ShapeDtypeStruct((2, 8, rows, cols), BF),
            jax.ShapeDtypeStruct(tok.shape, BF),
            jax.ShapeDtypeStruct(tok.shape[::-1], BF),
        ),
        in_specs=[hbm] * 3,
        out_specs=(hbm,) * 3,
        scratch_shapes=[
            pltpu.VMEM((2, rows, cols), BF),
            pltpu.VMEM(tok.shape, BF),
            pltpu.VMEM(tok.shape[::-1], BF),
            DMA((40,)), DMA((16,)), DMA((16,)), DMA((4,)), DMA((2,)), DMA((2,)),
        ],
        compiler_params=params(1),
    )(wk, wv, tok)


def split(a):
    hi = a.astype(BF)
    return hi, (a - hi.astype(F32)).astype(BF)


def same_head():
    r = lax.broadcasted_iota(jnp.int32, (LANE, LANE), 0) // HD
    c = lax.broadcasted_iota(jnp.int32, (LANE, LANE), 1) // HD
    return r == c


def fold(block, mask):
    b = jnp.where(mask, block, 0.0)
    return b[0:32] + b[32:64] + b[64:96] + b[96:128]


def unfold(state, mask):
    return jnp.where(mask, jnp.concatenate([state] * 4, axis=0), 0.0)


def put_state(ref, state, row):
    ref[0:4] = state.reshape(4, 8, LANE)
    ref[4] = jnp.broadcast_to(row, (8, LANE))


def dot(a, b):
    return lax.dot_general(a, b, (((1,), (0,)), ((), ())), preferred_element_type=F32)


def dot_t(a, b):
    return lax.dot_general(a, b, (((0,), (0,)), ((), ())), preferred_element_type=F32)


def inside(shape, width):
    lane = lax.broadcasted_iota(jnp.int32, shape, 1) + pl.program_id(0) * LANE
    return lane < width


SHARE = 3


def peers_of(s):
    places = [(s.sp + k) % 16 for k in range(16)]
    return places, [{"img": s.img, "sp": p} for p in places]


def share(ref, place):
    return ref.at[pl.ds(place * SHARE, SHARE)]


def total(s, part, sums, slots, sems):
    places, devs = peers_of(s)
    me = s.sp
    out, back = [], []
    for k in range(1, 16):
        c = remote(share(part, places[k]), slots.at[k], sems.at[0, k], sems.at[1, k], devs[k])
        c.start()
        out.append(c)
    acc = share(part, me)[...]
    for k in range(1, 16):
        out[k - 1].wait_recv()
        acc = acc + slots[k]
    mine = share(sums, me)
    mine[...] = acc
    for k in range(1, 16):
        c = remote(mine, mine, sems.at[2, k], sems.at[3, k], devs[k])
        c.start()
        back.append(c)
    for k in range(1, 16):
        ref = share(sums, (me + 16 - k) % 16)
        pltpu.make_async_copy(ref, ref, sems.at[3, k]).wait()
    for c in out + back:
        c.wait_send()


def project_kernel(width, tok_ref, w_ref, kv_ref, out_ref, part, sums, slots, sems):
    s = Seat()
    g = pl.program_id(0)
    bar = pltpu.get_barrier_semaphore()

    @pl.when(g == 0)
    def _():
        for d in peers_of(s)[1][1:]:
            pl.semaphore_signal(bar, inc=1, device_id=d, device_id_type=MESH)
        part[45:48] = jnp.zeros((3, 8, LANE), F32)

    both = jnp.concatenate([w_ref[0], w_ref[1]], axis=1)
    acc = dot(tok_ref[...], both)
    ok = inside((acc.shape[0], LANE), width)
    key = jnp.where(ok, jnp.maximum(acc[:, :LANE], 0.0), 0.0).astype(BF)
    val = jnp.where(ok, acc[:, LANE:], 0.0).astype(BF)
    kv_ref[0] = key
    kv_ref[1] = val
    put_state(
        part.at[pl.ds(5 * g, 5)],
        fold(dot_t(key, val), same_head()),
        jnp.sum(key.astype(F32), axis=0, keepdims=True),
    )

    @pl.when(g == pl.num_programs(0) - 1)
    def _():
        pl.semaphore_wait(bar, 15)
        total(s, part, sums, slots, sems)
        out_ref[...] = sums[...]


def project(tok, w):
    count, depth = tok.shape
    width = w.shape[2]
    steps = pl.cdiv(width, LANE)
    tiles = (48, 8, LANE)
    return pl.pallas_call(
        lambda *r: project_kernel(width, *r),
        name="project",
        grid=(steps,),
        out_shape=(
            jax.ShapeDtypeStruct((2, count, width), BF),
            jax.ShapeDtypeStruct(tiles, F32),
        ),
        in_specs=[
            pl.BlockSpec((count, depth), lambda g: (0, 0)),
            pl.BlockSpec((2, depth, LANE), lambda g: (0, 0, g)),
        ],
        out_specs=(
            pl.BlockSpec((2, count, LANE), lambda g: (0, 0, g)),
            pl.BlockSpec(tiles, lambda g: (0, 0, 0)),
        ),
        scratch_shapes=[
            pltpu.VMEM(tiles, F32),
            pltpu.VMEM(tiles, F32),
            pltpu.VMEM((16, SHARE, 8, LANE), F32),
            DMA((4, 16)),
        ],
        compiler_params=params(2),
    )(tok, w)


def dot_r(a, b):
    return lax.dot_general(a, b, (((1,), (1,)), ((), ())), preferred_element_type=F32)


def attend_kernel(width, q_ref, g_ref, st_ref, att_ref, dq_ref, part_ref):
    mask = same_head()
    state = st_ref[0:4].reshape(32, LANE)
    row = jnp.broadcast_to(st_ref[4][0:1], (LANE, LANE))
    col = jnp.transpose(row)[:, 0:1]
    kv = unfold(state, mask)
    kvh, kvl = split(kv)
    kvth, kvtl = split(jnp.transpose(kv))
    nh, nl = split(jnp.where(mask, row, 0.0))
    line = lax.broadcasted_iota(jnp.int32, q_ref.shape, 0) + pl.program_id(0) * LANE
    ok = line < width
    zero = jnp.zeros((), BF)
    q = jnp.where(ok, jnp.maximum(q_ref[...], zero), zero)
    g = jnp.where(ok, g_ref[...], zero).astype(F32)
    fwd = jnp.concatenate(
        [jnp.concatenate([kvth, kvtl], axis=1), jnp.concatenate([nh, nl], axis=1)], axis=0
    )
    both = dot(fwd, jnp.concatenate([q, q], axis=0))
    inv = 1.0 / (both[LANE:] + EPS_DEN)
    attn = both[:LANE] * inv
    att_ref[...] = attn.astype(BF)
    d_num = g * inv
    ones = jnp.where(mask, 1.0, 0.0).astype(BF)
    dots = dot(
        jnp.concatenate([ones, ones], axis=1), jnp.concatenate(split(g * attn), axis=0)
    )
    d_den = -dots * inv
    dnh, dnl = split(d_num)
    feat = dot(jnp.concatenate([kvh, kvh], axis=1), jnp.concatenate([dnh, dnl], axis=0))
    feat = feat + dot(kvl, dnh) + d_den * col
    dq_ref[...] = jnp.where(q > 0, feat, 0.0).astype(BF)
    gs = dot_r(q, jnp.concatenate([dnh, dnl], axis=0))
    gn = jnp.sum(d_den * q.astype(F32), axis=1, keepdims=True)
    put_state(
        part_ref,
        fold(gs[:, :LANE] + gs[:, LANE:], mask),
        jnp.transpose(jnp.broadcast_to(gn, (LANE, LANE)))[0:1],
    )


def attend(q, g, state):
    width, count = q.shape
    lines = pl.BlockSpec((LANE, count), lambda i: (i, 0))
    tiles = pl.BlockSpec((5, 8, LANE), lambda i: (i, 0, 0))
    return pl.pallas_call(
        lambda *r: attend_kernel(width, *r),
        name="attend",
        grid=(pl.cdiv(width, LANE),),
        out_shape=(
            jax.ShapeDtypeStruct((width, count), BF),
            jax.ShapeDtypeStruct((width, count), BF),
            jax.ShapeDtypeStruct((48, 8, LANE), F32),
        ),
        in_specs=[lines, lines, tiles],
        out_specs=(lines, lines, tiles),
        compiler_params=params(),
    )(q, g, state)


PIECE = 72
OFFS = (0, 72, 144, 208)
CUT = 640
SPLIT = 512
BAND = 448


def finish_kernel(scale, tok_img, part_ref, kv_ref, tok_ref, tok2_ref, w_ref, ok_ref, ov_ref, dt_ref,
                  cat, dcat, dboth, kvb, sums, slots, gp, relay, final, comb, res1, relay2, final2,
                  res2, zbuf, fin, wbuf, tbuf, ssem, rsem, lsem, csem, wsem, osem, tsem):
    s = Seat()
    core = s.core
    x_r, x_l, y_r, y_l = s.at(dx=1), s.at(dx=-1), s.at(dy=1), s.at(dy=-1)
    right1, left1 = s.at(dx=1 - core, dy=core), s.at(dx=core - 1, dy=-core)
    right2, left2 = s.at(dx=core, dy=1 - core), s.at(dx=-core, dy=core - 1)
    me1 = s.x * (1 - core) + s.y * core
    me2 = s.y * (1 - core) + s.x * core
    across, beside, partner = s.across(), s.beside(), s.partner()
    count, width = kv_ref.shape[1:]

    def loader(src, dst, i):
        return pltpu.make_async_copy(src, dst, lsem.at[i])

    lo, up = pl.ds(0, count), pl.ds(count, count)
    ld = [
        loader(kv_ref, kvb, 0),
        loader(tok_ref, cat.at[:, :, lo], 1),
        loader(tok2_ref, cat.at[:, :, up], 2),
    ]
    for c in ld:
        c.start()
    bands = w_ref.shape[1] // BAND

    def band_load(i):
        at = pl.ds(i * BAND, BAND)
        return pltpu.make_async_copy(w_ref.at[:, at], wbuf.at[i % 2], wsem.at[i])

    band_load(0).start()
    band_load(1).start()
    meet([x_r, x_l, across] + peers_of(s)[1][1:])
    total(s, part_ref, sums, slots, tsem)
    ld[0].wait()
    mask = same_head()

    def swap(i):
        at = pl.ds((0, SPLIT)[i], (SPLIT, width - SPLIT)[i])
        return remote(
            dboth.at[1 - core, :, at], dcat.at[up, at], ssem.at[22 + i], rsem.at[18 + i], partner
        )

    def features(g, at, n):
        gs = unfold(sums[pl.ds(5 * g, 4)].reshape(32, LANE) * tok_img, mask)[:n, :n]
        row = sums[5 * g + 4][0:1, :n] * tok_img
        gh, gl = split(gs)
        th, tl = split(jnp.transpose(gs))
        key, val = kvb[0, :, at], kvb[1, :, at]

        def twice(a, h, l):
            if n < LANE:
                return dot(a, h) + dot(a, l)
            return dot(jnp.concatenate([a, a], axis=1), jnp.concatenate([h, l], axis=0))

        dk = jnp.where(key > 0, twice(val, th, tl) + row, 0.0).astype(BF)
        dv = twice(key, gh, gl).astype(BF)
        dboth[0, :, at] = dk
        dboth[1, :, at] = dv
        dcat[lo, at] = jnp.where(core == 0, dk.astype(F32), dv.astype(F32)).astype(BF)

    def tile(g, _):
        features(g, pl.ds(pl.multiple_of(g * LANE, LANE), LANE), LANE)
        return 0

    lax.fori_loop(0, SPLIT // LANE, tile, 0)
    swap(0).start()
    lax.fori_loop(SPLIT // LANE, width // LANE, tile, 0)
    tail = width - width // LANE * LANE
    features(width // LANE, pl.ds(width - tail, tail), tail)
    swap(1).start()

    pending = []

    def copy(src, dst, i, device):
        return remote(src, dst, ssem.at[i], rsem.at[i], device)

    def go(src, dst, i, device):
        c = copy(src, dst, i, device)
        c.start()
        pending.append(c)

    def arrived(ref, sem):
        pltpu.make_async_copy(ref, ref, sem).wait()

    def nxt(v, k):
        return (v + k) % 4

    def bands_out(i):
        at = pl.ds(i * BAND, BAND)
        return pltpu.make_async_copy(tbuf.at[i % 2], dt_ref.at[at], osem.at[i])

    def band(i):
        band_load(i).wait()
        if i >= 2:
            bands_out(i - 2).wait()
        both = wbuf.at[i % 2]
        v = dot_r(both[0], dboth[0]) + dot_r(both[1], dboth[1])
        tbuf[i % 2] = v.astype(BF)
        bands_out(i).start()
        if i + 2 < bands:
            band_load(i + 2).start()

    def shard(h, dx):
        xx = nxt(s.x, dx)
        v = dot(cat[h * 4 + xx], dcat[...])
        for y in range(4):
            c = xx * (1 - core) + y * core
            j = y * (1 - core) + xx * core
            gp[h, c, j] = v[OFFS[y] : OFFS[y] + PIECE].astype(BF)

        @pl.when(core == 1)
        def _():
            j = xx
            d = (right1, left1)
            copy(gp.at[h, nxt(me1, 2), j], relay.at[h, j], h, d[h]).start()
            if h == 1:
                copy(gp.at[1, nxt(me1, 1), j], final.at[0, 1, j], 2, right1).start()
            else:
                copy(gp.at[0, nxt(me1, 3), j], final.at[1, 0, j], 3, left1).start()

        act = {
            (0, 2): (relay.at[0], 0, right1),
            (1, 2): (relay.at[1], 1, left1),
            (1, 1): (final.at[0, 1], 2, right1),
            (0, 3): (final.at[1, 0], 3, left1),
        }.get((h, dx))
        if act is not None:
            dst, i, dev = act

            @pl.when(core == 0)
            def _():
                copy(gp.at[h, nxt(me1, dx)], dst, i, dev).start()

    def add(dst, *srcs):
        def body(j, _):
            v = srcs[0][j].astype(F32)
            for r in srcs[1:]:
                v = v + r[j].astype(F32)
            dst[j] = v.astype(BF)
            return 0

        lax.fori_loop(0, 4, body, 0)

    def combine():
        arrived(relay.at[0], rsem.at[0])
        add(comb.at[0], gp.at[0, nxt(me1, 1)], relay.at[0])
        copy(comb.at[0], final.at[0, 0], 4, right1).start()
        arrived(relay.at[1], rsem.at[1])
        add(comb.at[1], gp.at[1, nxt(me1, 3)], relay.at[1])
        copy(comb.at[1], final.at[1, 1], 5, left1).start()

    for c in ld[1:]:
        c.wait()
    swap(0).wait()
    swap(1).wait()
    for h, dx in ((0, 2), (1, 2), (1, 1), (0, 3), (0, 1), (1, 3)):
        shard(h, dx)

    @pl.when(core == 0)
    def _():
        combine()

    shard(0, 0)
    shard(1, 0)

    @pl.when(core == 1)
    def _():
        combine()

    for i, dst in enumerate(
        (relay.at[0], relay.at[1], final.at[0, 1], final.at[1, 0], final.at[0, 0], final.at[1, 1])
    ):
        pending.append(copy(dst, dst, i, right1))

    band(0)
    band(1)
    band(2)
    arrived(final.at[1, 0], rsem.at[3])
    arrived(final.at[0, 1], rsem.at[2])
    arrived(final.at[0, 0], rsem.at[4])
    add(res1.at[0], gp.at[0, me1], final.at[0, 0], final.at[1, 0])

    go(res1.at[0, nxt(me2, 2)], relay2.at[0], 6, right2)
    arrived(final.at[1, 1], rsem.at[5])
    add(res1.at[1], gp.at[1, me1], final.at[0, 1], final.at[1, 1])
    go(res1.at[1, nxt(me2, 2)], relay2.at[1], 7, left2)
    go(res1.at[1, nxt(me2, 1)], final2.at[0, 1], 8, right2)
    go(res1.at[0, nxt(me2, 3)], final2.at[1, 0], 9, left2)
    band(3)

    def plus(*refs):
        v = refs[0][...].astype(F32)
        for r in refs[1:]:
            v = v + r[...].astype(F32)
        return v.astype(BF)

    arrived(relay2.at[0], rsem.at[6])
    relay2[0] = plus(relay2.at[0], res1.at[0, nxt(me2, 1)])
    go(relay2.at[0], final2.at[0, 0], 10, right2)
    arrived(relay2.at[1], rsem.at[7])
    relay2[1] = plus(relay2.at[1], res1.at[1, nxt(me2, 3)])
    go(relay2.at[1], final2.at[1, 1], 11, left2)
    band(4)
    arrived(final2.at[1, 0], rsem.at[9])
    arrived(final2.at[0, 1], rsem.at[8])
    arrived(final2.at[0, 0], rsem.at[10])
    res2[0] = plus(res1.at[0, me2], final2.at[0, 0], final2.at[1, 0])
    arrived(final2.at[1, 1], rsem.at[11])
    res2[1] = plus(res1.at[1, me2], final2.at[0, 1], final2.at[1, 1])

    go(res2.at[1 - s.zhi], zbuf.at[0], 12, across)
    arrived(zbuf.at[0], rsem.at[12])
    zbuf[2] = plus(res2.at[s.zhi], zbuf.at[0])
    go(zbuf.at[2], zbuf.at[1], 13, beside)
    arrived(zbuf.at[1], rsem.at[13])
    mine = fin.at[core, s.y]
    mine[...] = plus(zbuf.at[1], zbuf.at[2])

    yd, yu, yo = (s.y + 3) % 4, (s.y + 1) % 4, (s.y + 2) % 4
    go(mine, mine, 14, y_r)
    go(mine, mine, 15, y_l)

    def chip(ref, k):
        c = remote(ref, ref, ssem.at[k], csem.at[k - 18], partner)
        c.start()
        pending.append(c)

    chip(mine, 18)
    a, b = pl.ds(0, CUT), pl.ds(CUT, mine.shape[1] - CUT)
    arrived(fin.at[core, yd], rsem.at[14])
    go(fin.at[core, yd, :, a], fin.at[core, yd, :, a], 16, y_r)
    chip(fin.at[core, yd], 19)
    arrived(fin.at[core, yu], rsem.at[15])
    go(fin.at[core, yu, :, b], fin.at[core, yu, :, b], 17, y_l)
    chip(fin.at[core, yu], 20)
    arrived(fin.at[core, yo, :, a], rsem.at[16])
    arrived(fin.at[core, yo, :, b], rsem.at[17])
    chip(fin.at[core, yo], 21)
    for k, y in enumerate((s.y, yd, yu, yo)):
        arrived(fin.at[1 - core, y], csem.at[k])
    for c in pending:
        c.wait_send()
    for i in (bands - 2, bands - 1):
        bands_out(i).wait()
    for ref, i in ((ok_ref, 0), (ov_ref, 1)):
        for y in range(3):
            ref[pl.ds(PIECE * y, PIECE)] = fin[i, y].astype(F32) * scale
        ref[pl.ds(216, 64)] = fin[i, 3].astype(F32)[8:] * scale


def finish(part, kv, tok, tok2, w, scale, tok_img):
    _, count, width = kv.shape
    depth = tok.shape[0]
    rows = depth // 8
    vm = pl.BlockSpec(memory_space=pltpu.VMEM)
    hbm = pl.BlockSpec(memory_space=pl.ANY)
    p = (PIECE, width)
    return pl.pallas_call(
        lambda *r: finish_kernel(scale, tok_img, *r),
        name="finish",
        out_shape=(jax.ShapeDtypeStruct((rows, width), F32),) * 2
        + (jax.ShapeDtypeStruct((depth, count), BF),),
        in_specs=[vm] + [hbm] * 4,
        out_specs=(vm, vm, hbm),
        scratch_shapes=[
            pltpu.VMEM((8, rows, 2 * count), BF),
            pltpu.VMEM((2 * count, width), BF),
            pltpu.VMEM((2, count, width), BF),
            pltpu.VMEM((2, count, width), BF),
            pltpu.VMEM(part.shape, F32),
            pltpu.VMEM((16, SHARE, 8, LANE), F32),
            pltpu.VMEM((2, 4, 4) + p, BF),
            pltpu.VMEM((2, 4) + p, BF),
            pltpu.VMEM((2, 2, 4) + p, BF),
            pltpu.VMEM((2, 4) + p, BF),
            pltpu.VMEM((2, 4) + p, BF),
            pltpu.VMEM((2,) + p, BF),
            pltpu.VMEM((2, 2) + p, BF),
            pltpu.VMEM((2,) + p, BF),
            pltpu.VMEM((3,) + p, BF),
            pltpu.VMEM((2, 4) + p, BF),
            pltpu.VMEM((2, 2, BAND, width), BF),
            pltpu.VMEM((2, BAND, count), BF),
            DMA((24,)), DMA((20,)), DMA((3,)), DMA((4,)), DMA((5,)), DMA((5,)), DMA((4, 16)),
        ],
        compiler_params=params(5),
    )(part, kv, tok.reshape(8, rows, count), tok2.reshape(8, rows, count), w)


def body(tokens, queries, w_key, w_value, cotangent):
    tok = jnp.transpose(tokens[0])
    depth, count = tok.shape
    width = w_key.shape[1]
    tok_img = count * lax.axis_size("sp")
    images = lax.axis_size("img")
    w4, tok2, tok_t = gather(w_key, w_value, tok)
    w = w4.reshape(2, depth, width)
    kv, state = project(tok_t, w)
    att, dq, part = attend(jnp.transpose(queries[0]), jnp.transpose(cotangent[0]), state)
    scale = float((images * tok_img) ** -0.5)
    dwk, dwv, dt = finish(part, kv, tok, tok2, w, scale, float(tok_img))
    return jnp.transpose(att)[None], jnp.transpose(dt)[None], jnp.transpose(dq)[None], dwk, dwv


def solution(mesh):
    rows, flat = P("img", "sp", None), P("img", None)
    return jax.shard_map(
        body,
        mesh=mesh,
        in_specs=(rows, rows, flat, flat, rows),
        out_specs=(rows, rows, rows, flat, flat),
        check_vma=False,
    )
```

```python
import jax
import jax.numpy as jnp
from jax import lax
from jax.experimental import pallas as pl
from jax.experimental.pallas import tpu as pltpu
from jax.sharding import PartitionSpec as P

HD = 32
EPS_DEN = 1e-06
BF = jnp.bfloat16
F32 = jnp.float32
MESH = pl.DeviceIdType.MESH
LANE = 128
ROWS = 256
VMEM_MAX = 64 * 1024 * 1024 - 65536
DMA = pltpu.SemaphoreType.DMA


def params(cid=None, sem=None):
    return pltpu.CompilerParams(
        collective_id=cid,
        has_side_effects=cid is not None,
        vmem_limit_bytes=VMEM_MAX,
        dimension_semantics=sem,
    )


class Seat:
    def __init__(self):
        img, sp = lax.axis_index("img"), lax.axis_index("sp")
        self.img, self.sp = img, sp
        self.zhi, self.x = img // 4, img % 4
        self.y, self.zlo, self.core = sp // 4, (sp // 2) % 2, sp % 2

    def at(self, dx=0, dy=0, hi=None, lo=None, core=None):
        x = (self.x + dx + 4) % 4
        y = (self.y + dy + 4) % 4
        hi = self.zhi if hi is None else hi
        lo = self.zlo if lo is None else lo
        core = self.core if core is None else core
        return {"img": hi * 4 + x, "sp": (y * 2 + lo) * 2 + core}

    def across(self):
        return self.at(hi=1 - self.zhi, lo=1 - self.zlo)

    def beside(self):
        return self.at(lo=1 - self.zlo)

    def partner(self):
        return self.at(core=1 - self.core)


def meet(devices):
    bar = pltpu.get_barrier_semaphore()
    for d in devices:
        pl.semaphore_signal(bar, inc=1, device_id=d, device_id_type=MESH)
    pl.semaphore_wait(bar, len(devices))


def remote(src, dst, ssem, rsem, device):
    return pltpu.make_async_remote_copy(
        src_ref=src, dst_ref=dst, send_sem=ssem, recv_sem=rsem, device_id=device, device_id_type=MESH
    )


HALVES = ((0, 144), (144, 136))
L0, L1, R0, R1, O0, O1, YL0, YR0, YO0, YL1, YR1, YO1, ZM0, ZM1, ZN0, ZN1 = range(16)


PHASES = ((0, 640), (640, 480))
READY = 5


def gather_kernel(wk_ref, wv_ref, tok_ref, out, tok_out, kv_out, state_out, w_ref, tin, tup, wt, wlast,
                  kvb, part, sums, slots, ssem, rsem, csem, lsem, tsem, usem, wsem, sems):
    s = Seat()
    m = s.y % 2
    width = wk_ref.shape[1]
    rows = wk_ref.shape[0]
    right, left = s.at(dx=1), s.at(dx=-1)
    up, down = s.at(dy=1), s.at(dy=-1)
    partner, across = s.partner(), s.across()
    loads = [
        pltpu.make_async_copy(r, w_ref.at[i], lsem.at[2 + i]) for i, r in enumerate((wk_ref, wv_ref))
    ]
    read = pltpu.make_async_copy(tok_ref, tin, usem.at[0])
    for c in loads:
        c.start()
    read.start()
    meet([right, left, across] + peers_of(s)[1][1:])
    for c in loads:
        c.wait()

    def spot(mat, shard, h, p):
        row = pl.multiple_of(shard * rows + HALVES[h][0], 8)
        return out.at[mat, pl.ds(row, HALVES[h][1]), pl.ds(*PHASES[p])]

    def mine(mat, h, p):
        return w_ref.at[mat, pl.ds(*HALVES[h]), pl.ds(*PHASES[p])]

    def place(k, core, p):
        hi = (s.zhi + core) % 2
        if k >= ZM0:
            return spot(m if k < ZN0 else 1 - m, (1 - s.zhi) * 4 + s.x, (k - ZM0) % 2, p)
        dx, h = {
            L0: (3, 0), L1: (3, 1), R0: (1, 0), R1: (1, 1), O0: (2, 0), O1: (2, 1),
            YL0: (3, 0), YR0: (1, 0), YO0: (2, 0), YL1: (3, 1), YR1: (1, 1), YO1: (2, 1),
        }[k]
        return spot(m if k < YL0 else 1 - m, hi * 4 + (s.x + dx) % 4, h, p)

    is0, is1 = s.core == 0, s.core == 1
    hi = (s.zhi + s.core) % 2
    seed = hi * 4 + s.x
    always, second = [], []

    def new(src, dst, k, p, device, sem, only1=False):
        slot = len(always) + len(second)
        c = remote(src, dst, ssem.at[slot], sem.at[p, k], device)
        (second if only1 else always).append(c)
        return c

    zs, seeds0, seeds1, onward, chips = {}, {}, {}, {}, {}
    for p in range(2):
        for k, mat, h in ((ZM0, m, 0), (ZM1, m, 1), (ZN0, 1 - m, 0), (ZN1, 1 - m, 1)):
            zs[k, p] = new(mine(mat, h, p), spot(mat, s.img, h, p), k, p, across, rsem, True)
        for i, (h, k, d) in enumerate(((0, L0, right), (1, R1, left), (1, L1, right), (0, R0, left))):
            slot = ssem.at[len(always) + len(second)]
            there = spot(m, seed, h, p)
            seeds1[i, p] = remote(there, there, slot, rsem.at[p, k], d)
            seeds0[i, p] = new(mine(m, h, p), spot(m, s.img, h, p), k, p, d, rsem)
        for k, to, d in (
            (L0, O0, right), (R1, O1, left),
            (L0, YL0, up), (R0, YR0, up), (O0, YO0, up),
            (L1, YL1, down), (R1, YR1, down), (O1, YO1, down),
        ):
            ref = place(k, s.core, p)
            onward.setdefault((k, p), []).append(new(ref, ref, to, p, d, rsem))
        for k in range(16):
            ref = place(k, s.core, p)
            chips[k, p] = new(ref, ref, k, p, partner, csem, k >= ZM0)

    def got(k, p, sem, core):
        ref = place(k, core, p)
        pltpu.make_async_copy(ref, ref, sem.at[p, k]).wait()

    def arrive(p, *ks):
        for k in ks:
            got(k, p, rsem, s.core)
            for c in onward.get((k, p), ()):
                c.start()
            chips[k, p].start()

    def across_in(p, *ks):
        @pl.when(is1)
        def _():
            for k in ks:
                arrive(p, k)
                if k in (ZM0, ZM1):
                    h = k - ZM0
                    for i in ((0, 3), (1, 2))[h]:
                        seeds1[i, p].start()

    def seed0(p, *which):
        @pl.when(is0)
        def _():
            for i in which:
                seeds0[i, p].start()

    def settled(p):
        for k in range(ZM0):
            got(k, p, csem, 1 - s.core)

        @pl.when(is0)
        def _():
            for k in range(ZM0, 16):
                got(k, p, csem, 1)

    @pl.when(is1)
    def _():
        for k, p in (
            (ZM0, 0), (ZM1, 0), (ZM0, 1), (ZM1, 1), (ZN0, 0), (ZN1, 0), (ZN0, 1), (ZN1, 1)
        ):
            zs[k, p].start()

    seed0(0, 0, 1, 2, 3)
    seed0(1, 0, 1)
    swap = remote(tok_ref, tok_out, tsem.at[0], tsem.at[1], partner)
    owns = [
        pltpu.make_async_copy(
            w_ref.at[i],
            out.at[i, pl.ds(pl.multiple_of(s.img * rows, 8), rows)],
            lsem.at[i],
        )
        for i in range(2)
    ]
    for c in owns:
        c.start()
    read.wait()
    depth = tok_ref.shape[0]
    whole = depth // ROWS
    rest = depth - whole * ROWS

    def flip(i, _):
        at = pl.ds(pl.multiple_of(i * ROWS, ROWS), ROWS)
        tup[:, at] = jnp.transpose(tin[at])
        return 0

    lax.fori_loop(0, whole, flip, 0)
    at = pl.ds(whole * ROWS, rest)
    tup[:, at] = jnp.transpose(tin[at])
    across_in(0, ZM0, ZM1)
    across_in(1, ZM0, ZM1)
    arrive(0, L0, R1)
    seed0(1, 2, 3)
    arrive(0, L1, R0, YL0, YR1)
    swap.start()
    arrive(1, L0, R1)
    across_in(0, ZN0, ZN1)
    arrive(0, O0, O1, YR0, YL1)
    arrive(1, L1, R0)
    arrive(0, YO0, YO1)
    settled(0)
    for c in owns:
        c.wait()

    def tile_load(i):
        at = pl.ds(pl.multiple_of(i * LANE, LANE), LANE)
        slot = i % 2
        return [
            pltpu.make_async_copy(
                out.at[j, :, at], wt.at[slot, :, pl.ds(j * LANE, LANE)], wsem.at[slot]
            )
            for j in range(2)
        ]

    full = width // LANE
    tail = width - full * LANE
    last = pltpu.make_async_copy(out.at[:, :, pl.ds(full * LANE, tail)], wlast, usem.at[1])
    mask = same_head()
    part[45:48] = jnp.zeros((3, 8, LANE), F32)
    for c in tile_load(0):
        c.start()

    def keep(i, key, val, at):
        kvb[0, :, at] = key
        kvb[1, :, at] = val
        n = key.shape[1]
        state = dot_t(key, val)
        row = jnp.sum(key.astype(F32), axis=0, keepdims=True)
        if n < LANE:
            state = jnp.where(mask[:n, :n], state, 0.0)
            state = state[0:32] + state[32:64] + state[64:96]
            state = jnp.concatenate([state, jnp.zeros((32, LANE - n), F32)], axis=1)
            row = jnp.concatenate([row, jnp.zeros((1, LANE - n), F32)], axis=1)
        else:
            state = fold(state, mask)
        put_state(part.at[pl.ds(5 * i, 5)], state, row)

    def tile(i, _):
        @pl.when(i == 0)
        def _():
            arrive(1, O0, O1, YL0, YR1)

        @pl.when(i == 1)
        def _():
            across_in(1, ZN0, ZN1)
            arrive(1, YR0, YL1)

        @pl.when(i == 2)
        def _():
            arrive(1, YO0, YO1)

        @pl.when(i == READY)
        def _():
            settled(1)
            for c in tile_load(READY):
                c.start()
            last.start()

        slot = i % 2
        pltpu.make_async_copy(wt.at[slot], wt.at[slot], wsem.at[slot]).wait()

        @pl.when(jnp.logical_and(i + 1 < full, i + 1 != READY))
        def _():
            for c in tile_load(i + 1):
                c.start()

        acc = dot(tup[...], wt[slot])
        key = jnp.maximum(acc[:, :LANE], 0.0).astype(BF)
        keep(i, key, acc[:, LANE:].astype(BF), pl.ds(pl.multiple_of(i * LANE, LANE), LANE))
        return 0

    lax.fori_loop(0, full, tile, 0)
    last.wait()
    pad = jnp.zeros((depth, LANE - tail), BF)
    acc = dot(tup[...], jnp.concatenate([wlast[0], pad, wlast[1]], axis=1))
    key = jnp.maximum(acc[:, :tail], 0.0).astype(BF)
    keep(full, key, acc[:, LANE : LANE + tail].astype(BF), pl.ds(full * LANE, tail))
    kv_write = pltpu.make_async_copy(kvb, kv_out, usem.at[2])
    kv_write.start()
    total(s, part, sums, slots, sems)
    state_out[...] = sums[...]
    for c in always:
        c.wait_send()

    @pl.when(is1)
    def _():
        for c in second:
            c.wait_send()

    swap.wait()
    kv_write.wait()


def gather(wk, wv, tok):
    rows, cols = wk.shape
    depth, count = tok.shape
    hbm = pl.BlockSpec(memory_space=pl.ANY)
    vm = pl.BlockSpec(memory_space=pltpu.VMEM)
    tiles = (48, 8, LANE)
    return pl.pallas_call(
        gather_kernel,
        name="gather",
        out_shape=(
            jax.ShapeDtypeStruct((2, depth, cols), BF),
            jax.ShapeDtypeStruct(tok.shape, BF),
            jax.ShapeDtypeStruct((2, count, cols), BF),
            jax.ShapeDtypeStruct(tiles, F32),
        ),
        in_specs=[hbm] * 3,
        out_specs=(hbm, hbm, hbm, vm),
        scratch_shapes=[
            pltpu.VMEM((2, rows, cols), BF),
            pltpu.VMEM(tok.shape, BF),
            pltpu.VMEM(tok.shape[::-1], BF),
            pltpu.VMEM((2, depth, 2 * LANE), BF),
            pltpu.VMEM((2, depth, cols % LANE), BF),
            pltpu.VMEM((2, count, cols), BF),
            pltpu.VMEM(tiles, F32),
            pltpu.VMEM(tiles, F32),
            pltpu.VMEM((16, SHARE, 8, LANE), F32),
            DMA((64,)), DMA((2, 16)), DMA((2, 16)), DMA((4,)), DMA((2,)), DMA((3,)), DMA((2,)),
            DMA((4, 16)),
        ],
        compiler_params=params(1),
    )(wk, wv, tok)


def split(a):
    hi = a.astype(BF)
    return hi, (a - hi.astype(F32)).astype(BF)


def same_head():
    r = lax.broadcasted_iota(jnp.int32, (LANE, LANE), 0) // HD
    c = lax.broadcasted_iota(jnp.int32, (LANE, LANE), 1) // HD
    return r == c


def fold(block, mask):
    b = jnp.where(mask, block, 0.0)
    return b[0:32] + b[32:64] + b[64:96] + b[96:128]


def unfold(state, mask):
    return jnp.where(mask, jnp.concatenate([state] * 4, axis=0), 0.0)


def put_state(ref, state, row):
    ref[0:4] = state.reshape(4, 8, LANE)
    ref[4] = jnp.broadcast_to(row, (8, LANE))


def dot(a, b):
    return lax.dot_general(a, b, (((1,), (0,)), ((), ())), preferred_element_type=F32)


def dot_t(a, b):
    return lax.dot_general(a, b, (((0,), (0,)), ((), ())), preferred_element_type=F32)


SHARE = 3


def peers_of(s):
    places = [(s.sp + k) % 16 for k in range(16)]
    return places, [{"img": s.img, "sp": p} for p in places]


def share(ref, place):
    return ref.at[pl.ds(place * SHARE, SHARE)]


def total(s, part, sums, slots, sems):
    places, devs = peers_of(s)
    me = s.sp
    out, back = [], []
    for k in range(1, 16):
        c = remote(share(part, places[k]), slots.at[k], sems.at[0, k], sems.at[1, k], devs[k])
        c.start()
        out.append(c)
    acc = share(part, me)[...]
    for k in range(1, 16):
        out[k - 1].wait_recv()
        acc = acc + slots[k]
    mine = share(sums, me)
    mine[...] = acc
    for k in range(1, 16):
        c = remote(mine, mine, sems.at[2, k], sems.at[3, k], devs[k])
        c.start()
        back.append(c)
    for k in range(1, 16):
        ref = share(sums, (me + 16 - k) % 16)
        pltpu.make_async_copy(ref, ref, sems.at[3, k]).wait()
    for c in out + back:
        c.wait_send()


def dot_r(a, b):
    return lax.dot_general(a, b, (((1,), (1,)), ((), ())), preferred_element_type=F32)


def attend_kernel(width, q_ref, g_ref, st_ref, att_ref, dq_ref, part_ref):
    mask = same_head()
    state = st_ref[0:4].reshape(32, LANE)
    row = jnp.broadcast_to(st_ref[4][0:1], (LANE, LANE))
    col = jnp.transpose(row)[:, 0:1]
    kv = unfold(state, mask)
    kvh, kvl = split(kv)
    kvth, kvtl = split(jnp.transpose(kv))
    nh, nl = split(jnp.where(mask, row, 0.0))
    line = lax.broadcasted_iota(jnp.int32, q_ref.shape, 0) + pl.program_id(0) * LANE
    ok = line < width
    zero = jnp.zeros((), BF)
    q = jnp.where(ok, jnp.maximum(q_ref[...], zero), zero)
    g = jnp.where(ok, g_ref[...], zero).astype(F32)
    fwd = jnp.concatenate(
        [jnp.concatenate([kvth, kvtl], axis=1), jnp.concatenate([nh, nl], axis=1)], axis=0
    )
    both = dot(fwd, jnp.concatenate([q, q], axis=0))
    inv = 1.0 / (both[LANE:] + EPS_DEN)
    attn = both[:LANE] * inv
    att_ref[...] = attn.astype(BF)
    d_num = g * inv
    ones = jnp.where(mask, 1.0, 0.0).astype(BF)
    dots = dot(
        jnp.concatenate([ones, ones], axis=1), jnp.concatenate(split(g * attn), axis=0)
    )
    d_den = -dots * inv
    dnh, dnl = split(d_num)
    feat = dot(jnp.concatenate([kvh, kvh], axis=1), jnp.concatenate([dnh, dnl], axis=0))
    feat = feat + dot(kvl, dnh) + d_den * col
    dq_ref[...] = jnp.where(q > 0, feat, 0.0).astype(BF)
    gs = dot_r(q, jnp.concatenate([dnh, dnl], axis=0))
    gn = jnp.sum(d_den * q.astype(F32), axis=1, keepdims=True)
    put_state(
        part_ref,
        fold(gs[:, :LANE] + gs[:, LANE:], mask),
        jnp.transpose(jnp.broadcast_to(gn, (LANE, LANE)))[0:1],
    )


def attend(q, g, state):
    width, count = q.shape
    lines = pl.BlockSpec((LANE, count), lambda i: (i, 0))
    tiles = pl.BlockSpec((5, 8, LANE), lambda i: (i, 0, 0))
    return pl.pallas_call(
        lambda *r: attend_kernel(width, *r),
        name="attend",
        grid=(pl.cdiv(width, LANE),),
        out_shape=(
            jax.ShapeDtypeStruct((width, count), BF),
            jax.ShapeDtypeStruct((width, count), BF),
            jax.ShapeDtypeStruct((48, 8, LANE), F32),
        ),
        in_specs=[lines, lines, tiles],
        out_specs=(lines, lines, tiles),
        compiler_params=params(),
    )(q, g, state)


PIECE = 72
OFFS = (0, 72, 144, 208)
CUT = 640
SPLIT = 512
BAND = 448


def finish_kernel(scale, tok_img, part_ref, kv_ref, tok_ref, tok2_ref, w_ref, ok_ref, ov_ref, dt_ref,
                  cat, dcat, dboth, kvb, sums, slots, gp, relay, final, comb, res1, relay2, final2,
                  res2, zbuf, fin, wbuf, tbuf, ssem, rsem, lsem, csem, wsem, osem, tsem):
    s = Seat()
    core = s.core
    x_r, x_l, y_r, y_l = s.at(dx=1), s.at(dx=-1), s.at(dy=1), s.at(dy=-1)
    right1, left1 = s.at(dx=1 - core, dy=core), s.at(dx=core - 1, dy=-core)
    right2, left2 = s.at(dx=core, dy=1 - core), s.at(dx=-core, dy=core - 1)
    me1 = s.x * (1 - core) + s.y * core
    me2 = s.y * (1 - core) + s.x * core
    across, beside, partner = s.across(), s.beside(), s.partner()
    count, width = kv_ref.shape[1:]

    def loader(src, dst, i):
        return pltpu.make_async_copy(src, dst, lsem.at[i])

    lo, up = pl.ds(0, count), pl.ds(count, count)
    ld = [
        loader(kv_ref, kvb, 0),
        loader(tok_ref, cat.at[:, :, lo], 1),
        loader(tok2_ref, cat.at[:, :, up], 2),
    ]
    for c in ld:
        c.start()
    bands = w_ref.shape[1] // BAND

    def band_load(i):
        at = pl.ds(i * BAND, BAND)
        return pltpu.make_async_copy(w_ref.at[:, at], wbuf.at[i % 2], wsem.at[i])

    band_load(0).start()
    band_load(1).start()
    meet([x_r, x_l, across] + peers_of(s)[1][1:])
    total(s, part_ref, sums, slots, tsem)
    ld[0].wait()
    mask = same_head()

    def swap(i):
        at = pl.ds((0, SPLIT)[i], (SPLIT, width - SPLIT)[i])
        return remote(
            dboth.at[1 - core, :, at], dcat.at[up, at], ssem.at[22 + i], rsem.at[18 + i], partner
        )

    def features(g, at, n):
        gs = unfold(sums[pl.ds(5 * g, 4)].reshape(32, LANE) * tok_img, mask)[:n, :n]
        row = sums[5 * g + 4][0:1, :n] * tok_img
        gh, gl = split(gs)
        th, tl = split(jnp.transpose(gs))
        key, val = kvb[0, :, at], kvb[1, :, at]

        def twice(a, h, l):
            if n < LANE:
                return dot(a, h) + dot(a, l)
            return dot(jnp.concatenate([a, a], axis=1), jnp.concatenate([h, l], axis=0))

        dk = jnp.where(key > 0, twice(val, th, tl) + row, 0.0).astype(BF)
        dv = twice(key, gh, gl).astype(BF)
        dboth[0, :, at] = dk
        dboth[1, :, at] = dv
        dcat[lo, at] = jnp.where(core == 0, dk.astype(F32), dv.astype(F32)).astype(BF)

    def tile(g, _):
        features(g, pl.ds(pl.multiple_of(g * LANE, LANE), LANE), LANE)
        return 0

    lax.fori_loop(0, SPLIT // LANE, tile, 0)
    swap(0).start()
    lax.fori_loop(SPLIT // LANE, width // LANE, tile, 0)
    tail = width - width // LANE * LANE
    features(width // LANE, pl.ds(width - tail, tail), tail)
    swap(1).start()

    pending = []

    def copy(src, dst, i, device):
        return remote(src, dst, ssem.at[i], rsem.at[i], device)

    def go(src, dst, i, device):
        c = copy(src, dst, i, device)
        c.start()
        pending.append(c)

    def arrived(ref, sem):
        pltpu.make_async_copy(ref, ref, sem).wait()

    def nxt(v, k):
        return (v + k) % 4

    def bands_out(i):
        at = pl.ds(i * BAND, BAND)
        return pltpu.make_async_copy(tbuf.at[i % 2], dt_ref.at[at], osem.at[i])

    def band(i):
        band_load(i).wait()
        if i >= 2:
            bands_out(i - 2).wait()
        both = wbuf.at[i % 2]
        v = dot_r(both[0], dboth[0]) + dot_r(both[1], dboth[1])
        tbuf[i % 2] = v.astype(BF)
        bands_out(i).start()
        if i + 2 < bands:
            band_load(i + 2).start()

    def shard(h, dx):
        xx = nxt(s.x, dx)
        v = dot(cat[h * 4 + xx], dcat[...])
        for y in range(4):
            c = xx * (1 - core) + y * core
            j = y * (1 - core) + xx * core
            gp[h, c, j] = v[OFFS[y] : OFFS[y] + PIECE].astype(BF)

        @pl.when(core == 1)
        def _():
            j = xx
            d = (right1, left1)
            copy(gp.at[h, nxt(me1, 2), j], relay.at[h, j], h, d[h]).start()
            if h == 1:
                copy(gp.at[1, nxt(me1, 1), j], final.at[0, 1, j], 2, right1).start()
            else:
                copy(gp.at[0, nxt(me1, 3), j], final.at[1, 0, j], 3, left1).start()

        act = {
            (0, 2): (relay.at[0], 0, right1),
            (1, 2): (relay.at[1], 1, left1),
            (1, 1): (final.at[0, 1], 2, right1),
            (0, 3): (final.at[1, 0], 3, left1),
        }.get((h, dx))
        if act is not None:
            dst, i, dev = act

            @pl.when(core == 0)
            def _():
                copy(gp.at[h, nxt(me1, dx)], dst, i, dev).start()

    def add(dst, *srcs):
        def body(j, _):
            v = srcs[0][j].astype(F32)
            for r in srcs[1:]:
                v = v + r[j].astype(F32)
            dst[j] = v.astype(BF)
            return 0

        lax.fori_loop(0, 4, body, 0)

    def combine():
        arrived(relay.at[0], rsem.at[0])
        add(comb.at[0], gp.at[0, nxt(me1, 1)], relay.at[0])
        copy(comb.at[0], final.at[0, 0], 4, right1).start()
        arrived(relay.at[1], rsem.at[1])
        add(comb.at[1], gp.at[1, nxt(me1, 3)], relay.at[1])
        copy(comb.at[1], final.at[1, 1], 5, left1).start()

    for c in ld[1:]:
        c.wait()
    swap(0).wait()
    swap(1).wait()
    for h, dx in ((0, 2), (1, 2), (1, 1), (0, 3), (0, 1), (1, 3)):
        shard(h, dx)

    @pl.when(core == 0)
    def _():
        combine()

    shard(0, 0)
    shard(1, 0)

    @pl.when(core == 1)
    def _():
        combine()

    for i, dst in enumerate(
        (relay.at[0], relay.at[1], final.at[0, 1], final.at[1, 0], final.at[0, 0], final.at[1, 1])
    ):
        pending.append(copy(dst, dst, i, right1))

    band(0)
    band(1)
    band(2)
    arrived(final.at[1, 0], rsem.at[3])
    arrived(final.at[0, 1], rsem.at[2])
    arrived(final.at[0, 0], rsem.at[4])
    add(res1.at[0], gp.at[0, me1], final.at[0, 0], final.at[1, 0])

    go(res1.at[0, nxt(me2, 2)], relay2.at[0], 6, right2)
    arrived(final.at[1, 1], rsem.at[5])
    add(res1.at[1], gp.at[1, me1], final.at[0, 1], final.at[1, 1])
    go(res1.at[1, nxt(me2, 2)], relay2.at[1], 7, left2)
    go(res1.at[1, nxt(me2, 1)], final2.at[0, 1], 8, right2)
    go(res1.at[0, nxt(me2, 3)], final2.at[1, 0], 9, left2)
    band(3)

    def plus(*refs):
        v = refs[0][...].astype(F32)
        for r in refs[1:]:
            v = v + r[...].astype(F32)
        return v.astype(BF)

    arrived(relay2.at[0], rsem.at[6])
    relay2[0] = plus(relay2.at[0], res1.at[0, nxt(me2, 1)])
    go(relay2.at[0], final2.at[0, 0], 10, right2)
    arrived(relay2.at[1], rsem.at[7])
    relay2[1] = plus(relay2.at[1], res1.at[1, nxt(me2, 3)])
    go(relay2.at[1], final2.at[1, 1], 11, left2)
    band(4)
    arrived(final2.at[1, 0], rsem.at[9])
    arrived(final2.at[0, 1], rsem.at[8])
    arrived(final2.at[0, 0], rsem.at[10])
    res2[0] = plus(res1.at[0, me2], final2.at[0, 0], final2.at[1, 0])
    arrived(final2.at[1, 1], rsem.at[11])
    res2[1] = plus(res1.at[1, me2], final2.at[0, 1], final2.at[1, 1])

    go(res2.at[1 - s.zhi], zbuf.at[0], 12, across)
    arrived(zbuf.at[0], rsem.at[12])
    zbuf[2] = plus(res2.at[s.zhi], zbuf.at[0])
    go(zbuf.at[2], zbuf.at[1], 13, beside)
    arrived(zbuf.at[1], rsem.at[13])
    mine = fin.at[core, s.y]
    mine[...] = plus(zbuf.at[1], zbuf.at[2])

    yd, yu, yo = (s.y + 3) % 4, (s.y + 1) % 4, (s.y + 2) % 4
    go(mine, mine, 14, y_r)
    go(mine, mine, 15, y_l)

    def chip(ref, k):
        c = remote(ref, ref, ssem.at[k], csem.at[k - 18], partner)
        c.start()
        pending.append(c)

    chip(mine, 18)
    a, b = pl.ds(0, CUT), pl.ds(CUT, mine.shape[1] - CUT)
    arrived(fin.at[core, yd], rsem.at[14])
    go(fin.at[core, yd, :, a], fin.at[core, yd, :, a], 16, y_r)
    chip(fin.at[core, yd], 19)
    arrived(fin.at[core, yu], rsem.at[15])
    go(fin.at[core, yu, :, b], fin.at[core, yu, :, b], 17, y_l)
    chip(fin.at[core, yu], 20)
    arrived(fin.at[core, yo, :, a], rsem.at[16])
    arrived(fin.at[core, yo, :, b], rsem.at[17])
    chip(fin.at[core, yo], 21)
    for k, y in enumerate((s.y, yd, yu, yo)):
        arrived(fin.at[1 - core, y], csem.at[k])
    for c in pending:
        c.wait_send()
    for i in (bands - 2, bands - 1):
        bands_out(i).wait()
    for ref, i in ((ok_ref, 0), (ov_ref, 1)):
        for y in range(3):
            ref[pl.ds(PIECE * y, PIECE)] = fin[i, y].astype(F32) * scale
        ref[pl.ds(216, 64)] = fin[i, 3].astype(F32)[8:] * scale


def finish(part, kv, tok, tok2, w, scale, tok_img):
    _, count, width = kv.shape
    depth = tok.shape[0]
    rows = depth // 8
    vm = pl.BlockSpec(memory_space=pltpu.VMEM)
    hbm = pl.BlockSpec(memory_space=pl.ANY)
    p = (PIECE, width)
    return pl.pallas_call(
        lambda *r: finish_kernel(scale, tok_img, *r),
        name="finish",
        out_shape=(jax.ShapeDtypeStruct((rows, width), F32),) * 2
        + (jax.ShapeDtypeStruct((depth, count), BF),),
        in_specs=[vm] + [hbm] * 4,
        out_specs=(vm, vm, hbm),
        scratch_shapes=[
            pltpu.VMEM((8, rows, 2 * count), BF),
            pltpu.VMEM((2 * count, width), BF),
            pltpu.VMEM((2, count, width), BF),
            pltpu.VMEM((2, count, width), BF),
            pltpu.VMEM(part.shape, F32),
            pltpu.VMEM((16, SHARE, 8, LANE), F32),
            pltpu.VMEM((2, 4, 4) + p, BF),
            pltpu.VMEM((2, 4) + p, BF),
            pltpu.VMEM((2, 2, 4) + p, BF),
            pltpu.VMEM((2, 4) + p, BF),
            pltpu.VMEM((2, 4) + p, BF),
            pltpu.VMEM((2,) + p, BF),
            pltpu.VMEM((2, 2) + p, BF),
            pltpu.VMEM((2,) + p, BF),
            pltpu.VMEM((3,) + p, BF),
            pltpu.VMEM((2, 4) + p, BF),
            pltpu.VMEM((2, 2, BAND, width), BF),
            pltpu.VMEM((2, BAND, count), BF),
            DMA((24,)), DMA((20,)), DMA((3,)), DMA((4,)), DMA((5,)), DMA((5,)), DMA((4, 16)),
        ],
        compiler_params=params(5),
    )(part, kv, tok.reshape(8, rows, count), tok2.reshape(8, rows, count), w)


def body(tokens, queries, w_key, w_value, cotangent):
    tok = jnp.transpose(tokens[0])
    depth, count = tok.shape
    width = w_key.shape[1]
    tok_img = count * lax.axis_size("sp")
    images = lax.axis_size("img")
    w, tok2, kv, state = gather(w_key, w_value, tok)
    att, dq, part = attend(jnp.transpose(queries[0]), jnp.transpose(cotangent[0]), state)
    scale = float((images * tok_img) ** -0.5)
    dwk, dwv, dt = finish(part, kv, tok, tok2, w, scale, float(tok_img))
    return jnp.transpose(att)[None], jnp.transpose(dt)[None], jnp.transpose(dq)[None], dwk, dwv


def solution(mesh):
    rows, flat = P("img", "sp", None), P("img", None)
    return jax.shard_map(
        body,
        mesh=mesh,
        in_specs=(rows, rows, flat, flat, rows),
        out_specs=(rows, rows, rows, flat, flat),
        check_vma=False,
    )
```

```python
import jax
import jax.numpy as jnp
from jax import lax
from jax.experimental import pallas as pl
from jax.experimental.pallas import tpu as pltpu
from jax.sharding import PartitionSpec as P

HD = 32
EPS_DEN = 1e-06
BF = jnp.bfloat16
F32 = jnp.float32
MESH = pl.DeviceIdType.MESH
LANE = 128
ROWS = 256
VMEM_MAX = 64 * 1024 * 1024 - 65536
DMA = pltpu.SemaphoreType.DMA


def params(cid=None, sem=None):
    return pltpu.CompilerParams(
        collective_id=cid,
        has_side_effects=cid is not None,
        vmem_limit_bytes=VMEM_MAX,
        dimension_semantics=sem,
    )


class Seat:
    def __init__(self):
        img, sp = lax.axis_index("img"), lax.axis_index("sp")
        self.img, self.sp = img, sp
        self.zhi, self.x = img // 4, img % 4
        self.y, self.zlo, self.core = sp // 4, (sp // 2) % 2, sp % 2

    def at(self, dx=0, dy=0, hi=None, lo=None, core=None):
        x = (self.x + dx + 4) % 4
        y = (self.y + dy + 4) % 4
        hi = self.zhi if hi is None else hi
        lo = self.zlo if lo is None else lo
        core = self.core if core is None else core
        return {"img": hi * 4 + x, "sp": (y * 2 + lo) * 2 + core}

    def across(self):
        return self.at(hi=1 - self.zhi, lo=1 - self.zlo)

    def beside(self):
        return self.at(lo=1 - self.zlo)

    def partner(self):
        return self.at(core=1 - self.core)


def meet(devices):
    bar = pltpu.get_barrier_semaphore()
    for d in devices:
        pl.semaphore_signal(bar, inc=1, device_id=d, device_id_type=MESH)
    pl.semaphore_wait(bar, len(devices))


def remote(src, dst, ssem, rsem, device):
    return pltpu.make_async_remote_copy(
        src_ref=src, dst_ref=dst, send_sem=ssem, recv_sem=rsem, device_id=device, device_id_type=MESH
    )


HALVES = ((0, 144), (144, 136))
L0, L1, R0, R1, O0, O1, YL0, YR0, YO0, YL1, YR1, YO1, ZM0, ZM1, ZN0, ZN1 = range(16)


PHASES = ((0, 640), (640, 480))
READY = 5


def gather_kernel(wk_ref, wv_ref, tok_ref, out, tok_out, kv_out, state_out, w_ref, tin, tup, wt, wlast,
                  kvb, part, sums, slots, ssem, rsem, csem, lsem, tsem, usem, wsem, sems):
    s = Seat()
    m = s.y % 2
    width = wk_ref.shape[1]
    rows = wk_ref.shape[0]
    right, left = s.at(dx=1), s.at(dx=-1)
    up, down = s.at(dy=1), s.at(dy=-1)
    partner, across = s.partner(), s.across()
    loads = [
        pltpu.make_async_copy(r, w_ref.at[i], lsem.at[2 + i]) for i, r in enumerate((wk_ref, wv_ref))
    ]
    read = pltpu.make_async_copy(tok_ref, tin, usem.at[0])
    for c in loads:
        c.start()
    read.start()
    meet([right, left, across] + peers_of(s)[1][1:])
    for c in loads:
        c.wait()

    def spot(mat, shard, h, p):
        row = pl.multiple_of(shard * rows + HALVES[h][0], 8)
        return out.at[mat, pl.ds(row, HALVES[h][1]), pl.ds(*PHASES[p])]

    def mine(mat, h, p):
        return w_ref.at[mat, pl.ds(*HALVES[h]), pl.ds(*PHASES[p])]

    def place(k, core, p):
        hi = (s.zhi + core) % 2
        if k >= ZM0:
            return spot(m if k < ZN0 else 1 - m, (1 - s.zhi) * 4 + s.x, (k - ZM0) % 2, p)
        dx, h = {
            L0: (3, 0), L1: (3, 1), R0: (1, 0), R1: (1, 1), O0: (2, 0), O1: (2, 1),
            YL0: (3, 0), YR0: (1, 0), YO0: (2, 0), YL1: (3, 1), YR1: (1, 1), YO1: (2, 1),
        }[k]
        return spot(m if k < YL0 else 1 - m, hi * 4 + (s.x + dx) % 4, h, p)

    is0, is1 = s.core == 0, s.core == 1
    hi = (s.zhi + s.core) % 2
    seed = hi * 4 + s.x
    always, second = [], []

    def new(src, dst, k, p, device, sem, only1=False):
        slot = len(always) + len(second)
        c = remote(src, dst, ssem.at[slot], sem.at[p, k], device)
        (second if only1 else always).append(c)
        return c

    zs, seeds0, seeds1, onward, chips = {}, {}, {}, {}, {}
    for p in range(2):
        for k, mat, h in ((ZM0, m, 0), (ZM1, m, 1), (ZN0, 1 - m, 0), (ZN1, 1 - m, 1)):
            zs[k, p] = new(mine(mat, h, p), spot(mat, s.img, h, p), k, p, across, rsem, True)
        for i, (h, k, d) in enumerate(((0, L0, right), (1, R1, left), (1, L1, right), (0, R0, left))):
            slot = ssem.at[len(always) + len(second)]
            there = spot(m, seed, h, p)
            seeds1[i, p] = remote(there, there, slot, rsem.at[p, k], d)
            seeds0[i, p] = new(mine(m, h, p), spot(m, s.img, h, p), k, p, d, rsem)
        for k, to, d in (
            (L0, O0, right), (R1, O1, left),
            (L0, YL0, up), (R0, YR0, up), (O0, YO0, up),
            (L1, YL1, down), (R1, YR1, down), (O1, YO1, down),
        ):
            ref = place(k, s.core, p)
            onward.setdefault((k, p), []).append(new(ref, ref, to, p, d, rsem))
        for k in range(16):
            ref = place(k, s.core, p)
            chips[k, p] = new(ref, ref, k, p, partner, csem, k >= ZM0)

    def got(k, p, sem, core):
        ref = place(k, core, p)
        pltpu.make_async_copy(ref, ref, sem.at[p, k]).wait()

    def arrive(p, *ks):
        for k in ks:
            got(k, p, rsem, s.core)
            for c in onward.get((k, p), ()):
                c.start()
            chips[k, p].start()

    def across_in(p, *ks):
        @pl.when(is1)
        def _():
            for k in ks:
                arrive(p, k)
                if k in (ZM0, ZM1):
                    h = k - ZM0
                    for i in ((0, 3), (1, 2))[h]:
                        seeds1[i, p].start()

    def seed0(p, *which):
        @pl.when(is0)
        def _():
            for i in which:
                seeds0[i, p].start()

    def settled(p):
        for k in range(ZM0):
            got(k, p, csem, 1 - s.core)

        @pl.when(is0)
        def _():
            for k in range(ZM0, 16):
                got(k, p, csem, 1)

    @pl.when(is1)
    def _():
        for k, p in (
            (ZM0, 0), (ZM1, 0), (ZM0, 1), (ZM1, 1), (ZN0, 0), (ZN1, 0), (ZN0, 1), (ZN1, 1)
        ):
            zs[k, p].start()

    seed0(0, 0, 1, 2, 3)
    swap = remote(tok_ref, tok_out, tsem.at[0], tsem.at[1], partner)
    owns = [
        pltpu.make_async_copy(
            w_ref.at[i],
            out.at[i, pl.ds(pl.multiple_of(s.img * rows, 8), rows)],
            lsem.at[i],
        )
        for i in range(2)
    ]
    for c in owns:
        c.start()
    read.wait()
    depth = tok_ref.shape[0]
    whole = depth // ROWS
    rest = depth - whole * ROWS

    def flip(i, _):
        at = pl.ds(pl.multiple_of(i * ROWS, ROWS), ROWS)
        tup[:, at] = jnp.transpose(tin[at])
        return 0

    lax.fori_loop(0, 2, flip, 0)
    across_in(0, ZM0, ZM1)
    lax.fori_loop(2, 3, flip, 0)
    arrive(0, L0, R1)
    seed0(1, 0, 1)
    lax.fori_loop(3, 4, flip, 0)
    arrive(0, L1, R0)
    seed0(1, 2, 3)
    across_in(1, ZM0, ZM1)
    lax.fori_loop(4, 5, flip, 0)
    arrive(0, YL0, YR1)
    across_in(0, ZN0, ZN1)
    lax.fori_loop(5, 6, flip, 0)
    arrive(0, O0, O1)
    swap.start()
    arrive(1, L0, R1)
    lax.fori_loop(6, whole, flip, 0)
    arrive(0, YR0, YL1)
    arrive(1, L1, R0)
    at = pl.ds(whole * ROWS, rest)
    tup[:, at] = jnp.transpose(tin[at])
    arrive(0, YO0, YO1)
    settled(0)
    for c in owns:
        c.wait()

    def tile_load(i):
        at = pl.ds(pl.multiple_of(i * LANE, LANE), LANE)
        slot = i % 2
        return [
            pltpu.make_async_copy(
                out.at[j, :, at], wt.at[slot, :, pl.ds(j * LANE, LANE)], wsem.at[slot]
            )
            for j in range(2)
        ]

    full = width // LANE
    tail = width - full * LANE
    last = pltpu.make_async_copy(out.at[:, :, pl.ds(full * LANE, tail)], wlast, usem.at[1])
    mask = same_head()
    part[45:48] = jnp.zeros((3, 8, LANE), F32)
    for c in tile_load(0):
        c.start()

    def keep(i, key, val, at):
        kvb[0, :, at] = key
        kvb[1, :, at] = val
        n = key.shape[1]
        state = dot_t(key, val)
        row = jnp.sum(key.astype(F32), axis=0, keepdims=True)
        if n < LANE:
            state = jnp.where(mask[:n, :n], state, 0.0)
            state = state[0:32] + state[32:64] + state[64:96]
            state = jnp.concatenate([state, jnp.zeros((32, LANE - n), F32)], axis=1)
            row = jnp.concatenate([row, jnp.zeros((1, LANE - n), F32)], axis=1)
        else:
            state = fold(state, mask)
        put_state(part.at[pl.ds(5 * i, 5)], state, row)

    def tile(i, _):
        @pl.when(i == 0)
        def _():
            arrive(1, O0, O1, YL0, YR1)

        @pl.when(i == 1)
        def _():
            across_in(1, ZN0, ZN1)
            arrive(1, YR0, YL1)

        @pl.when(i == 2)
        def _():
            arrive(1, YO0, YO1)

        @pl.when(i == READY)
        def _():
            settled(1)
            for c in tile_load(READY):
                c.start()
            last.start()

        slot = i % 2
        pltpu.make_async_copy(wt.at[slot], wt.at[slot], wsem.at[slot]).wait()

        @pl.when(jnp.logical_and(i + 1 < full, i + 1 != READY))
        def _():
            for c in tile_load(i + 1):
                c.start()

        acc = dot(tup[...], wt[slot])
        key = jnp.maximum(acc[:, :LANE], 0.0).astype(BF)
        keep(i, key, acc[:, LANE:].astype(BF), pl.ds(pl.multiple_of(i * LANE, LANE), LANE))
        return 0

    lax.fori_loop(0, full, tile, 0)
    last.wait()
    pad = jnp.zeros((depth, LANE - tail), BF)
    acc = dot(tup[...], jnp.concatenate([wlast[0], pad, wlast[1]], axis=1))
    key = jnp.maximum(acc[:, :tail], 0.0).astype(BF)
    keep(full, key, acc[:, LANE : LANE + tail].astype(BF), pl.ds(full * LANE, tail))
    kv_write = pltpu.make_async_copy(kvb, kv_out, usem.at[2])
    kv_write.start()
    total(s, part, sums, slots, sems)
    state_out[...] = sums[...]
    for c in always:
        c.wait_send()

    @pl.when(is1)
    def _():
        for c in second:
            c.wait_send()

    swap.wait()
    kv_write.wait()


def gather(wk, wv, tok):
    rows, cols = wk.shape
    depth, count = tok.shape
    hbm = pl.BlockSpec(memory_space=pl.ANY)
    vm = pl.BlockSpec(memory_space=pltpu.VMEM)
    tiles = (48, 8, LANE)
    return pl.pallas_call(
        gather_kernel,
        name="gather",
        out_shape=(
            jax.ShapeDtypeStruct((2, depth, cols), BF),
            jax.ShapeDtypeStruct(tok.shape, BF),
            jax.ShapeDtypeStruct((2, count, cols), BF),
            jax.ShapeDtypeStruct(tiles, F32),
        ),
        in_specs=[hbm] * 3,
        out_specs=(hbm, hbm, hbm, vm),
        scratch_shapes=[
            pltpu.VMEM((2, rows, cols), BF),
            pltpu.VMEM(tok.shape, BF),
            pltpu.VMEM(tok.shape[::-1], BF),
            pltpu.VMEM((2, depth, 2 * LANE), BF),
            pltpu.VMEM((2, depth, cols % LANE), BF),
            pltpu.VMEM((2, count, cols), BF),
            pltpu.VMEM(tiles, F32),
            pltpu.VMEM(tiles, F32),
            pltpu.VMEM((16, SHARE, 8, LANE), F32),
            DMA((64,)), DMA((2, 16)), DMA((2, 16)), DMA((4,)), DMA((2,)), DMA((3,)), DMA((2,)),
            DMA((4, 16)),
        ],
        compiler_params=params(1),
    )(wk, wv, tok)


def split(a):
    hi = a.astype(BF)
    return hi, (a - hi.astype(F32)).astype(BF)


def same_head():
    r = lax.broadcasted_iota(jnp.int32, (LANE, LANE), 0) // HD
    c = lax.broadcasted_iota(jnp.int32, (LANE, LANE), 1) // HD
    return r == c


def fold(block, mask):
    b = jnp.where(mask, block, 0.0)
    return b[0:32] + b[32:64] + b[64:96] + b[96:128]


def unfold(state, mask):
    return jnp.where(mask, jnp.concatenate([state] * 4, axis=0), 0.0)


def put_state(ref, state, row):
    ref[0:4] = state.reshape(4, 8, LANE)
    ref[4] = jnp.broadcast_to(row, (8, LANE))


def dot(a, b):
    return lax.dot_general(a, b, (((1,), (0,)), ((), ())), preferred_element_type=F32)


def dot_t(a, b):
    return lax.dot_general(a, b, (((0,), (0,)), ((), ())), preferred_element_type=F32)


SHARE = 3


def peers_of(s):
    places = [(s.sp + k) % 16 for k in range(16)]
    return places, [{"img": s.img, "sp": p} for p in places]


def share(ref, place):
    return ref.at[pl.ds(place * SHARE, SHARE)]


def total(s, part, sums, slots, sems):
    places, devs = peers_of(s)
    me = s.sp
    out, back = [], []
    for k in range(1, 16):
        c = remote(share(part, places[k]), slots.at[k], sems.at[0, k], sems.at[1, k], devs[k])
        c.start()
        out.append(c)
    acc = share(part, me)[...]
    for k in range(1, 16):
        out[k - 1].wait_recv()
        acc = acc + slots[k]
    mine = share(sums, me)
    mine[...] = acc
    for k in range(1, 16):
        c = remote(mine, mine, sems.at[2, k], sems.at[3, k], devs[k])
        c.start()
        back.append(c)
    for k in range(1, 16):
        ref = share(sums, (me + 16 - k) % 16)
        pltpu.make_async_copy(ref, ref, sems.at[3, k]).wait()
    for c in out + back:
        c.wait_send()


def dot_r(a, b):
    return lax.dot_general(a, b, (((1,), (1,)), ((), ())), preferred_element_type=F32)


def attend_kernel(width, q_ref, g_ref, st_ref, att_ref, dq_ref, part_ref):
    mask = same_head()
    state = st_ref[0:4].reshape(32, LANE)
    row = jnp.broadcast_to(st_ref[4][0:1], (LANE, LANE))
    col = jnp.transpose(row)[:, 0:1]
    kv = unfold(state, mask)
    kvh, kvl = split(kv)
    kvth, kvtl = split(jnp.transpose(kv))
    nh, nl = split(jnp.where(mask, row, 0.0))
    line = lax.broadcasted_iota(jnp.int32, q_ref.shape, 0) + pl.program_id(0) * LANE
    ok = line < width
    zero = jnp.zeros((), BF)
    q = jnp.where(ok, jnp.maximum(q_ref[...], zero), zero)
    g = jnp.where(ok, g_ref[...], zero).astype(F32)
    fwd = jnp.concatenate(
        [jnp.concatenate([kvth, kvtl], axis=1), jnp.concatenate([nh, nl], axis=1)], axis=0
    )
    both = dot(fwd, jnp.concatenate([q, q], axis=0))
    inv = 1.0 / (both[LANE:] + EPS_DEN)
    attn = both[:LANE] * inv
    att_ref[...] = attn.astype(BF)
    d_num = g * inv
    ones = jnp.where(mask, 1.0, 0.0).astype(BF)
    dots = dot(
        jnp.concatenate([ones, ones], axis=1), jnp.concatenate(split(g * attn), axis=0)
    )
    d_den = -dots * inv
    dnh, dnl = split(d_num)
    pair = jnp.concatenate([dnh, dnl], axis=0)
    back = jnp.concatenate(
        [
            jnp.concatenate([kvh, kvh], axis=1),
            jnp.concatenate([kvl, jnp.zeros_like(kvl)], axis=1),
        ],
        axis=0,
    )
    feat = dot(back, pair)
    feat = feat[:LANE] + feat[LANE:] + d_den * col
    dq_ref[...] = jnp.where(q > 0, feat, 0.0).astype(BF)
    gs = dot_r(q, pair)
    gn = jnp.sum(d_den * q.astype(F32), axis=1, keepdims=True)
    put_state(
        part_ref,
        fold(gs[:, :LANE] + gs[:, LANE:], mask),
        jnp.transpose(jnp.broadcast_to(gn, (LANE, LANE)))[0:1],
    )


def attend(q, g, state):
    width, count = q.shape
    lines = pl.BlockSpec((LANE, count), lambda i: (i, 0))
    tiles = pl.BlockSpec((5, 8, LANE), lambda i: (i, 0, 0))
    return pl.pallas_call(
        lambda *r: attend_kernel(width, *r),
        name="attend",
        grid=(pl.cdiv(width, LANE),),
        out_shape=(
            jax.ShapeDtypeStruct((width, count), BF),
            jax.ShapeDtypeStruct((width, count), BF),
            jax.ShapeDtypeStruct((48, 8, LANE), F32),
        ),
        in_specs=[lines, lines, tiles],
        out_specs=(lines, lines, tiles),
        compiler_params=params(),
    )(q, g, state)


PIECE = 72
OFFS = (0, 72, 144, 208)
CUT = 640
SPLIT = 512
BAND = 448


def finish_kernel(scale, tok_img, part_ref, kv_ref, tok_ref, tok2_ref, w_ref, ok_ref, ov_ref, dt_ref,
                  cat, dcat, dboth, kvb, sums, slots, gp, relay, final, comb, res1, relay2, final2,
                  res2, zbuf, fin, wbuf, tbuf, ssem, rsem, lsem, csem, wsem, osem, tsem, psem):
    s = Seat()
    core = s.core
    x_r, x_l, y_r, y_l = s.at(dx=1), s.at(dx=-1), s.at(dy=1), s.at(dy=-1)
    right1, left1 = s.at(dx=1 - core, dy=core), s.at(dx=core - 1, dy=-core)
    right2, left2 = s.at(dx=core, dy=1 - core), s.at(dx=-core, dy=core - 1)
    me1 = s.x * (1 - core) + s.y * core
    me2 = s.y * (1 - core) + s.x * core
    across, beside, partner = s.across(), s.beside(), s.partner()
    count, width = kv_ref.shape[1:]

    def loader(src, dst, i):
        return pltpu.make_async_copy(src, dst, lsem.at[i])

    lo, up = pl.ds(0, count), pl.ds(count, count)
    ld = [
        loader(kv_ref, kvb, 0),
        loader(tok_ref, cat.at[:, :, lo], 1),
        loader(tok2_ref, cat.at[:, :, up], 2),
    ]
    for c in ld:
        c.start()
    bands = w_ref.shape[1] // BAND

    def band_load(i):
        at = pl.ds(i * BAND, BAND)
        return pltpu.make_async_copy(w_ref.at[:, at], wbuf.at[i % 2], wsem.at[i])

    band_load(0).start()
    band_load(1).start()
    meet([x_r, x_l, across] + peers_of(s)[1][1:])
    total(s, part_ref, sums, slots, tsem)
    ld[0].wait()
    mask = same_head()

    def swap(i):
        at = pl.ds((0, SPLIT)[i], (SPLIT, width - SPLIT)[i])
        return remote(
            dboth.at[1 - core, :, at], dcat.at[up, at], ssem.at[22 + i], rsem.at[18 + i], partner
        )

    def features(g, at, n):
        gs = unfold(sums[pl.ds(5 * g, 4)].reshape(32, LANE) * tok_img, mask)[:n, :n]
        row = sums[5 * g + 4][0:1, :n] * tok_img
        gh, gl = split(gs)
        th, tl = split(jnp.transpose(gs))
        key, val = kvb[0, :, at], kvb[1, :, at]

        def twice(a, h, l):
            if n < LANE:
                return dot(a, h) + dot(a, l)
            return dot(jnp.concatenate([a, a], axis=1), jnp.concatenate([h, l], axis=0))

        dk = jnp.where(key > 0, twice(val, th, tl) + row, 0.0).astype(BF)
        dv = twice(key, gh, gl).astype(BF)
        dboth[0, :, at] = dk
        dboth[1, :, at] = dv
        dcat[lo, at] = jnp.where(core == 0, dk.astype(F32), dv.astype(F32)).astype(BF)

    def tile(g, _):
        features(g, pl.ds(pl.multiple_of(g * LANE, LANE), LANE), LANE)
        return 0

    lax.fori_loop(0, SPLIT // LANE, tile, 0)
    swap(0).start()
    lax.fori_loop(SPLIT // LANE, width // LANE, tile, 0)
    tail = width - width // LANE * LANE
    features(width // LANE, pl.ds(width - tail, tail), tail)
    swap(1).start()

    pending = []

    def copy(src, dst, i, device):
        return remote(src, dst, ssem.at[i], rsem.at[i], device)

    def go(src, dst, i, device):
        c = copy(src, dst, i, device)
        c.start()
        pending.append(c)

    def arrived(ref, sem):
        pltpu.make_async_copy(ref, ref, sem).wait()

    def nxt(v, k):
        return (v + k) % 4

    def bands_out(i):
        at = pl.ds(i * BAND, BAND)
        return pltpu.make_async_copy(tbuf.at[i % 2], dt_ref.at[at], osem.at[i])

    def band(i):
        band_load(i).wait()
        if i >= 2:
            bands_out(i - 2).wait()
        both = wbuf.at[i % 2]
        v = dot_r(both[0], dboth[0]) + dot_r(both[1], dboth[1])
        tbuf[i % 2] = v.astype(BF)
        bands_out(i).start()
        if i + 2 < bands:
            band_load(i + 2).start()

    def shard(h, dx):
        xx = nxt(s.x, dx)
        v = dot(cat[h * 4 + xx], dcat[...])
        for y in range(4):
            c = xx * (1 - core) + y * core
            j = y * (1 - core) + xx * core
            gp[h, c, j] = v[OFFS[y] : OFFS[y] + PIECE].astype(BF)

        @pl.when(core == 1)
        def _():
            j = xx
            d = (right1, left1)
            remote(
                gp.at[h, nxt(me1, 2), j], relay.at[h, j], psem.at[0, h, dx], psem.at[1, h, dx], d[h]
            ).start()
            if h == 1:
                copy(gp.at[1, nxt(me1, 1), j], final.at[0, 1, j], 2, right1).start()
            else:
                copy(gp.at[0, nxt(me1, 3), j], final.at[1, 0, j], 3, left1).start()

        act = {
            (0, 2): (relay.at[0], 0, right1),
            (1, 2): (relay.at[1], 1, left1),
            (1, 1): (final.at[0, 1], 2, right1),
            (0, 3): (final.at[1, 0], 3, left1),
        }.get((h, dx))
        if act is not None:
            dst, i, dev = act

            @pl.when(core == 0)
            def _():
                copy(gp.at[h, nxt(me1, dx)], dst, i, dev).start()

    def add(dst, *srcs):
        def body(j, _):
            v = srcs[0][j].astype(F32)
            for r in srcs[1:]:
                v = v + r[j].astype(F32)
            dst[j] = v.astype(BF)
            return 0

        lax.fori_loop(0, 4, body, 0)

    def combine():
        arrived(relay.at[0], rsem.at[0])
        add(comb.at[0], gp.at[0, nxt(me1, 1)], relay.at[0])
        copy(comb.at[0], final.at[0, 0], 4, right1).start()
        arrived(relay.at[1], rsem.at[1])
        add(comb.at[1], gp.at[1, nxt(me1, 3)], relay.at[1])
        copy(comb.at[1], final.at[1, 1], 5, left1).start()

    def combine_piece(h, dx):
        j = nxt(s.x, dx)
        arrived(relay.at[h, j], psem.at[1, h, dx])
        mine = gp[h, nxt(me1, (1, 3)[h]), j].astype(F32)
        comb[h, j] = (mine + relay[h, j].astype(F32)).astype(BF)
        dst = (final.at[0, 0, j], final.at[1, 1, j])[h]
        copy(comb.at[h, j], dst, 4 + h, (right1, left1)[h]).start()

    for c in ld[1:]:
        c.wait()
    swap(0).wait()
    swap(1).wait()
    for h, dx in ((0, 2), (1, 2), (1, 1), (0, 3), (0, 1), (1, 3)):
        shard(h, dx)

    @pl.when(core == 0)
    def _():
        combine()

    @pl.when(core == 1)
    def _():
        for h, dx in ((0, 2), (1, 2), (1, 1), (0, 3)):
            combine_piece(h, dx)

    shard(0, 0)

    @pl.when(core == 1)
    def _():
        for h, dx in ((0, 1), (1, 3)):
            combine_piece(h, dx)

    shard(1, 0)

    @pl.when(core == 1)
    def _():
        for h, dx in ((0, 0), (1, 0)):
            combine_piece(h, dx)

    for i, dst in (
        (2, final.at[0, 1]), (3, final.at[1, 0]), (4, final.at[0, 0]), (5, final.at[1, 1])
    ):
        pending.append(copy(dst, dst, i, right1))

    band(0)
    band(1)
    band(2)
    arrived(final.at[1, 0], rsem.at[3])
    arrived(final.at[0, 1], rsem.at[2])
    arrived(final.at[0, 0], rsem.at[4])
    add(res1.at[0], gp.at[0, me1], final.at[0, 0], final.at[1, 0])

    go(res1.at[0, nxt(me2, 2)], relay2.at[0], 6, right2)
    arrived(final.at[1, 1], rsem.at[5])
    add(res1.at[1], gp.at[1, me1], final.at[0, 1], final.at[1, 1])
    go(res1.at[1, nxt(me2, 2)], relay2.at[1], 7, left2)
    go(res1.at[1, nxt(me2, 1)], final2.at[0, 1], 8, right2)
    go(res1.at[0, nxt(me2, 3)], final2.at[1, 0], 9, left2)
    band(3)

    def plus(*refs):
        v = refs[0][...].astype(F32)
        for r in refs[1:]:
            v = v + r[...].astype(F32)
        return v.astype(BF)

    arrived(relay2.at[0], rsem.at[6])
    relay2[0] = plus(relay2.at[0], res1.at[0, nxt(me2, 1)])
    go(relay2.at[0], final2.at[0, 0], 10, right2)
    arrived(relay2.at[1], rsem.at[7])
    relay2[1] = plus(relay2.at[1], res1.at[1, nxt(me2, 3)])
    go(relay2.at[1], final2.at[1, 1], 11, left2)
    band(4)
    arrived(final2.at[1, 0], rsem.at[9])
    arrived(final2.at[0, 1], rsem.at[8])
    arrived(final2.at[0, 0], rsem.at[10])
    res2[0] = plus(res1.at[0, me2], final2.at[0, 0], final2.at[1, 0])
    arrived(final2.at[1, 1], rsem.at[11])
    res2[1] = plus(res1.at[1, me2], final2.at[0, 1], final2.at[1, 1])

    go(res2.at[1 - s.zhi], zbuf.at[0], 12, across)
    arrived(zbuf.at[0], rsem.at[12])
    zbuf[2] = plus(res2.at[s.zhi], zbuf.at[0])
    go(zbuf.at[2], zbuf.at[1], 13, beside)
    arrived(zbuf.at[1], rsem.at[13])
    mine = fin.at[core, s.y]
    mine[...] = plus(zbuf.at[1], zbuf.at[2])

    yd, yu, yo = (s.y + 3) % 4, (s.y + 1) % 4, (s.y + 2) % 4
    go(mine, mine, 14, y_r)
    go(mine, mine, 15, y_l)

    def chip(ref, k):
        c = remote(ref, ref, ssem.at[k], csem.at[k - 18], partner)
        c.start()
        pending.append(c)

    chip(mine, 18)
    a, b = pl.ds(0, CUT), pl.ds(CUT, mine.shape[1] - CUT)
    arrived(fin.at[core, yd], rsem.at[14])
    go(fin.at[core, yd, :, a], fin.at[core, yd, :, a], 16, y_r)
    chip(fin.at[core, yd], 19)
    arrived(fin.at[core, yu], rsem.at[15])
    go(fin.at[core, yu, :, b], fin.at[core, yu, :, b], 17, y_l)
    chip(fin.at[core, yu], 20)
    arrived(fin.at[core, yo, :, a], rsem.at[16])
    arrived(fin.at[core, yo, :, b], rsem.at[17])
    chip(fin.at[core, yo], 21)
    for k, y in enumerate((s.y, yd, yu, yo)):
        arrived(fin.at[1 - core, y], csem.at[k])
    for c in pending:
        c.wait_send()

    @pl.when(core == 0)
    def _():
        for h in range(2):
            copy(relay.at[h], relay.at[h], h, right1).wait_send()

    @pl.when(core == 1)
    def _():
        for h in range(2):
            for dx in range(4):
                ref = relay.at[h, nxt(s.x, dx)]
                remote(ref, ref, psem.at[0, h, dx], psem.at[1, h, dx], right1).wait_send()

    for i in (bands - 2, bands - 1):
        bands_out(i).wait()
    for ref, i in ((ok_ref, 0), (ov_ref, 1)):
        for y in range(3):
            ref[pl.ds(PIECE * y, PIECE)] = fin[i, y].astype(F32) * scale
        ref[pl.ds(216, 64)] = fin[i, 3].astype(F32)[8:] * scale


def finish(part, kv, tok, tok2, w, scale, tok_img):
    _, count, width = kv.shape
    depth = tok.shape[0]
    rows = depth // 8
    vm = pl.BlockSpec(memory_space=pltpu.VMEM)
    hbm = pl.BlockSpec(memory_space=pl.ANY)
    p = (PIECE, width)
    return pl.pallas_call(
        lambda *r: finish_kernel(scale, tok_img, *r),
        name="finish",
        out_shape=(jax.ShapeDtypeStruct((rows, width), F32),) * 2
        + (jax.ShapeDtypeStruct((depth, count), BF),),
        in_specs=[vm] + [hbm] * 4,
        out_specs=(vm, vm, hbm),
        scratch_shapes=[
            pltpu.VMEM((8, rows, 2 * count), BF),
            pltpu.VMEM((2 * count, width), BF),
            pltpu.VMEM((2, count, width), BF),
            pltpu.VMEM((2, count, width), BF),
            pltpu.VMEM(part.shape, F32),
            pltpu.VMEM((16, SHARE, 8, LANE), F32),
            pltpu.VMEM((2, 4, 4) + p, BF),
            pltpu.VMEM((2, 4) + p, BF),
            pltpu.VMEM((2, 2, 4) + p, BF),
            pltpu.VMEM((2, 4) + p, BF),
            pltpu.VMEM((2, 4) + p, BF),
            pltpu.VMEM((2,) + p, BF),
            pltpu.VMEM((2, 2) + p, BF),
            pltpu.VMEM((2,) + p, BF),
            pltpu.VMEM((3,) + p, BF),
            pltpu.VMEM((2, 4) + p, BF),
            pltpu.VMEM((2, 2, BAND, width), BF),
            pltpu.VMEM((2, BAND, count), BF),
            DMA((24,)), DMA((20,)), DMA((3,)), DMA((4,)), DMA((5,)), DMA((5,)), DMA((4, 16)),
            DMA((2, 2, 4)),
        ],
        compiler_params=params(5),
    )(part, kv, tok.reshape(8, rows, count), tok2.reshape(8, rows, count), w)


def body(tokens, queries, w_key, w_value, cotangent):
    tok = jnp.transpose(tokens[0])
    depth, count = tok.shape
    width = w_key.shape[1]
    tok_img = count * lax.axis_size("sp")
    images = lax.axis_size("img")
    w, tok2, kv, state = gather(w_key, w_value, tok)
    att, dq, part = attend(jnp.transpose(queries[0]), jnp.transpose(cotangent[0]), state)
    scale = float((images * tok_img) ** -0.5)
    dwk, dwv, dt = finish(part, kv, tok, tok2, w, scale, float(tok_img))
    return jnp.transpose(att)[None], jnp.transpose(dt)[None], jnp.transpose(dq)[None], dwk, dwv


def solution(mesh):
    rows, flat = P("img", "sp", None), P("img", None)
    return jax.shard_map(
        body,
        mesh=mesh,
        in_specs=(rows, rows, flat, flat, rows),
        out_specs=(rows, rows, rows, flat, flat),
        check_vma=False,
    )
```

```python
import jax
import jax.numpy as jnp
from jax import lax
from jax.experimental import pallas as pl
from jax.experimental.pallas import tpu as pltpu
from jax.sharding import PartitionSpec as P

HD = 32
EPS_DEN = 1e-06
BF = jnp.bfloat16
F32 = jnp.float32
MESH = pl.DeviceIdType.MESH
LANE = 128
ROWS = 256
VMEM_MAX = 64 * 1024 * 1024 - 65536
DMA = pltpu.SemaphoreType.DMA


def params(cid=None, sem=None, grant=VMEM_MAX):
    return pltpu.CompilerParams(
        collective_id=cid,
        has_side_effects=cid is not None,
        vmem_limit_bytes=grant,
        dimension_semantics=sem,
    )


class Seat:
    def __init__(self):
        img, sp = lax.axis_index("img"), lax.axis_index("sp")
        self.img, self.sp = img, sp
        self.zhi, self.x = img // 4, img % 4
        self.y, self.zlo, self.core = sp // 4, (sp // 2) % 2, sp % 2

    def at(self, dx=0, dy=0, hi=None, lo=None, core=None):
        x = (self.x + dx + 4) % 4
        y = (self.y + dy + 4) % 4
        hi = self.zhi if hi is None else hi
        lo = self.zlo if lo is None else lo
        core = self.core if core is None else core
        return {"img": hi * 4 + x, "sp": (y * 2 + lo) * 2 + core}

    def across(self):
        return self.at(hi=1 - self.zhi, lo=1 - self.zlo)

    def beside(self):
        return self.at(lo=1 - self.zlo)

    def partner(self):
        return self.at(core=1 - self.core)


def meet(devices):
    bar = pltpu.get_barrier_semaphore()
    for d in devices:
        pl.semaphore_signal(bar, inc=1, device_id=d, device_id_type=MESH)
    pl.semaphore_wait(bar, len(devices))


def remote(src, dst, ssem, rsem, device):
    return pltpu.make_async_remote_copy(
        src_ref=src, dst_ref=dst, send_sem=ssem, recv_sem=rsem, device_id=device, device_id_type=MESH
    )


HALVES = ((0, 144), (144, 136))
L0, L1, R0, R1, O0, O1, YL0, YR0, YO0, YL1, YR1, YO1, ZM0, ZM1, ZN0, ZN1 = range(16)


PHASES = ((0, 640), (640, 480))
READY = 5


def gather_kernel(wk_ref, wv_ref, tok_ref, out, tok_out, kv_out, state_out, w_ref, tin, tup, wt, wlast,
                  kvb, part, sums, slots, ssem, rsem, csem, lsem, tsem, usem, wsem, sems):
    s = Seat()
    m = s.y % 2
    width = wk_ref.shape[1]
    rows = wk_ref.shape[0]
    right, left = s.at(dx=1), s.at(dx=-1)
    up, down = s.at(dy=1), s.at(dy=-1)
    partner, across = s.partner(), s.across()
    loads = [
        pltpu.make_async_copy(r, w_ref.at[i], lsem.at[2 + i]) for i, r in enumerate((wk_ref, wv_ref))
    ]
    read = pltpu.make_async_copy(tok_ref, tin, usem.at[0])
    for c in loads:
        c.start()
    read.start()
    meet([right, left, across] + peers_of(s)[1][1:])
    for c in loads:
        c.wait()

    def spot(mat, shard, h, p):
        row = pl.multiple_of(shard * rows + HALVES[h][0], 8)
        return out.at[mat, pl.ds(row, HALVES[h][1]), pl.ds(*PHASES[p])]

    def mine(mat, h, p):
        return w_ref.at[mat, pl.ds(*HALVES[h]), pl.ds(*PHASES[p])]

    def place(k, core, p):
        hi = (s.zhi + core) % 2
        if k >= ZM0:
            return spot(m if k < ZN0 else 1 - m, (1 - s.zhi) * 4 + s.x, (k - ZM0) % 2, p)
        dx, h = {
            L0: (3, 0), L1: (3, 1), R0: (1, 0), R1: (1, 1), O0: (2, 0), O1: (2, 1),
            YL0: (3, 0), YR0: (1, 0), YO0: (2, 0), YL1: (3, 1), YR1: (1, 1), YO1: (2, 1),
        }[k]
        return spot(m if k < YL0 else 1 - m, hi * 4 + (s.x + dx) % 4, h, p)

    is0, is1 = s.core == 0, s.core == 1
    hi = (s.zhi + s.core) % 2
    seed = hi * 4 + s.x
    always, second = [], []

    def new(src, dst, k, p, device, sem, only1=False):
        slot = len(always) + len(second)
        c = remote(src, dst, ssem.at[slot], sem.at[p, k], device)
        (second if only1 else always).append(c)
        return c

    zs, seeds0, seeds1, onward, chips = {}, {}, {}, {}, {}
    for p in range(2):
        for k, mat, h in ((ZM0, m, 0), (ZM1, m, 1), (ZN0, 1 - m, 0), (ZN1, 1 - m, 1)):
            zs[k, p] = new(mine(mat, h, p), spot(mat, s.img, h, p), k, p, across, rsem, True)
        for i, (h, k, d) in enumerate(((0, L0, right), (1, R1, left), (1, L1, right), (0, R0, left))):
            slot = ssem.at[len(always) + len(second)]
            there = spot(m, seed, h, p)
            seeds1[i, p] = remote(there, there, slot, rsem.at[p, k], d)
            seeds0[i, p] = new(mine(m, h, p), spot(m, s.img, h, p), k, p, d, rsem)
        for k, to, d in (
            (L0, O0, right), (R1, O1, left),
            (L0, YL0, up), (R0, YR0, up), (O0, YO0, up),
            (L1, YL1, down), (R1, YR1, down), (O1, YO1, down),
        ):
            ref = place(k, s.core, p)
            onward.setdefault((k, p), []).append(new(ref, ref, to, p, d, rsem))
        for k in range(16):
            ref = place(k, s.core, p)
            chips[k, p] = new(ref, ref, k, p, partner, csem, k >= ZM0)

    def got(k, p, sem, core):
        ref = place(k, core, p)
        pltpu.make_async_copy(ref, ref, sem.at[p, k]).wait()

    def arrive(p, *ks):
        for k in ks:
            got(k, p, rsem, s.core)
            for c in onward.get((k, p), ()):
                c.start()
            chips[k, p].start()

    def across_in(p, *ks):
        @pl.when(is1)
        def _():
            for k in ks:
                arrive(p, k)
                if k in (ZM0, ZM1):
                    h = k - ZM0
                    for i in ((0, 3), (1, 2))[h]:
                        seeds1[i, p].start()

    def seed0(p, *which):
        @pl.when(is0)
        def _():
            for i in which:
                seeds0[i, p].start()

    def settled(p):
        for k in range(ZM0):
            got(k, p, csem, 1 - s.core)

        @pl.when(is0)
        def _():
            for k in range(ZM0, 16):
                got(k, p, csem, 1)

    @pl.when(is1)
    def _():
        for k, p in (
            (ZM0, 0), (ZM1, 0), (ZM0, 1), (ZM1, 1), (ZN0, 0), (ZN1, 0), (ZN0, 1), (ZN1, 1)
        ):
            zs[k, p].start()

    seed0(0, 0, 1, 2, 3)
    swap = remote(tok_ref, tok_out, tsem.at[0], tsem.at[1], partner)
    owns = [
        pltpu.make_async_copy(
            w_ref.at[i],
            out.at[i, pl.ds(pl.multiple_of(s.img * rows, 8), rows)],
            lsem.at[i],
        )
        for i in range(2)
    ]
    for c in owns:
        c.start()
    read.wait()
    depth = tok_ref.shape[0]
    whole = depth // ROWS
    rest = depth - whole * ROWS

    def flip(i, _):
        at = pl.ds(pl.multiple_of(i * ROWS, ROWS), ROWS)
        tup[:, at] = jnp.transpose(tin[at])
        return 0

    lax.fori_loop(0, 2, flip, 0)
    across_in(0, ZM0, ZM1)
    lax.fori_loop(2, 3, flip, 0)
    arrive(0, L0, R1)
    seed0(1, 0, 1)
    lax.fori_loop(3, 4, flip, 0)
    arrive(0, L1, R0)
    seed0(1, 2, 3)
    across_in(1, ZM0, ZM1)
    lax.fori_loop(4, 5, flip, 0)
    arrive(0, YL0, YR1)
    across_in(0, ZN0, ZN1)
    lax.fori_loop(5, 6, flip, 0)
    arrive(0, O0, O1)
    swap.start()
    arrive(1, L0, R1)
    lax.fori_loop(6, whole, flip, 0)
    arrive(0, YR0, YL1)
    arrive(1, L1, R0)
    at = pl.ds(whole * ROWS, rest)
    tup[:, at] = jnp.transpose(tin[at])
    arrive(0, YO0, YO1)
    settled(0)
    for c in owns:
        c.wait()

    def tile_load(i):
        at = pl.ds(pl.multiple_of(i * LANE, LANE), LANE)
        slot = i % 2
        return [
            pltpu.make_async_copy(
                out.at[j, :, at], wt.at[slot, :, pl.ds(j * LANE, LANE)], wsem.at[slot]
            )
            for j in range(2)
        ]

    full = width // LANE
    tail = width - full * LANE
    last = pltpu.make_async_copy(out.at[:, :, pl.ds(full * LANE, tail)], wlast, usem.at[1])
    mask = same_head()
    part[45:48] = jnp.zeros((3, 8, LANE), F32)
    for c in tile_load(0):
        c.start()

    def keep(i, key, val, at):
        kvb[0, :, at] = key
        kvb[1, :, at] = val
        n = key.shape[1]
        state = dot_t(key, val)
        row = jnp.sum(key.astype(F32), axis=0, keepdims=True)
        if n < LANE:
            state = jnp.where(mask[:n, :n], state, 0.0)
            state = state[0:32] + state[32:64] + state[64:96]
            state = jnp.concatenate([state, jnp.zeros((32, LANE - n), F32)], axis=1)
            row = jnp.concatenate([row, jnp.zeros((1, LANE - n), F32)], axis=1)
        else:
            state = fold(state, mask)
        put_state(part.at[pl.ds(5 * i, 5)], state, row)

    def tile(i, _):
        @pl.when(i == 0)
        def _():
            arrive(1, O0, O1, YL0, YR1)

        @pl.when(i == 1)
        def _():
            across_in(1, ZN0, ZN1)
            arrive(1, YR0, YL1)

        @pl.when(i == 2)
        def _():
            arrive(1, YO0, YO1)

        @pl.when(i == READY)
        def _():
            settled(1)
            for c in tile_load(READY):
                c.start()
            last.start()

        slot = i % 2
        pltpu.make_async_copy(wt.at[slot], wt.at[slot], wsem.at[slot]).wait()

        @pl.when(jnp.logical_and(i + 1 < full, i + 1 != READY))
        def _():
            for c in tile_load(i + 1):
                c.start()

        acc = dot(tup[...], wt[slot])
        key = jnp.maximum(acc[:, :LANE], 0.0).astype(BF)
        keep(i, key, acc[:, LANE:].astype(BF), pl.ds(pl.multiple_of(i * LANE, LANE), LANE))
        return 0

    lax.fori_loop(0, full, tile, 0)
    last.wait()
    pad = jnp.zeros((depth, LANE - tail), BF)
    acc = dot(tup[...], jnp.concatenate([wlast[0], pad, wlast[1]], axis=1))
    key = jnp.maximum(acc[:, :tail], 0.0).astype(BF)
    keep(full, key, acc[:, LANE : LANE + tail].astype(BF), pl.ds(full * LANE, tail))
    kv_write = pltpu.make_async_copy(kvb, kv_out, usem.at[2])
    kv_write.start()
    total(s, part, sums, slots, sems)
    state_out[...] = sums[...]
    for c in always:
        c.wait_send()

    @pl.when(is1)
    def _():
        for c in second:
            c.wait_send()

    swap.wait()
    kv_write.wait()


def gather(wk, wv, tok):
    rows, cols = wk.shape
    depth, count = tok.shape
    hbm = pl.BlockSpec(memory_space=pl.ANY)
    vm = pl.BlockSpec(memory_space=pltpu.VMEM)
    tiles = (48, 8, LANE)
    return pl.pallas_call(
        gather_kernel,
        name="gather",
        out_shape=(
            jax.ShapeDtypeStruct((2, depth, cols), BF),
            jax.ShapeDtypeStruct(tok.shape, BF),
            jax.ShapeDtypeStruct((2, count, cols), BF),
            jax.ShapeDtypeStruct(tiles, F32),
        ),
        in_specs=[hbm] * 3,
        out_specs=(hbm, hbm, hbm, vm),
        scratch_shapes=[
            pltpu.VMEM((2, rows, cols), BF),
            pltpu.VMEM(tok.shape, BF),
            pltpu.VMEM(tok.shape[::-1], BF),
            pltpu.VMEM((2, depth, 2 * LANE), BF),
            pltpu.VMEM((2, depth, cols % LANE), BF),
            pltpu.VMEM((2, count, cols), BF),
            pltpu.VMEM(tiles, F32),
            pltpu.VMEM(tiles, F32),
            pltpu.VMEM((16, SHARE, 8, LANE), F32),
            DMA((64,)), DMA((2, 16)), DMA((2, 16)), DMA((4,)), DMA((2,)), DMA((3,)), DMA((2,)),
            DMA((4, 16)),
        ],
        compiler_params=params(1),
    )(wk, wv, tok)


def split(a):
    hi = a.astype(BF)
    return hi, (a - hi.astype(F32)).astype(BF)


def same_head():
    r = lax.broadcasted_iota(jnp.int32, (LANE, LANE), 0) // HD
    c = lax.broadcasted_iota(jnp.int32, (LANE, LANE), 1) // HD
    return r == c


def fold(block, mask):
    b = jnp.where(mask, block, 0.0)
    return b[0:32] + b[32:64] + b[64:96] + b[96:128]


def unfold(state, mask):
    return jnp.where(mask, jnp.concatenate([state] * 4, axis=0), 0.0)


def put_state(ref, state, row):
    ref[0:4] = state.reshape(4, 8, LANE)
    ref[4] = jnp.broadcast_to(row, (8, LANE))


def dot(a, b):
    return lax.dot_general(a, b, (((1,), (0,)), ((), ())), preferred_element_type=F32)


def dot_t(a, b):
    return lax.dot_general(a, b, (((0,), (0,)), ((), ())), preferred_element_type=F32)


SHARE = 3


def peers_of(s):
    places = [(s.sp + k) % 16 for k in range(16)]
    return places, [{"img": s.img, "sp": p} for p in places]


def share(ref, place):
    return ref.at[pl.ds(place * SHARE, SHARE)]


def total(s, part, sums, slots, sems):
    places, devs = peers_of(s)
    me = s.sp
    out, back = [], []
    for k in range(1, 16):
        c = remote(share(part, places[k]), slots.at[k], sems.at[0, k], sems.at[1, k], devs[k])
        c.start()
        out.append(c)
    acc = share(part, me)[...]
    for k in range(1, 16):
        out[k - 1].wait_recv()
        acc = acc + slots[k]
    mine = share(sums, me)
    mine[...] = acc
    for k in range(1, 16):
        c = remote(mine, mine, sems.at[2, k], sems.at[3, k], devs[k])
        c.start()
        back.append(c)
    for k in range(1, 16):
        ref = share(sums, (me + 16 - k) % 16)
        pltpu.make_async_copy(ref, ref, sems.at[3, k]).wait()
    for c in out + back:
        c.wait_send()


def dot_r(a, b):
    return lax.dot_general(a, b, (((1,), (1,)), ((), ())), preferred_element_type=F32)


def attend_kernel(width, q_ref, g_ref, st_ref, att_ref, dq_ref, part_ref):
    mask = same_head()
    state = st_ref[0:4].reshape(32, LANE)
    row = jnp.broadcast_to(st_ref[4][0:1], (LANE, LANE))
    col = jnp.transpose(row)[:, 0:1]
    kv = unfold(state, mask)
    kvh, kvl = split(kv)
    kvth, kvtl = split(jnp.transpose(kv))
    nh, nl = split(jnp.where(mask, row, 0.0))
    line = lax.broadcasted_iota(jnp.int32, q_ref.shape, 0) + pl.program_id(0) * LANE
    ok = line < width
    zero = jnp.zeros((), BF)
    q = jnp.where(ok, jnp.maximum(q_ref[...], zero), zero)
    g = jnp.where(ok, g_ref[...], zero).astype(F32)
    fwd = jnp.concatenate(
        [jnp.concatenate([kvth, kvtl], axis=1), jnp.concatenate([nh, nl], axis=1)], axis=0
    )
    both = dot(fwd, jnp.concatenate([q, q], axis=0))
    inv = 1.0 / (both[LANE:] + EPS_DEN)
    attn = both[:LANE] * inv
    att_ref[...] = attn.astype(BF)
    d_num = g * inv
    ones = jnp.where(mask, 1.0, 0.0).astype(BF)
    dots = dot(
        jnp.concatenate([ones, ones], axis=1), jnp.concatenate(split(g * attn), axis=0)
    )
    d_den = -dots * inv
    dnh, dnl = split(d_num)
    pair = jnp.concatenate([dnh, dnl], axis=0)
    back = jnp.concatenate(
        [
            jnp.concatenate([kvh, kvh], axis=1),
            jnp.concatenate([kvl, jnp.zeros_like(kvl)], axis=1),
        ],
        axis=0,
    )
    feat = dot(back, pair)
    feat = feat[:LANE] + feat[LANE:] + d_den * col
    dq_ref[...] = jnp.where(q > 0, feat, 0.0).astype(BF)
    gs = dot_r(q, pair)
    gn = jnp.sum(d_den * q.astype(F32), axis=1, keepdims=True)
    put_state(
        part_ref,
        fold(gs[:, :LANE] + gs[:, LANE:], mask),
        jnp.transpose(jnp.broadcast_to(gn, (LANE, LANE)))[0:1],
    )


def attend(q, g, state):
    width, count = q.shape
    lines = pl.BlockSpec((LANE, count), lambda i: (i, 0))
    tiles = pl.BlockSpec((5, 8, LANE), lambda i: (i, 0, 0))
    return pl.pallas_call(
        lambda *r: attend_kernel(width, *r),
        name="attend",
        grid=(pl.cdiv(width, LANE),),
        out_shape=(
            jax.ShapeDtypeStruct((width, count), BF),
            jax.ShapeDtypeStruct((width, count), BF),
            jax.ShapeDtypeStruct((48, 8, LANE), F32),
        ),
        in_specs=[lines, lines, tiles],
        out_specs=(lines, lines, tiles),
        compiler_params=params(),
    )(q, g, state)


PIECE = 72
OFFS = (0, 72, 144, 208)
CUT = 640
SPLIT = 512
BAND = 448


def finish_kernel(scale, tok_img, part_ref, kv_ref, tok_ref, tok2_ref, w_ref, ok_ref, ov_ref, dt_ref,
                  cat, dcat, dboth, kvb, sums, slots, gp, relay, final, comb, res1, relay2, final2,
                  res2, zbuf, fin, wbuf, ssem, rsem, lsem, csem, wsem, tsem):
    s = Seat()
    core = s.core
    x_r, x_l, y_r, y_l = s.at(dx=1), s.at(dx=-1), s.at(dy=1), s.at(dy=-1)
    right1, left1 = s.at(dx=1 - core, dy=core), s.at(dx=core - 1, dy=-core)
    right2, left2 = s.at(dx=core, dy=1 - core), s.at(dx=-core, dy=core - 1)
    me1 = s.x * (1 - core) + s.y * core
    me2 = s.y * (1 - core) + s.x * core
    across, beside, partner = s.across(), s.beside(), s.partner()
    count, width = kv_ref.shape[1:]

    def loader(src, dst, i):
        return pltpu.make_async_copy(src, dst, lsem.at[i])

    lo, up = pl.ds(0, count), pl.ds(count, count)
    ld = [
        loader(kv_ref, kvb, 0),
        loader(tok_ref, cat.at[:, :, lo], 1),
        loader(tok2_ref, cat.at[:, :, up], 2),
    ]
    for c in ld:
        c.start()
    bands = w_ref.shape[1] // BAND

    def band_load(i):
        at = pl.ds(i * BAND, BAND)
        return pltpu.make_async_copy(w_ref.at[:, at], wbuf.at[i % 2], wsem.at[i])

    band_load(0).start()
    band_load(1).start()
    meet([x_r, x_l, across] + peers_of(s)[1][1:])
    total(s, part_ref, sums, slots, tsem)
    ld[0].wait()
    mask = same_head()

    def swap(i):
        at = pl.ds((0, SPLIT)[i], (SPLIT, width - SPLIT)[i])
        return remote(
            dboth.at[1 - core, :, at], dcat.at[up, at], ssem.at[22 + i], rsem.at[18 + i], partner
        )

    def features(g, at, n):
        gs = unfold(sums[pl.ds(5 * g, 4)].reshape(32, LANE) * tok_img, mask)[:n, :n]
        row = sums[5 * g + 4][0:1, :n] * tok_img
        gh, gl = split(gs)
        th, tl = split(jnp.transpose(gs))
        key, val = kvb[0, :, at], kvb[1, :, at]

        def twice(a, h, l):
            if n < LANE:
                return dot(a, h) + dot(a, l)
            return dot(jnp.concatenate([a, a], axis=1), jnp.concatenate([h, l], axis=0))

        dk = jnp.where(key > 0, twice(val, th, tl) + row, 0.0).astype(BF)
        dv = twice(key, gh, gl).astype(BF)
        dboth[0, :, at] = dk
        dboth[1, :, at] = dv
        dcat[lo, at] = jnp.where(core == 0, dk.astype(F32), dv.astype(F32)).astype(BF)

    def tile(g, _):
        features(g, pl.ds(pl.multiple_of(g * LANE, LANE), LANE), LANE)
        return 0

    lax.fori_loop(0, SPLIT // LANE, tile, 0)
    swap(0).start()
    lax.fori_loop(SPLIT // LANE, width // LANE, tile, 0)
    tail = width - width // LANE * LANE
    features(width // LANE, pl.ds(width - tail, tail), tail)
    swap(1).start()

    pending = []

    def copy(src, dst, i, device):
        return remote(src, dst, ssem.at[i], rsem.at[i], device)

    def go(src, dst, i, device):
        c = copy(src, dst, i, device)
        c.start()
        pending.append(c)

    def arrived(ref, sem):
        pltpu.make_async_copy(ref, ref, sem).wait()

    def nxt(v, k):
        return (v + k) % 4

    def band(i):
        band_load(i).wait()
        both = wbuf.at[i % 2]
        v = dot_r(both[0], dboth[0]) + dot_r(both[1], dboth[1])
        dt_ref[pl.ds(i * BAND, BAND)] = v.astype(BF)
        if i + 2 < bands:
            band_load(i + 2).start()

    def shard(h, dx, first=False):
        xx = nxt(s.x, dx)
        if first:
            v = dot(cat[h * 4 + xx, :, lo], dcat[lo])
            swap(0).wait()
            swap(1).wait()
            v = v + dot(cat[h * 4 + xx, :, up], dcat[up])
        else:
            v = dot(cat[h * 4 + xx], dcat[...])
        for y in range(4):
            c = xx * (1 - core) + y * core
            j = y * (1 - core) + xx * core
            gp[h, c, j] = v[OFFS[y] : OFFS[y] + PIECE].astype(BF)

        @pl.when(core == 1)
        def _():
            j = xx
            d = (right1, left1)
            copy(gp.at[h, nxt(me1, 2), j], relay.at[h, j], h, d[h]).start()
            if h == 1:
                copy(gp.at[1, nxt(me1, 1), j], final.at[0, 1, j], 2, right1).start()
            else:
                copy(gp.at[0, nxt(me1, 3), j], final.at[1, 0, j], 3, left1).start()

        act = {
            (0, 2): (relay.at[0], 0, right1),
            (1, 2): (relay.at[1], 1, left1),
            (1, 1): (final.at[0, 1], 2, right1),
            (0, 3): (final.at[1, 0], 3, left1),
        }.get((h, dx))
        if act is not None:
            dst, i, dev = act

            @pl.when(core == 0)
            def _():
                copy(gp.at[h, nxt(me1, dx)], dst, i, dev).start()

    def add(dst, *srcs):
        def body(j, _):
            v = srcs[0][j].astype(F32)
            for r in srcs[1:]:
                v = v + r[j].astype(F32)
            dst[j] = v.astype(BF)
            return 0

        lax.fori_loop(0, 4, body, 0)

    def combine():
        arrived(relay.at[0], rsem.at[0])
        add(comb.at[0], gp.at[0, nxt(me1, 1)], relay.at[0])
        copy(comb.at[0], final.at[0, 0], 4, right1).start()
        arrived(relay.at[1], rsem.at[1])
        add(comb.at[1], gp.at[1, nxt(me1, 3)], relay.at[1])
        copy(comb.at[1], final.at[1, 1], 5, left1).start()

    for c in ld[1:]:
        c.wait()
    for h, dx in ((0, 2), (1, 2), (1, 1), (0, 3), (0, 1), (1, 3), (0, 0)):
        shard(h, dx, (h, dx) == (0, 2))

    @pl.when(core == 0)
    def _():
        combine()

    shard(1, 0)

    @pl.when(core == 1)
    def _():
        combine()

    for i, dst in enumerate(
        (relay.at[0], relay.at[1], final.at[0, 1], final.at[1, 0], final.at[0, 0], final.at[1, 1])
    ):
        pending.append(copy(dst, dst, i, right1))

    band(0)
    band(1)
    band(2)
    arrived(final.at[1, 0], rsem.at[3])
    arrived(final.at[0, 1], rsem.at[2])
    arrived(final.at[0, 0], rsem.at[4])
    add(res1.at[0], gp.at[0, me1], final.at[0, 0], final.at[1, 0])

    go(res1.at[0, nxt(me2, 2)], relay2.at[0], 6, right2)
    arrived(final.at[1, 1], rsem.at[5])
    add(res1.at[1], gp.at[1, me1], final.at[0, 1], final.at[1, 1])
    go(res1.at[1, nxt(me2, 2)], relay2.at[1], 7, left2)
    go(res1.at[1, nxt(me2, 1)], final2.at[0, 1], 8, right2)
    go(res1.at[0, nxt(me2, 3)], final2.at[1, 0], 9, left2)
    band(3)

    def plus(*refs):
        v = refs[0][...].astype(F32)
        for r in refs[1:]:
            v = v + r[...].astype(F32)
        return v.astype(BF)

    arrived(relay2.at[0], rsem.at[6])
    relay2[0] = plus(relay2.at[0], res1.at[0, nxt(me2, 1)])
    go(relay2.at[0], final2.at[0, 0], 10, right2)
    arrived(relay2.at[1], rsem.at[7])
    relay2[1] = plus(relay2.at[1], res1.at[1, nxt(me2, 3)])
    go(relay2.at[1], final2.at[1, 1], 11, left2)
    band(4)
    arrived(final2.at[1, 0], rsem.at[9])
    arrived(final2.at[0, 1], rsem.at[8])
    arrived(final2.at[0, 0], rsem.at[10])
    res2[0] = plus(res1.at[0, me2], final2.at[0, 0], final2.at[1, 0])
    arrived(final2.at[1, 1], rsem.at[11])
    res2[1] = plus(res1.at[1, me2], final2.at[0, 1], final2.at[1, 1])

    go(res2.at[1 - s.zhi], zbuf.at[0], 12, across)
    arrived(zbuf.at[0], rsem.at[12])
    zbuf[2] = plus(res2.at[s.zhi], zbuf.at[0])
    go(zbuf.at[2], zbuf.at[1], 13, beside)
    arrived(zbuf.at[1], rsem.at[13])
    mine = fin.at[core, s.y]
    mine[...] = plus(zbuf.at[1], zbuf.at[2])

    yd, yu, yo = (s.y + 3) % 4, (s.y + 1) % 4, (s.y + 2) % 4
    go(mine, mine, 14, y_r)
    go(mine, mine, 15, y_l)

    def chip(ref, k):
        c = remote(ref, ref, ssem.at[k], csem.at[k - 18], partner)
        c.start()
        pending.append(c)

    chip(mine, 18)
    a, b = pl.ds(0, CUT), pl.ds(CUT, mine.shape[1] - CUT)
    arrived(fin.at[core, yd], rsem.at[14])
    go(fin.at[core, yd, :, a], fin.at[core, yd, :, a], 16, y_r)
    chip(fin.at[core, yd], 19)
    arrived(fin.at[core, yu], rsem.at[15])
    go(fin.at[core, yu, :, b], fin.at[core, yu, :, b], 17, y_l)
    chip(fin.at[core, yu], 20)
    arrived(fin.at[core, yo, :, a], rsem.at[16])
    arrived(fin.at[core, yo, :, b], rsem.at[17])
    chip(fin.at[core, yo], 21)
    for k, y in enumerate((s.y, yd, yu, yo)):
        arrived(fin.at[1 - core, y], csem.at[k])
    for c in pending:
        c.wait_send()
    for ref, i in ((ok_ref, 0), (ov_ref, 1)):
        for y in range(3):
            ref[pl.ds(PIECE * y, PIECE)] = fin[i, y].astype(F32) * scale
        ref[pl.ds(216, 64)] = fin[i, 3].astype(F32)[8:] * scale


def finish(part, kv, tok, tok2, w, scale, tok_img):
    _, count, width = kv.shape
    depth = tok.shape[0]
    rows = depth // 8
    vm = pl.BlockSpec(memory_space=pltpu.VMEM)
    hbm = pl.BlockSpec(memory_space=pl.ANY)
    p = (PIECE, width)
    return pl.pallas_call(
        lambda *r: finish_kernel(scale, tok_img, *r),
        name="finish",
        out_shape=(pltpu.VMEM((rows, width), F32),) * 2
        + (pltpu.VMEM((depth, count), BF),),
        in_specs=[vm] + [hbm] * 4,
        out_specs=(vm, vm, vm),
        scratch_shapes=[
            pltpu.VMEM((8, rows, 2 * count), BF),
            pltpu.VMEM((2 * count, width), BF),
            pltpu.VMEM((2, count, width), BF),
            pltpu.VMEM((2, count, width), BF),
            pltpu.VMEM(part.shape, F32),
            pltpu.VMEM((16, SHARE, 8, LANE), F32),
            pltpu.VMEM((2, 4, 4) + p, BF),
            pltpu.VMEM((2, 4) + p, BF),
            pltpu.VMEM((2, 2, 4) + p, BF),
            pltpu.VMEM((2, 4) + p, BF),
            pltpu.VMEM((2, 4) + p, BF),
            pltpu.VMEM((2,) + p, BF),
            pltpu.VMEM((2, 2) + p, BF),
            pltpu.VMEM((2,) + p, BF),
            pltpu.VMEM((3,) + p, BF),
            pltpu.VMEM((2, 4) + p, BF),
            pltpu.VMEM((2, 2, BAND, width), BF),
            DMA((24,)), DMA((20,)), DMA((3,)), DMA((4,)), DMA((5,)), DMA((4, 16)),
        ],
        compiler_params=params(5, grant=52 * 1024 * 1024),
    )(part, kv, tok.reshape(8, rows, count), tok2.reshape(8, rows, count), w)


def body(tokens, queries, w_key, w_value, cotangent):
    tok = jnp.transpose(tokens[0])
    depth, count = tok.shape
    width = w_key.shape[1]
    tok_img = count * lax.axis_size("sp")
    images = lax.axis_size("img")
    w, tok2, kv, state = gather(w_key, w_value, tok)
    att, dq, part = attend(jnp.transpose(queries[0]), jnp.transpose(cotangent[0]), state)
    scale = float((images * tok_img) ** -0.5)
    dwk, dwv, dt = finish(part, kv, tok, tok2, w, scale, float(tok_img))
    return jnp.transpose(att)[None], jnp.transpose(dt)[None], jnp.transpose(dq)[None], dwk, dwv


def solution(mesh):
    rows, flat = P("img", "sp", None), P("img", None)
    return jax.shard_map(
        body,
        mesh=mesh,
        in_specs=(rows, rows, flat, flat, rows),
        out_specs=(rows, rows, rows, flat, flat),
        check_vma=False,
    )
```

```python
import jax
import jax.numpy as jnp
from jax import lax
from jax.experimental import pallas as pl
from jax.experimental.pallas import tpu as pltpu
from jax.sharding import PartitionSpec as P

HD = 32
EPS_DEN = 1e-06
BF = jnp.bfloat16
F32 = jnp.float32
MESH = pl.DeviceIdType.MESH
LANE = 128
ROWS = 256
VMEM_MAX = 64 * 1024 * 1024 - 65536
DMA = pltpu.SemaphoreType.DMA


def params(cid=None, sem=None, grant=VMEM_MAX):
    return pltpu.CompilerParams(
        collective_id=cid,
        has_side_effects=cid is not None,
        vmem_limit_bytes=grant,
        dimension_semantics=sem,
    )


class Seat:
    def __init__(self):
        img, sp = lax.axis_index("img"), lax.axis_index("sp")
        self.img, self.sp = img, sp
        self.zhi, self.x = img // 4, img % 4
        self.y, self.zlo, self.core = sp // 4, (sp // 2) % 2, sp % 2

    def at(self, dx=0, dy=0, hi=None, lo=None, core=None):
        x = (self.x + dx + 4) % 4
        y = (self.y + dy + 4) % 4
        hi = self.zhi if hi is None else hi
        lo = self.zlo if lo is None else lo
        core = self.core if core is None else core
        return {"img": hi * 4 + x, "sp": (y * 2 + lo) * 2 + core}

    def across(self):
        return self.at(hi=1 - self.zhi, lo=1 - self.zlo)

    def beside(self):
        return self.at(lo=1 - self.zlo)

    def partner(self):
        return self.at(core=1 - self.core)


def meet(devices):
    bar = pltpu.get_barrier_semaphore()
    for d in devices:
        pl.semaphore_signal(bar, inc=1, device_id=d, device_id_type=MESH)
    pl.semaphore_wait(bar, len(devices))


def remote(src, dst, ssem, rsem, device):
    return pltpu.make_async_remote_copy(
        src_ref=src, dst_ref=dst, send_sem=ssem, recv_sem=rsem, device_id=device, device_id_type=MESH
    )


HALVES = ((0, 144), (144, 136))
L0, L1, R0, R1, O0, O1, YL0, YR0, YO0, YL1, YR1, YO1, ZM0, ZM1, ZN0, ZN1 = range(16)


PHASES = ((0, 640), (640, 480))
READY = 5


def gather_kernel(wk_ref, wv_ref, tok_ref, out, tok_out, kv_out, state_out, w_ref, tin, tup, wt, wlast,
                  kvb, part, sums, slots, ssem, rsem, csem, lsem, tsem, usem, wsem, sems):
    s = Seat()
    m = s.y % 2
    width = wk_ref.shape[1]
    rows = wk_ref.shape[0]
    right, left = s.at(dx=1), s.at(dx=-1)
    up, down = s.at(dy=1), s.at(dy=-1)
    partner, across = s.partner(), s.across()
    loads = [
        pltpu.make_async_copy(r, w_ref.at[i], lsem.at[2 + i]) for i, r in enumerate((wk_ref, wv_ref))
    ]
    read = pltpu.make_async_copy(tok_ref, tin, usem.at[0])
    for c in loads:
        c.start()
    read.start()
    meet([right, left, across] + peers_of(s)[1][1:])
    for c in loads:
        c.wait()

    def spot(mat, shard, h, p):
        row = pl.multiple_of(shard * rows + HALVES[h][0], 8)
        return out.at[mat, pl.ds(row, HALVES[h][1]), pl.ds(*PHASES[p])]

    def mine(mat, h, p):
        return w_ref.at[mat, pl.ds(*HALVES[h]), pl.ds(*PHASES[p])]

    def place(k, core, p):
        hi = (s.zhi + core) % 2
        if k >= ZM0:
            return spot(m if k < ZN0 else 1 - m, (1 - s.zhi) * 4 + s.x, (k - ZM0) % 2, p)
        dx, h = {
            L0: (3, 0), L1: (3, 1), R0: (1, 0), R1: (1, 1), O0: (2, 0), O1: (2, 1),
            YL0: (3, 0), YR0: (1, 0), YO0: (2, 0), YL1: (3, 1), YR1: (1, 1), YO1: (2, 1),
        }[k]
        return spot(m if k < YL0 else 1 - m, hi * 4 + (s.x + dx) % 4, h, p)

    is0, is1 = s.core == 0, s.core == 1
    hi = (s.zhi + s.core) % 2
    seed = hi * 4 + s.x
    always, second = [], []

    def new(src, dst, k, p, device, sem, only1=False):
        slot = len(always) + len(second)
        c = remote(src, dst, ssem.at[slot], sem.at[p, k], device)
        (second if only1 else always).append(c)
        return c

    zs, seeds0, seeds1, onward, chips = {}, {}, {}, {}, {}
    for p in range(2):
        for k, mat, h in ((ZM0, m, 0), (ZM1, m, 1), (ZN0, 1 - m, 0), (ZN1, 1 - m, 1)):
            zs[k, p] = new(mine(mat, h, p), spot(mat, s.img, h, p), k, p, across, rsem, True)
        for i, (h, k, d) in enumerate(((0, L0, right), (1, R1, left), (1, L1, right), (0, R0, left))):
            slot = ssem.at[len(always) + len(second)]
            there = spot(m, seed, h, p)
            seeds1[i, p] = remote(there, there, slot, rsem.at[p, k], d)
            seeds0[i, p] = new(mine(m, h, p), spot(m, s.img, h, p), k, p, d, rsem)
        for k, to, d in (
            (L0, O0, right), (R1, O1, left),
            (L0, YL0, up), (R0, YR0, up), (O0, YO0, up),
            (L1, YL1, down), (R1, YR1, down), (O1, YO1, down),
        ):
            ref = place(k, s.core, p)
            onward.setdefault((k, p), []).append(new(ref, ref, to, p, d, rsem))
        for k in range(16):
            ref = place(k, s.core, p)
            chips[k, p] = new(ref, ref, k, p, partner, csem, k >= ZM0)

    def got(k, p, sem, core):
        ref = place(k, core, p)
        pltpu.make_async_copy(ref, ref, sem.at[p, k]).wait()

    def arrive(p, *ks):
        for k in ks:
            got(k, p, rsem, s.core)
            for c in onward.get((k, p), ()):
                c.start()
            chips[k, p].start()

    def across_in(p, *ks):
        @pl.when(is1)
        def _():
            for k in ks:
                arrive(p, k)
                if k in (ZM0, ZM1):
                    h = k - ZM0
                    for i in ((0, 3), (1, 2))[h]:
                        seeds1[i, p].start()

    def seed0(p, *which):
        @pl.when(is0)
        def _():
            for i in which:
                seeds0[i, p].start()

    def settled(p):
        for k in range(ZM0):
            got(k, p, csem, 1 - s.core)

        @pl.when(is0)
        def _():
            for k in range(ZM0, 16):
                got(k, p, csem, 1)

    @pl.when(is1)
    def _():
        for k, p in (
            (ZM0, 0), (ZM1, 0), (ZM0, 1), (ZM1, 1), (ZN0, 0), (ZN1, 0), (ZN0, 1), (ZN1, 1)
        ):
            zs[k, p].start()

    seed0(0, 0, 1, 2, 3)
    swap = remote(tok_ref, tok_out, tsem.at[0], tsem.at[1], partner)
    owns = [
        pltpu.make_async_copy(
            w_ref.at[i],
            out.at[i, pl.ds(pl.multiple_of(s.img * rows, 8), rows)],
            lsem.at[i],
        )
        for i in range(2)
    ]
    for c in owns:
        c.start()
    read.wait()
    depth = tok_ref.shape[0]
    whole = depth // ROWS
    rest = depth - whole * ROWS

    def flip(i, _):
        at = pl.ds(pl.multiple_of(i * ROWS, ROWS), ROWS)
        tup[:, at] = jnp.transpose(tin[at])
        return 0

    lax.fori_loop(0, 2, flip, 0)
    across_in(0, ZM0, ZM1)
    lax.fori_loop(2, 3, flip, 0)
    arrive(0, L0, R1)
    seed0(1, 0, 1)
    lax.fori_loop(3, 4, flip, 0)
    arrive(0, L1, R0)
    seed0(1, 2, 3)
    across_in(1, ZM0, ZM1)
    lax.fori_loop(4, 5, flip, 0)
    arrive(0, YL0, YR1)
    across_in(0, ZN0, ZN1)
    lax.fori_loop(5, 6, flip, 0)
    arrive(0, O0, O1)
    swap.start()
    arrive(1, L0, R1)
    lax.fori_loop(6, whole, flip, 0)
    arrive(0, YR0, YL1)
    arrive(1, L1, R0)
    at = pl.ds(whole * ROWS, rest)
    tup[:, at] = jnp.transpose(tin[at])
    arrive(0, YO0, YO1)
    settled(0)
    for c in owns:
        c.wait()

    def tile_load(i):
        at = pl.ds(pl.multiple_of(i * LANE, LANE), LANE)
        slot = i % 2
        return [
            pltpu.make_async_copy(
                out.at[j, :, at], wt.at[slot, :, pl.ds(j * LANE, LANE)], wsem.at[slot]
            )
            for j in range(2)
        ]

    full = width // LANE
    tail = width - full * LANE
    last = pltpu.make_async_copy(out.at[:, :, pl.ds(full * LANE, tail)], wlast, usem.at[1])
    mask = same_head()
    part[45:48] = jnp.zeros((3, 8, LANE), F32)
    for c in tile_load(0):
        c.start()

    def keep(i, key, val, at):
        kvb[0, :, at] = key
        kvb[1, :, at] = val
        n = key.shape[1]
        state = dot_t(key, val)
        row = jnp.sum(key.astype(F32), axis=0, keepdims=True)
        if n < LANE:
            state = jnp.where(mask[:n, :n], state, 0.0)
            state = state[0:32] + state[32:64] + state[64:96]
            state = jnp.concatenate([state, jnp.zeros((32, LANE - n), F32)], axis=1)
            row = jnp.concatenate([row, jnp.zeros((1, LANE - n), F32)], axis=1)
        else:
            state = fold(state, mask)
        put_state(part.at[pl.ds(5 * i, 5)], state, row)

    def tile(i, _):
        @pl.when(i == 0)
        def _():
            arrive(1, O0, O1, YL0, YR1)

        @pl.when(i == 1)
        def _():
            across_in(1, ZN0, ZN1)
            arrive(1, YR0, YL1)

        @pl.when(i == 2)
        def _():
            arrive(1, YO0, YO1)

        @pl.when(i == READY)
        def _():
            settled(1)
            for c in tile_load(READY):
                c.start()
            last.start()

        slot = i % 2
        pltpu.make_async_copy(wt.at[slot], wt.at[slot], wsem.at[slot]).wait()

        @pl.when(jnp.logical_and(i + 1 < full, i + 1 != READY))
        def _():
            for c in tile_load(i + 1):
                c.start()

        acc = dot(tup[...], wt[slot])
        key = jnp.maximum(acc[:, :LANE], 0.0).astype(BF)
        keep(i, key, acc[:, LANE:].astype(BF), pl.ds(pl.multiple_of(i * LANE, LANE), LANE))
        return 0

    lax.fori_loop(0, full, tile, 0)
    last.wait()
    pad = jnp.zeros((depth, LANE - tail), BF)
    acc = dot(tup[...], jnp.concatenate([wlast[0], pad, wlast[1]], axis=1))
    key = jnp.maximum(acc[:, :tail], 0.0).astype(BF)
    keep(full, key, acc[:, LANE : LANE + tail].astype(BF), pl.ds(full * LANE, tail))
    kv_write = pltpu.make_async_copy(kvb, kv_out, usem.at[2])
    kv_write.start()
    total(s, part, sums, slots, sems)
    state_out[...] = sums[...]
    for c in always:
        c.wait_send()

    @pl.when(is1)
    def _():
        for c in second:
            c.wait_send()

    swap.wait()
    kv_write.wait()


def gather(wk, wv, tok):
    rows, cols = wk.shape
    depth, count = tok.shape
    hbm = pl.BlockSpec(memory_space=pl.ANY)
    vm = pl.BlockSpec(memory_space=pltpu.VMEM)
    tiles = (48, 8, LANE)
    return pl.pallas_call(
        gather_kernel,
        name="gather",
        out_shape=(
            jax.ShapeDtypeStruct((2, depth, cols), BF),
            jax.ShapeDtypeStruct(tok.shape, BF),
            jax.ShapeDtypeStruct((2, count, cols), BF),
            jax.ShapeDtypeStruct(tiles, F32),
        ),
        in_specs=[hbm] * 3,
        out_specs=(hbm, hbm, hbm, vm),
        scratch_shapes=[
            pltpu.VMEM((2, rows, cols), BF),
            pltpu.VMEM(tok.shape, BF),
            pltpu.VMEM(tok.shape[::-1], BF),
            pltpu.VMEM((2, depth, 2 * LANE), BF),
            pltpu.VMEM((2, depth, cols % LANE), BF),
            pltpu.VMEM((2, count, cols), BF),
            pltpu.VMEM(tiles, F32),
            pltpu.VMEM(tiles, F32),
            pltpu.VMEM((16, SHARE, 8, LANE), F32),
            DMA((64,)), DMA((2, 16)), DMA((2, 16)), DMA((4,)), DMA((2,)), DMA((3,)), DMA((2,)),
            DMA((4, 16)),
        ],
        compiler_params=params(1),
    )(wk, wv, tok)


def split(a):
    hi = a.astype(BF)
    return hi, (a - hi.astype(F32)).astype(BF)


def same_head():
    r = lax.broadcasted_iota(jnp.int32, (LANE, LANE), 0) // HD
    c = lax.broadcasted_iota(jnp.int32, (LANE, LANE), 1) // HD
    return r == c


def fold(block, mask):
    b = jnp.where(mask, block, 0.0)
    return b[0:32] + b[32:64] + b[64:96] + b[96:128]


def unfold(state, mask):
    return jnp.where(mask, jnp.concatenate([state] * 4, axis=0), 0.0)


def put_state(ref, state, row):
    ref[0:4] = state.reshape(4, 8, LANE)
    ref[4] = jnp.broadcast_to(row, (8, LANE))


def dot(a, b):
    return lax.dot_general(a, b, (((1,), (0,)), ((), ())), preferred_element_type=F32)


def dot_t(a, b):
    return lax.dot_general(a, b, (((0,), (0,)), ((), ())), preferred_element_type=F32)


SHARE = 3


def peers_of(s):
    places = [(s.sp + k) % 16 for k in range(16)]
    return places, [{"img": s.img, "sp": p} for p in places]


def share(ref, place):
    return ref.at[pl.ds(place * SHARE, SHARE)]


def total(s, part, sums, slots, sems):
    places, devs = peers_of(s)
    me = s.sp
    out, back = [], []
    for k in range(1, 16):
        c = remote(share(part, places[k]), slots.at[k], sems.at[0, k], sems.at[1, k], devs[k])
        c.start()
        out.append(c)
    acc = share(part, me)[...]
    for k in range(1, 16):
        out[k - 1].wait_recv()
        acc = acc + slots[k]
    mine = share(sums, me)
    mine[...] = acc
    for k in range(1, 16):
        c = remote(mine, mine, sems.at[2, k], sems.at[3, k], devs[k])
        c.start()
        back.append(c)
    for k in range(1, 16):
        ref = share(sums, (me + 16 - k) % 16)
        pltpu.make_async_copy(ref, ref, sems.at[3, k]).wait()
    for c in out + back:
        c.wait_send()


def dot_r(a, b):
    return lax.dot_general(a, b, (((1,), (1,)), ((), ())), preferred_element_type=F32)


def attend_kernel(width, q_ref, g_ref, st_ref, att_ref, dq_ref, part_ref):
    mask = same_head()
    state = st_ref[0:4].reshape(32, LANE)
    row = jnp.broadcast_to(st_ref[4][0:1], (LANE, LANE))
    col = jnp.transpose(row)[:, 0:1]
    kv = unfold(state, mask)
    kvh, kvl = split(kv)
    kvth, kvtl = split(jnp.transpose(kv))
    nh, nl = split(jnp.where(mask, row, 0.0))
    line = lax.broadcasted_iota(jnp.int32, q_ref.shape, 0) + pl.program_id(0) * LANE
    ok = line < width
    zero = jnp.zeros((), BF)
    q = jnp.where(ok, jnp.maximum(q_ref[...], zero), zero)
    g = jnp.where(ok, g_ref[...], zero).astype(F32)
    fwd = jnp.concatenate(
        [jnp.concatenate([kvth, kvtl], axis=1), jnp.concatenate([nh, nl], axis=1)], axis=0
    )
    both = dot(fwd, jnp.concatenate([q, q], axis=0))
    inv = 1.0 / (both[LANE:] + EPS_DEN)
    attn = both[:LANE] * inv
    att_ref[...] = attn.astype(BF)
    d_num = g * inv
    ones = jnp.where(mask, 1.0, 0.0).astype(BF)
    dots = dot(
        jnp.concatenate([ones, ones], axis=1), jnp.concatenate(split(g * attn), axis=0)
    )
    d_den = -dots * inv
    dnh, dnl = split(d_num)
    pair = jnp.concatenate([dnh, dnl], axis=0)
    back = jnp.concatenate(
        [
            jnp.concatenate([kvh, kvh], axis=1),
            jnp.concatenate([kvl, jnp.zeros_like(kvl)], axis=1),
        ],
        axis=0,
    )
    feat = dot(back, pair)
    feat = feat[:LANE] + feat[LANE:] + d_den * col
    dq_ref[...] = jnp.where(q > 0, feat, 0.0).astype(BF)
    gs = dot_r(q, pair)
    gn = jnp.sum(d_den * q.astype(F32), axis=1, keepdims=True)
    put_state(
        part_ref,
        fold(gs[:, :LANE] + gs[:, LANE:], mask),
        jnp.transpose(jnp.broadcast_to(gn, (LANE, LANE)))[0:1],
    )


def attend(q, g, state):
    width, count = q.shape
    lines = pl.BlockSpec((LANE, count), lambda i: (i, 0))
    tiles = pl.BlockSpec((5, 8, LANE), lambda i: (i, 0, 0))
    return pl.pallas_call(
        lambda *r: attend_kernel(width, *r),
        name="attend",
        grid=(pl.cdiv(width, LANE),),
        out_shape=(
            jax.ShapeDtypeStruct((width, count), BF),
            jax.ShapeDtypeStruct((width, count), BF),
            jax.ShapeDtypeStruct((48, 8, LANE), F32),
        ),
        in_specs=[lines, lines, tiles],
        out_specs=(lines, lines, tiles),
        compiler_params=params(),
    )(q, g, state)


PIECE = 72
OFFS = (0, 72, 144, 208)
CUT = 640
SPLIT = 512
BAND = 448


def finish_kernel(scale, tok_img, part_ref, kv_ref, tok_ref, tok2_ref, w_ref, ok_ref, ov_ref, dt_ref,
                  cat, dcat, dboth, kvb, sums, slots, gp, relay, final, comb, res1, relay2, final2,
                  res2, zbuf, fin, wbuf, ssem, rsem, lsem, csem, wsem, tsem):
    s = Seat()
    core = s.core
    x_r, x_l, y_r, y_l = s.at(dx=1), s.at(dx=-1), s.at(dy=1), s.at(dy=-1)
    right1, left1 = s.at(dx=1 - core, dy=core), s.at(dx=core - 1, dy=-core)
    right2, left2 = s.at(dx=core, dy=1 - core), s.at(dx=-core, dy=core - 1)
    me1 = s.x * (1 - core) + s.y * core
    me2 = s.y * (1 - core) + s.x * core
    across, beside, partner = s.across(), s.beside(), s.partner()
    count, width = kv_ref.shape[1:]

    def loader(src, dst, i):
        return pltpu.make_async_copy(src, dst, lsem.at[i])

    lo, up = pl.ds(0, count), pl.ds(count, count)
    ld = [
        loader(kv_ref, kvb, 0),
        loader(tok_ref, cat.at[:, :, lo], 1),
        loader(tok2_ref, cat.at[:, :, up], 2),
    ]
    for c in ld:
        c.start()
    bands = w_ref.shape[1] // BAND

    def band_load(i):
        at = pl.ds(i * BAND, BAND)
        return pltpu.make_async_copy(w_ref.at[:, at], wbuf.at[i % 2], wsem.at[i])

    band_load(0).start()
    band_load(1).start()
    meet([x_r, x_l, across] + peers_of(s)[1][1:])
    total(s, part_ref, sums, slots, tsem)
    ld[0].wait()
    mask = same_head()

    def swap(i):
        at = pl.ds((0, SPLIT)[i], (SPLIT, width - SPLIT)[i])
        return remote(
            dboth.at[1 - core, :, at], dcat.at[up, at], ssem.at[22 + i], rsem.at[18 + i], partner
        )

    def features(g, at, n):
        gs = unfold(sums[pl.ds(5 * g, 4)].reshape(32, LANE) * tok_img, mask)[:n, :n]
        row = sums[5 * g + 4][0:1, :n] * tok_img
        gh, gl = split(gs)
        th, tl = split(jnp.transpose(gs))
        key, val = kvb[0, :, at], kvb[1, :, at]

        def twice(a, h, l):
            if n < LANE:
                return dot(a, h) + dot(a, l)
            return dot(jnp.concatenate([a, a], axis=1), jnp.concatenate([h, l], axis=0))

        dk = jnp.where(key > 0, twice(val, th, tl) + row, 0.0).astype(BF)
        dv = twice(key, gh, gl).astype(BF)
        dboth[0, :, at] = dk
        dboth[1, :, at] = dv
        dcat[lo, at] = jnp.where(core == 0, dk.astype(F32), dv.astype(F32)).astype(BF)

    def tile(g, _):
        features(g, pl.ds(pl.multiple_of(g * LANE, LANE), LANE), LANE)
        return 0

    lax.fori_loop(0, SPLIT // LANE, tile, 0)
    swap(0).start()
    lax.fori_loop(SPLIT // LANE, width // LANE, tile, 0)
    tail = width - width // LANE * LANE
    features(width // LANE, pl.ds(width - tail, tail), tail)
    swap(1).start()

    pending = []

    def copy(src, dst, i, device):
        return remote(src, dst, ssem.at[i], rsem.at[i], device)

    def go(src, dst, i, device):
        c = copy(src, dst, i, device)
        c.start()
        pending.append(c)

    def arrived(ref, sem):
        pltpu.make_async_copy(ref, ref, sem).wait()

    def nxt(v, k):
        return (v + k) % 4

    def band(i):
        band_load(i).wait()
        both = wbuf.at[i % 2]
        v = dot_r(both[0], dboth[0]) + dot_r(both[1], dboth[1])
        dt_ref[pl.ds(i * BAND, BAND)] = v.astype(BF)
        if i + 2 < bands:
            band_load(i + 2).start()

    def shard(h, dx, first=False):
        xx = nxt(s.x, dx)
        if first:
            v = dot(cat[h * 4 + xx, :, lo], dcat[lo])
            swap(0).wait()
            swap(1).wait()
            v = v + dot(cat[h * 4 + xx, :, up], dcat[up])
        else:
            v = dot(cat[h * 4 + xx], dcat[...])
        for y in range(4):
            c = xx * (1 - core) + y * core
            j = y * (1 - core) + xx * core
            gp[h, c, j] = v[OFFS[y] : OFFS[y] + PIECE].astype(BF)

        @pl.when(core == 1)
        def _():
            j = xx
            d = (right1, left1)
            copy(gp.at[h, nxt(me1, 2), j], relay.at[h, j], h, d[h]).start()
            if h == 1:
                copy(gp.at[1, nxt(me1, 1), j], final.at[0, 1, j], 2, right1).start()
            else:
                copy(gp.at[0, nxt(me1, 3), j], final.at[1, 0, j], 3, left1).start()

        act = {
            (0, 2): (relay.at[0], 0, right1),
            (1, 2): (relay.at[1], 1, left1),
            (1, 1): (final.at[0, 1], 2, right1),
            (0, 3): (final.at[1, 0], 3, left1),
        }.get((h, dx))
        if act is not None:
            dst, i, dev = act

            @pl.when(core == 0)
            def _():
                copy(gp.at[h, nxt(me1, dx)], dst, i, dev).start()

    def add(dst, *srcs):
        def body(j, _):
            v = srcs[0][j].astype(F32)
            for r in srcs[1:]:
                v = v + r[j].astype(F32)
            dst[j] = v.astype(BF)
            return 0

        lax.fori_loop(0, 4, body, 0)

    def combine():
        arrived(relay.at[0], rsem.at[0])
        add(comb.at[0], gp.at[0, nxt(me1, 1)], relay.at[0])
        copy(comb.at[0], final.at[0, 0], 4, right1).start()
        arrived(relay.at[1], rsem.at[1])
        add(comb.at[1], gp.at[1, nxt(me1, 3)], relay.at[1])
        copy(comb.at[1], final.at[1, 1], 5, left1).start()

    for c in ld[1:]:
        c.wait()
    for h, dx in ((0, 2), (1, 2), (1, 1), (0, 3), (0, 1), (1, 3), (0, 0)):
        shard(h, dx, (h, dx) == (0, 2))

    @pl.when(core == 0)
    def _():
        combine()

    shard(1, 0)

    @pl.when(core == 1)
    def _():
        combine()

    for i, dst in enumerate(
        (relay.at[0], relay.at[1], final.at[0, 1], final.at[1, 0], final.at[0, 0], final.at[1, 1])
    ):
        pending.append(copy(dst, dst, i, right1))

    band(0)
    band(1)
    band(2)
    arrived(final.at[1, 0], rsem.at[3])
    arrived(final.at[0, 1], rsem.at[2])
    arrived(final.at[0, 0], rsem.at[4])
    add(res1.at[0], gp.at[0, me1], final.at[0, 0], final.at[1, 0])

    go(res1.at[0, nxt(me2, 2)], relay2.at[0], 6, right2)
    arrived(final.at[1, 1], rsem.at[5])
    add(res1.at[1], gp.at[1, me1], final.at[0, 1], final.at[1, 1])
    go(res1.at[1, nxt(me2, 2)], relay2.at[1], 7, left2)
    go(res1.at[1, nxt(me2, 1)], final2.at[0, 1], 8, right2)
    go(res1.at[0, nxt(me2, 3)], final2.at[1, 0], 9, left2)
    band(3)

    def plus(*refs):
        v = refs[0][...].astype(F32)
        for r in refs[1:]:
            v = v + r[...].astype(F32)
        return v.astype(BF)

    arrived(relay2.at[0], rsem.at[6])
    relay2[0] = plus(relay2.at[0], res1.at[0, nxt(me2, 1)])
    go(relay2.at[0], final2.at[0, 0], 10, right2)
    arrived(relay2.at[1], rsem.at[7])
    relay2[1] = plus(relay2.at[1], res1.at[1, nxt(me2, 3)])
    go(relay2.at[1], final2.at[1, 1], 11, left2)
    band(4)
    arrived(final2.at[1, 0], rsem.at[9])
    arrived(final2.at[0, 1], rsem.at[8])
    arrived(final2.at[0, 0], rsem.at[10])
    res2[0] = plus(res1.at[0, me2], final2.at[0, 0], final2.at[1, 0])
    arrived(final2.at[1, 1], rsem.at[11])
    res2[1] = plus(res1.at[1, me2], final2.at[0, 1], final2.at[1, 1])

    a, b = pl.ds(0, CUT), pl.ds(CUT, width - CUT)
    mine = fin.at[core, s.y]
    yd, yu, yo = (s.y + 3) % 4, (s.y + 1) % 4, (s.y + 2) % 4
    halves = ((a, 12, 13, 14, 15), (b, 24, 25, 26, 27))
    for c, i, _, _, _ in halves:
        go(res2.at[1 - s.zhi, :, c], zbuf.at[0, :, c], i, across)
    for c, i, j, _, _ in halves:
        arrived(zbuf.at[0, :, c], rsem.at[i])
        zbuf[2, :, c] = plus(res2.at[s.zhi, :, c], zbuf.at[0, :, c])
        go(zbuf.at[2, :, c], zbuf.at[1, :, c], j, beside)

    for c, _, j, r, l in halves:
        arrived(zbuf.at[1, :, c], rsem.at[j])
        fin[core, s.y, :, c] = plus(zbuf.at[1, :, c], zbuf.at[2, :, c])
        go(mine.at[:, c], mine.at[:, c], r, y_r)
        go(mine.at[:, c], mine.at[:, c], l, y_l)

    def chip(ref, k):
        c = remote(ref, ref, ssem.at[k], csem.at[k - 18], partner)
        c.start()
        pending.append(c)

    chip(mine, 18)
    arrived(fin.at[core, yd, :, a], rsem.at[14])
    go(fin.at[core, yd, :, a], fin.at[core, yd, :, a], 16, y_r)
    arrived(fin.at[core, yu, :, a], rsem.at[15])
    arrived(fin.at[core, yu, :, b], rsem.at[27])
    go(fin.at[core, yu, :, b], fin.at[core, yu, :, b], 17, y_l)
    chip(fin.at[core, yu], 20)
    arrived(fin.at[core, yd, :, b], rsem.at[26])
    chip(fin.at[core, yd], 19)
    arrived(fin.at[core, yo, :, a], rsem.at[16])
    arrived(fin.at[core, yo, :, b], rsem.at[17])
    chip(fin.at[core, yo], 21)
    for k, y in enumerate((s.y, yd, yu, yo)):
        arrived(fin.at[1 - core, y], csem.at[k])
    for c in pending:
        c.wait_send()
    for ref, i in ((ok_ref, 0), (ov_ref, 1)):
        for y in range(3):
            ref[pl.ds(PIECE * y, PIECE)] = fin[i, y].astype(F32) * scale
        ref[pl.ds(216, 64)] = fin[i, 3].astype(F32)[8:] * scale


def finish(part, kv, tok, tok2, w, scale, tok_img):
    _, count, width = kv.shape
    depth = tok.shape[0]
    rows = depth // 8
    vm = pl.BlockSpec(memory_space=pltpu.VMEM)
    hbm = pl.BlockSpec(memory_space=pl.ANY)
    p = (PIECE, width)
    return pl.pallas_call(
        lambda *r: finish_kernel(scale, tok_img, *r),
        name="finish",
        out_shape=(pltpu.VMEM((rows, width), F32),) * 2
        + (pltpu.VMEM((depth, count), BF),),
        in_specs=[vm] + [hbm] * 4,
        out_specs=(vm, vm, vm),
        scratch_shapes=[
            pltpu.VMEM((8, rows, 2 * count), BF),
            pltpu.VMEM((2 * count, width), BF),
            pltpu.VMEM((2, count, width), BF),
            pltpu.VMEM((2, count, width), BF),
            pltpu.VMEM(part.shape, F32),
            pltpu.VMEM((16, SHARE, 8, LANE), F32),
            pltpu.VMEM((2, 4, 4) + p, BF),
            pltpu.VMEM((2, 4) + p, BF),
            pltpu.VMEM((2, 2, 4) + p, BF),
            pltpu.VMEM((2, 4) + p, BF),
            pltpu.VMEM((2, 4) + p, BF),
            pltpu.VMEM((2,) + p, BF),
            pltpu.VMEM((2, 2) + p, BF),
            pltpu.VMEM((2,) + p, BF),
            pltpu.VMEM((3,) + p, BF),
            pltpu.VMEM((2, 4) + p, BF),
            pltpu.VMEM((2, 2, BAND, width), BF),
            DMA((28,)), DMA((28,)), DMA((3,)), DMA((4,)), DMA((5,)), DMA((4, 16)),
        ],
        compiler_params=params(5, grant=52 * 1024 * 1024),
    )(part, kv, tok.reshape(8, rows, count), tok2.reshape(8, rows, count), w)


def body(tokens, queries, w_key, w_value, cotangent):
    tok = jnp.transpose(tokens[0])
    depth, count = tok.shape
    width = w_key.shape[1]
    tok_img = count * lax.axis_size("sp")
    images = lax.axis_size("img")
    w, tok2, kv, state = gather(w_key, w_value, tok)
    att, dq, part = attend(jnp.transpose(queries[0]), jnp.transpose(cotangent[0]), state)
    scale = float((images * tok_img) ** -0.5)
    dwk, dwv, dt = finish(part, kv, tok, tok2, w, scale, float(tok_img))
    return jnp.transpose(att)[None], jnp.transpose(dt)[None], jnp.transpose(dq)[None], dwk, dwv


def solution(mesh):
    rows, flat = P("img", "sp", None), P("img", None)
    return jax.shard_map(
        body,
        mesh=mesh,
        in_specs=(rows, rows, flat, flat, rows),
        out_specs=(rows, rows, rows, flat, flat),
        check_vma=False,
    )
```
